32 devices in a mesh: space: 8 (over y, x, core), dp: 4 (over z).
Axes of the slice: x: 2, y: 2, z: 4, core: 2. Of those that a mesh axis runs over, the one named last changes fastest.
Arguments:
- block_in: bfloat16 [4, 8, 56, 56, 128], P('dp', 'space'), may hold values from -6 to 6
- weights: bfloat16 [3, 3, 128, 128], replicated, may hold values from -0.1875 to 0.1875
- out_bias: float32 [128], replicated, may hold values from -3 to 3
- adjacency: int32 [8, 8, 2], P('space'), may hold values from 0 to 7, as said below
- cotangent: bfloat16 [4, 8, 56, 56, 128], P('dp', 'space'), may hold values from -6 to 6
Outputs:
- block_out: bfloat16 [4, 8, 56, 56, 128], P('dp', 'space')
- weight_grad: float32 [3, 3, 128, 128], replicated
- grad_in: bfloat16 [4, 8, 56, 56, 128], P('dp', 'space')
The draws below stay inside these ranges and needn't reach their ends.
Inputs may be any that keep to these rules, and one draw needn't show every extreme that they name: adjacency[t, e] = (p, f) for e < 4 means that adjacency[p, f] = (t, e): edges are glued in pairs; entries 4 + k hold a tile and corner k' with adjacency[p, 4 + k'] = (t, k), corners glued in pairs. The corner pairing need not follow the edge pairing. Every edge and every corner of every tile appears exactly once as a partner. Column 1 lies in 0..3.
All inputs are finite; a program needn't handle non-finite values.
Results may differ from the reference program's by a relative error of at most 0.0031.
Values may be sent and summed in bfloat16 or wider, within the bound.
A program may use at most 64 MiB of HBM per device.

```python
import jax
import jax.numpy as jnp
from jax import lax

S = 56
C = 128
TILES = 8
BATCH = 4


def pair_up(key, slot_count):
    shuffled = jax.random.permutation(key, slot_count).astype(jnp.int32)
    partner = jnp.zeros((slot_count,), jnp.int32)
    partner = partner.at[shuffled[0::2]].set(shuffled[1::2])
    partner = partner.at[shuffled[1::2]].set(shuffled[0::2])
    return partner


def draw_adjacency(key, part):
    edge_mate = pair_up(jax.random.fold_in(key, 11), 4 * TILES)
    corner_mate = pair_up(jax.random.fold_in(key, 12), 4 * TILES)
    edge_part = jnp.stack([edge_mate // 4, edge_mate % 4], -1).reshape(TILES, 4, 2)
    corner_part = jnp.stack([corner_mate // 4, corner_mate % 4], -1).reshape(TILES, 4, 2)
    return jnp.concatenate([edge_part, corner_part], 1).astype(jnp.int32)


def block_scale(own_key, extent, shards, low, largest):
    def one(position, parts):
        steps = jax.random.uniform(jax.random.fold_in(jax.random.fold_in(own_key, 6), position), (parts,), jnp.float32, low / len(shards), largest / len(shards))
        return jnp.repeat(jnp.exp(steps), extent[position] // parts).reshape((-1,) + (1,) * (len(extent) - position - 1))

    factor_of = one(*shards[0])
    for cut in shards[1:]:
        factor_of = factor_of * one(*cut)
    return factor_of


def noise(rng, dims, spread, most, cuts=(), dtype=jnp.bfloat16):
    drawn = jax.random.normal(rng, dims, jnp.float32) * spread
    if len(cuts) > 0:
        drawn = block_scale(rng, dims, cuts, -0.22, 0.18) * drawn
    return jnp.clip(drawn, min=-most, max=most).astype(dtype)


def setup_inputs(seed: int = 0) -> dict:
    key_of = jax.random.split(jax.random.key(seed), 6)
    return {
        "block_in": noise(key_of[0], (BATCH, TILES, S, S, C), 1.0, 6.0, ((0, 4), (1, 8))),
        "weights": noise(key_of[1], (3, 3, C, C), (9 * C) ** -0.5, 0.1875),
        "out_bias": noise(key_of[2], (C,), 0.5, 3.0, (), jnp.float32),
        "adjacency": draw_adjacency(jax.random.fold_in(key_of[5], 71), 0),
        "cotangent": noise(key_of[4], (BATCH, TILES, S, S, C), 1.0, 6.0, ((0, 4), (1, 8))),
    }


def tile_edges(field):
    top_rim = field[..., 0, :, :]
    right_rim = field[..., :, -1, :]
    bottom_rim = jnp.flip(field[..., -1, :, :], -2)
    left_rim = jnp.flip(field[..., :, 0, :], -2)
    return jnp.stack([top_rim, right_rim, bottom_rim, left_rim], -3)


def tile_corners(field):
    return jnp.stack([field[..., 0, 0, :], field[..., 0, -1, :], field[..., -1, -1, :], field[..., -1, 0, :]], -2)


def assemble(field, near_edges, near_corners):
    top_row = jnp.concatenate([near_corners[0:1], jnp.flip(near_edges[0], 0), near_corners[1:2]], 0)
    bottom_row = jnp.concatenate([near_corners[3:4], near_edges[2], near_corners[2:3]], 0)
    middle = jnp.concatenate([near_edges[3][:, None], field, jnp.flip(near_edges[1], 0)[:, None]], 1)
    return jnp.concatenate([top_row[None], middle, bottom_row[None]], 0)


def conv_forward(padded, weights):
    side = padded.shape[0] - 2
    width = padded.shape[2]
    running = jnp.zeros((side * side, weights.shape[3]), jnp.float32)
    for row_off in range(3):
        for col_off in range(3):
            window = padded[row_off:row_off + side, col_off:col_off + side].reshape(side * side, width)
            running = running + jnp.dot(window, weights[row_off, col_off], preferred_element_type=jnp.float32)
    return running.reshape(side, side, -1)


def conv_backward(padded, grad_out, weights):
    side = padded.shape[0] - 2
    width = padded.shape[2]
    grad_rows = grad_out.reshape(side * side, -1)
    grad_pad = jnp.zeros(padded.shape, jnp.float32)
    kernel_rows = []
    for row_off in range(3):
        kernel_cols = []
        for col_off in range(3):
            window = padded[row_off:row_off + side, col_off:col_off + side].reshape(side * side, width)
            kernel_cols.append(jnp.dot(window.T, grad_rows, preferred_element_type=jnp.float32))
            back = jnp.dot(grad_rows, weights[row_off, col_off].T, preferred_element_type=jnp.float32)
            grad_pad = grad_pad + jnp.pad(back.reshape(side, side, width), ((row_off, 2 - row_off), (col_off, 2 - col_off), (0, 0)))
        kernel_rows.append(jnp.stack(kernel_cols, 0))
    return jnp.stack(kernel_rows, 0), grad_pad


def rim_grads(grad_pad):
    top_rim = grad_pad[0, 1:-1]
    right_rim = grad_pad[1:-1, -1]
    bottom_rim = jnp.flip(grad_pad[-1, 1:-1], 0)
    left_rim = jnp.flip(grad_pad[1:-1, 0], 0)
    rim_edges = jnp.stack([top_rim, right_rim, bottom_rim, left_rim], 0).astype(jnp.bfloat16)
    rim_corners = jnp.stack([grad_pad[0, 0], grad_pad[0, -1], grad_pad[-1, -1], grad_pad[-1, 0]], 0).astype(jnp.bfloat16)
    return rim_edges, rim_corners


def add_back(interior, back_edges, back_corners):
    edge_vals = back_edges.astype(jnp.float32)
    corner_vals = back_corners.astype(jnp.float32)
    interior = interior.at[0, :].add(jnp.flip(edge_vals[0], 0))
    interior = interior.at[:, -1].add(jnp.flip(edge_vals[1], 0))
    interior = interior.at[-1, :].add(edge_vals[2])
    interior = interior.at[:, 0].add(edge_vals[3])
    interior = interior.at[0, 0].add(corner_vals[0])
    interior = interior.at[0, -1].add(corner_vals[1])
    interior = interior.at[-1, -1].add(corner_vals[2])
    interior = interior.at[-1, 0].add(corner_vals[3])
    return interior


def reference(block_in, weights, out_bias, adjacency, cotangent):
    edge_tile = adjacency[:, 0:4, 0]
    edge_side = adjacency[:, 0:4, 1]
    corner_tile = adjacency[:, 4:8, 0]
    corner_side = adjacency[:, 4:8, 1]
    grad_acc = jnp.zeros(weights.shape, jnp.float32)
    results = []
    grads = []
    for sample in range(BATCH):
        inputs = block_in[sample]
        activation = jax.nn.silu(inputs.astype(jnp.float32)).astype(jnp.bfloat16)
        near_edges = tile_edges(activation)[edge_tile, edge_side]
        near_corners = tile_corners(activation)[corner_tile, corner_side]
        padded = jax.vmap(assemble)(activation, near_edges, near_corners)

        def tile_step(running, tile_items):
            pad_tile, tile_in, tile_cot = tile_items
            conv_sum = conv_forward(pad_tile, weights)
            result = (tile_in.astype(jnp.float32) + conv_sum + out_bias).astype(jnp.bfloat16)
            kernel_grad, grad_pad = conv_backward(pad_tile, tile_cot, weights)
            rim_edges, rim_corners = rim_grads(grad_pad)
            return running + kernel_grad, (result, grad_pad[1:-1, 1:-1], rim_edges, rim_corners)

        grad_acc, (result, interior, rim_edges, rim_corners) = lax.scan(tile_step, grad_acc, (padded, inputs, cotangent[sample]))
        back_edges = rim_edges[edge_tile, edge_side]
        back_corners = rim_corners[corner_tile, corner_side]
        act_grad = jax.vmap(add_back)(interior, back_edges, back_corners)
        input_f = inputs.astype(jnp.float32)
        sigmoid_x = jax.nn.sigmoid(input_f)
        grad_in = (cotangent[sample].astype(jnp.float32) + act_grad * sigmoid_x * (1.0 + input_f * (1.0 - sigmoid_x))).astype(jnp.bfloat16)
        results.append(result)
        grads.append(grad_in)
    return jnp.stack(results, 0), grad_acc, jnp.stack(grads, 0)
```

```python
import functools

import jax
import jax.numpy as jnp
from jax import lax
from jax.experimental import pallas as pl
from jax.experimental.pallas import tpu as pltpu
from jax.sharding import PartitionSpec as P

MESH = pl.DeviceIdType.MESH
ROWS = 8
F32 = jnp.float32
BF16 = jnp.bfloat16
CODE = jnp.int16


def silu(v):
    return v / (1.0 + jnp.exp(-v))


def encode(v):
    top = jnp.maximum(jnp.max(jnp.abs(v), axis=0, keepdims=True), 1e-30)
    power = jnp.ceil(jnp.log2(top))
    code = jnp.clip(jnp.round(v * jnp.exp2(15.0 - power)), -32767.0, 32767.0)
    rows = jnp.concatenate([code, jnp.broadcast_to(power, (16, v.shape[1]))], axis=0)
    return rows.astype(jnp.int32).astype(CODE)


def decode(rows):
    v = rows.astype(jnp.int32).astype(F32)
    size = v.shape[0] - 16
    return v[:size] * jnp.exp2(v[size:size + 1] - 15.0)


def wide_of(side):
    return -(-(side + 4) // 16) * 16


def block_kernel(
    n_sp, n_dp, side,
    adj_hbm, x_hbm, w_hbm, bias_hbm, g_hbm,
    out, wg_out, gin_out,
    x_in, g_in, w_in, bias, adj, adj_all, adj_row,
    taps, gtaps, pad_grad, wt, vt, wgf, corr, half_in, col_a, col_b, col_c, col_d,
    ends, la, lg, sent, parts, dps, full,
    in_sem, es, er, js, jr, hs, hr, ss, sr, ds_, dr, gs, gr,
):
    wide = wide_of(side)
    chan = 128
    chunks = side // ROWS
    me = lax.axis_index("space")
    my_dp = lax.axis_index("dp")
    core = lax.rem(me, 2)
    chip = me // 2
    chips = n_sp // 2
    partner = me + 1 - 2 * core

    barrier = pltpu.get_barrier_semaphore()

    def greet_sp(k, c):
        pl.semaphore_signal(barrier, inc=1, device_id=(lax.rem(me + k, n_sp), my_dp), device_id_type=MESH)
        return c

    def greet_dp(k, c):
        pl.semaphore_signal(barrier, inc=1, device_id=(me, lax.rem(my_dp + k, n_dp)), device_id_type=MESH)
        return c

    loads = [
        pltpu.make_async_copy(x_hbm, x_in, in_sem.at[0]),
        pltpu.make_async_copy(g_hbm, g_in, in_sem.at[1]),
        pltpu.make_async_copy(adj_hbm, adj, in_sem.at[2]),
        pltpu.make_async_copy(w_hbm, w_in, in_sem.at[3]),
        pltpu.make_async_copy(bias_hbm, bias, in_sem.at[4]),
    ]
    for one in loads:
        one.start()
    lax.fori_loop(1, n_sp, greet_sp, 0)
    lax.fori_loop(1, n_dp, greet_dp, 0)

    def alike(k):
        return lax.rem(me + 2 * k, n_sp)

    def beside(tile):
        return tile + 1 - 2 * lax.rem(tile, 2)

    def remote(src, dst, send, recv, peer, dp=None):
        return pltpu.make_async_remote_copy(
            src_ref=src, dst_ref=dst, send_sem=send, recv_sem=recv,
            device_id=(peer, my_dp if dp is None else dp), device_id_type=MESH)

    def push(buf, slot, peer, send, recv):
        return remote(buf.at[slot], buf.at[slot], send, recv.at[slot], peer)

    def pair_begin(buf, send, recv):
        def go(k, c):
            push(buf, me, alike(k), send.at[alike(k)], recv).start()
            return c
        lax.fori_loop(1, chips, go, 0)
        push(buf, me, partner, send.at[partner], recv).start()

    def pair_relay(buf, send, recv):
        def go(k, c):
            tile = alike(k)
            push(buf, tile, partner, send.at[beside(tile)], recv).wait_recv()
            push(buf, tile, partner, send.at[beside(tile)], recv).start()
            return c
        lax.fori_loop(1, chips, go, 0)

    def pair_finish(buf, send, recv):
        push(buf, partner, partner, send.at[partner], recv).wait()
        def go(k, c):
            tile = alike(k)
            push(buf, me, tile, send.at[tile], recv).wait_send()
            push(buf, beside(tile), partner, send.at[beside(tile)], recv).wait()
            return c
        lax.fori_loop(1, chips, go, 0)

    r64 = lax.broadcasted_iota(jnp.int32, (wide, chan), 0)
    ra = lax.broadcasted_iota(jnp.int32, (wide, wide), 0)
    rb = lax.broadcasted_iota(jnp.int32, (wide, wide), 1)
    mirror = jnp.where(ra + rb == side - 1, 1.0, 0.0).astype(BF16)

    def flip(v):
        return jnp.dot(mirror, v, preferred_element_type=F32)

    s8 = lax.broadcasted_iota(jnp.int32, (ROWS, 8, chan), 1)

    def column(block, at):
        return jnp.sum(jnp.where(s8 == at, block, 0.0), axis=1)

    tail = jnp.zeros((wide - side, chan), F32)

    def widen(v):
        return jnp.concatenate([v, tail], axis=0)

    loads[0].wait()
    for c in range(chunks):
        lo = c * ROWS
        col_a[lo:lo + ROWS, :] = silu(column(x_in[lo:lo + ROWS, 0:8, :].astype(F32), 0))
        col_b[lo:lo + ROWS, :] = silu(column(x_in[lo:lo + ROWS, side - 8:side, :].astype(F32), 7))
    for col in (col_a, col_b, col_c, col_d):
        col[side:wide, :] = tail
    ends[me, 0] = widen(silu(x_in[0].astype(F32))).astype(BF16)
    ends[me, 1] = col_b[...].astype(BF16)
    ends[me, 2] = flip(widen(silu(x_in[side - 1].astype(F32))).astype(BF16)).astype(BF16)
    ends[me, 3] = flip(col_a[...].astype(BF16)).astype(BF16)
    loads[1].wait()
    for c in range(chunks):
        lo = c * ROWS
        col_c[lo:lo + ROWS, :] = column(g_in[lo:lo + ROWS, 0:8, :].astype(F32), 0)
        col_d[lo:lo + ROWS, :] = column(g_in[lo:lo + ROWS, side - 8:side, :].astype(F32), 7)
    ends[me, 4] = flip(widen(g_in[0].astype(F32)).astype(BF16)).astype(BF16)
    ends[me, 5] = flip(col_d[...].astype(BF16)).astype(BF16)
    ends[me, 6] = widen(g_in[side - 1].astype(F32)).astype(BF16)
    ends[me, 7] = col_c[...].astype(BF16)
    loads[2].wait()
    lane = lax.broadcasted_iota(jnp.int32, (1, chan), 1)
    row = jnp.zeros((1, chan), jnp.int32)
    for k in range(8):
        for part in range(2):
            row = jnp.where(lane == 2 * k + part, adj[0, part, k], row)
    adj_row[me] = row
    pl.semaphore_wait(barrier, n_sp + n_dp - 2)
    pair_begin(ends, es, er)
    pair_begin(adj_row, js, jr)

    zero_row = jnp.zeros((wide, 3 * chan), BF16)
    for buf in (taps, gtaps):
        buf[0] = zero_row
        buf[side + 1] = zero_row

    def shifts(v):
        return jnp.concatenate(
            [pltpu.roll(v, 1, 0).astype(BF16), v.astype(BF16), pltpu.roll(v, wide - 1, 0).astype(BF16)], axis=1)

    def spread(c, carry):
        for k in range(ROWS):
            i = c * ROWS + k
            taps[i + 1] = shifts(widen(silu(x_in[i].astype(F32))))
            gtaps[i + 1] = shifts(widen(g_in[i].astype(F32)))
        return carry

    lax.fori_loop(0, chunks, spread, 0)

    wgf[...] = jnp.zeros_like(wgf)

    def kernel_chunk(c, carry):
        y0 = c * ROWS + 1
        lhs = jnp.concatenate(
            [taps[pl.ds(y0 - 1 + r, ROWS), :, chan:2 * chan].reshape(ROWS * wide, chan).T for r in range(3)], axis=0)
        res = jnp.dot(lhs, gtaps[pl.ds(y0, ROWS)].reshape(ROWS * wide, 3 * chan), preferred_element_type=F32)
        for r in range(3):
            for b in range(3):
                at = (3 * r + 2 - b) * chan
                wgf[at:at + chan, :] += res[r * chan:(r + 1) * chan, b * chan:(b + 1) * chan]
        return carry

    lax.fori_loop(0, chunks, kernel_chunk, 0)

    size = full.shape[1]
    half = chips * size
    swap = remote(
        wgf.at[pl.ds(pl.multiple_of((1 - core) * half, 16), half)], half_in, hs.at[0], hr.at[0], partner)
    swap.start()

    loads[3].wait()
    loads[4].wait()
    for r in range(3):
        for c in range(3):
            block = w_in[2 - r, (2 - c) * chan:(3 - c) * chan, :].astype(F32)
            wt[r, c * chan:(c + 1) * chan, :] = block.T.astype(BF16)
    for k in range(3):
        to = slice(k * chan, (k + 1) * chan)
        for e, (r, c) in enumerate(((2, 2 - k), (2 - k, 0), (0, k), (k, 2))):
            vt[e, to, :] = wt[r, c * chan:(c + 1) * chan, :]
    swap.wait()

    def half_rows(h):
        at = pl.multiple_of(h * size, 16)
        return wgf[pl.ds(pl.multiple_of(core * half + h * size, 16), size), :] + half_in[pl.ds(at, size), :]

    def scatter_copy(k):
        peer = alike(k)
        start = remote(sent.at[peer // 2], parts.at[chip], ss.at[peer // 2], sr.at[chip], peer)
        wait = remote(sent.at[peer // 2], parts.at[peer // 2], ss.at[peer // 2], sr.at[peer // 2], peer)
        return start, wait

    def scatter_start(k, c):
        h = alike(k) // 2
        sent[h] = encode(half_rows(h))
        scatter_copy(k)[0].start()
        return c

    lax.fori_loop(1, chips, scatter_start, 0)

    pair_relay(ends, es, er)
    pair_relay(adj_row, js, jr)

    def grad_chunk(c, carry):
        first = c * ROWS
        total = jnp.zeros((ROWS * wide, chan), F32)
        for r in range(3):
            total += jnp.dot(
                gtaps[pl.ds(first + r, ROWS)].reshape(ROWS * wide, 3 * chan), wt[r],
                preferred_element_type=F32)
        pad_grad[pl.ds(first, ROWS)] = total.reshape(ROWS, wide, chan)
        return carry

    lax.fori_loop(0, chunks, grad_chunk, 0)

    pair_finish(ends, es, er)
    pair_finish(adj_row, js, jr)
    spill = pltpu.make_async_copy(adj_row, adj_all, in_sem.at[5])
    spill.start()
    spill.wait()

    group = la.shape[1] // wide
    corr[...] = jnp.zeros_like(corr)

    def rim_group(n, carry):
        def fill(j, c2):
            t = n * group + j
            at = pl.ds(pl.multiple_of(j * wide, 16), wide)
            for e in range(4):
                v = ends[adj_all[t, 0, 2 * e], adj_all[t, 0, 2 * e + 1]].astype(F32)
                k = ends[adj_all[t, 0, 8 + 2 * e], adj_all[t, 0, 9 + 2 * e]].astype(F32)[0:1]
                la[e, at, :] = jnp.where(r64 < side, v, jnp.where(r64 == side, k, 0.0)).astype(BF16)
                lg[e, at, :] = shifts(ends[t, 4 + e].astype(F32))
            return c2

        lax.fori_loop(0, group, fill, 0)
        for e in range(4):
            res = jnp.dot(la[e].T, lg[e], preferred_element_type=F32)
            for k in range(3):
                r, c = ((0, k), (k, 2), (2, 2 - k), (2 - k, 0))[e]
                at = (3 * r + c) * chan
                corr[at:at + chan, :] += res[:, k * chan:(k + 1) * chan]
        return carry

    lax.fori_loop(0, n_sp // group, rim_group, 0)

    def scatter_wait(k, c):
        scatter_copy(k)[1].wait()
        return c

    lax.fori_loop(1, chips, scatter_wait, 0)
    slot = core * chips + chip
    mine = half_rows(chip) + corr[pl.ds(pl.multiple_of(slot * size, 16), size), :]
    mine = lax.fori_loop(1, chips, lambda k, t: t + decode(parts[alike(k) // 2]), mine)
    dps[my_dp] = encode(mine)

    def sample_copy(k):
        peer = lax.rem(my_dp + k, n_dp)
        start = remote(dps.at[my_dp], dps.at[my_dp], ds_.at[peer], dr.at[my_dp], me, peer)
        wait = remote(dps.at[my_dp], dps.at[peer], ds_.at[peer], dr.at[peer], me, peer)
        return start, wait

    def sample_start(k, c):
        sample_copy(k)[0].start()
        return c

    def sample_wait(k, c):
        sample_copy(k)[1].wait()
        return c

    lax.fori_loop(1, n_dp, sample_start, 0)

    def near(buf, e):
        return buf[adj[0, 0, e], adj[0, 1, e]]

    def put_taps(row, a):
        taps[row] = shifts(a)

    corner = [ends[adj[0, 0, 4 + k], adj[0, 1, 4 + k]].astype(F32)[0:1] for k in range(4)]

    def rim_row(v, behind, ahead):
        return jnp.where(r64 < side, v, jnp.where(r64 == side, behind, jnp.where(r64 == wide - 1, ahead, 0.0)))

    put_taps(0, rim_row(flip(near(ends, 0)), corner[1], corner[0]))
    put_taps(side + 1, rim_row(near(ends, 2).astype(F32), corner[2], corner[3]))
    col_a[...] = near(ends, 3).astype(F32)
    col_b[...] = flip(near(ends, 1))
    s16 = lax.broadcasted_iota(jnp.int32, (ROWS, 16, chan), 1)
    at_right = (side - 1) // 16 * 16
    for c in range(chunks):
        lo = c * ROWS
        v = taps[lo + 1:lo + 1 + ROWS, 0:16, 0:chan].astype(F32)
        v = jnp.where(s16 == 0, col_a[lo:lo + ROWS, :][:, None, :], v)
        taps[lo + 1:lo + 1 + ROWS, 0:16, 0:chan] = v.astype(BF16)
        v = taps[lo + 1:lo + 1 + ROWS, at_right:at_right + 16, 2 * chan:].astype(F32)
        v = jnp.where(s16 == side - 1 - at_right, col_b[lo:lo + ROWS, :][:, None, :], v)
        taps[lo + 1:lo + 1 + ROWS, at_right:at_right + 16, 2 * chan:] = v.astype(BF16)

    def conv_chunk(c, carry):
        i0 = c * ROWS
        total = jnp.zeros((ROWS * wide, chan), F32)
        for r in range(3):
            total += jnp.dot(
                taps[pl.ds(i0 + r, ROWS)].reshape(ROWS * wide, 3 * chan), w_in[r],
                preferred_element_type=F32)
        conv = total.reshape(ROWS, wide, chan)[:, :side, :]
        field = x_in[pl.ds(i0, ROWS)].astype(F32)
        out[pl.ds(i0, ROWS)] = (field + conv + bias[...].reshape(1, 1, chan)).astype(BF16)
        return carry

    lax.fori_loop(0, chunks, conv_chunk, 0)

    lax.fori_loop(1, n_dp, sample_wait, 0)
    total = decode(dps[0])
    for d in range(1, n_dp):
        total = total + decode(dps[d])
    full[me] = total.astype(BF16)
    pair_begin(full, gs, gr)

    def rim_grad(e):
        at = adj[0, 1, e]
        v = jnp.dot(shifts(ends[adj[0, 0, e], 4 + at].astype(F32)), vt[at], preferred_element_type=F32)
        return jnp.where(r64 < side, v, 0.0).astype(BF16)

    def rim_corner(k):
        at = adj[0, 1, 4 + k]
        v = jnp.dot(ends[adj[0, 0, 4 + k], 4 + at], vt[at, 0:chan, :], preferred_element_type=F32)
        return v[side - 1:side].astype(BF16).astype(F32)

    add = [rim_corner(k) for k in range(4)]
    pad_grad[0] += rim_grad(0).astype(F32)
    pad_grad[side - 1] += flip(rim_grad(2))
    col_a[...] = flip(rim_grad(3)) + jnp.where(r64 == 0, add[0], jnp.where(r64 == side - 1, add[3], 0.0))
    col_b[...] = rim_grad(1).astype(F32) + jnp.where(r64 == 0, add[1], jnp.where(r64 == side - 1, add[2], 0.0))

    r56 = lax.broadcasted_iota(jnp.int32, (side, chan), 0)

    def finish_rows(c, carry):
        for k in range(ROWS):
            i = c * ROWS + k
            p = pad_grad[i, 0:side]
            p = p + jnp.where(r56 == 0, col_a[pl.ds(i, 1), :], jnp.where(r56 == side - 1, col_b[pl.ds(i, 1), :], 0.0))
            v = x_in[i].astype(F32)
            s = 1.0 / (1.0 + jnp.exp(-v))
            gin_out[i] = (g_in[i].astype(F32) + p * s * (1.0 + v * (1.0 - s))).astype(BF16)
        return carry

    lax.fori_loop(0, chunks, finish_rows, 0)

    pair_relay(full, gs, gr)
    pair_finish(full, gs, gr)

    def open_rows(t, carry):
        at = (lax.rem(t, 2) * chips + t // 2) * size
        wg_out[pl.ds(pl.multiple_of(at, 16), size), :] = full[t].astype(F32)
        return carry

    lax.fori_loop(0, n_sp, open_rows, 0)


def hand_on(a, wg, c, a_out, wg_out, c_out, sems):
    used = wg_out.shape[0]
    copies = [
        pltpu.make_async_copy(a, a_out, sems.at[0]),
        pltpu.make_async_copy(c, c_out, sems.at[1]),
        pltpu.make_async_copy(wg.at[pl.ds(0, used)], wg_out, sems.at[2]),
    ]
    for one in copies:
        one.start()
    for one in copies:
        one.wait()


def per_device(n_sp, n_dp, block_in, weights, out_bias, adjacency, cotangent):
    side, chan = block_in.shape[2], block_in.shape[4]
    wide = wide_of(side)
    chips = n_sp // 2
    size = -(-9 * chan // (16 * n_sp)) * 16
    group = min(n_sp, 8)
    vmem = pl.BlockSpec(memory_space=pltpu.VMEM)
    hbm = pl.BlockSpec(memory_space=pltpu.HBM)
    sem = pltpu.SemaphoreType.DMA
    tile = (side, side, chan)
    held = pl.pallas_call(
        functools.partial(block_kernel, n_sp, n_dp, side),
        out_shape=(pltpu.VMEM(tile, BF16), pltpu.VMEM((n_sp * size, chan), F32), pltpu.VMEM(tile, BF16)),
        in_specs=[hbm] * 5,
        out_specs=(vmem, vmem, vmem),
        scratch_shapes=[
            pltpu.VMEM(tile, BF16),
            pltpu.VMEM(tile, BF16),
            pltpu.VMEM((3, 3 * chan, chan), BF16),
            pltpu.VMEM((1, chan), F32),
            pltpu.SMEM((1, 2, 8), jnp.int32),
            pltpu.SMEM((n_sp, 1, chan), jnp.int32),
            pltpu.VMEM((n_sp, 1, chan), jnp.int32),
            pltpu.VMEM((side + 2, wide, 3 * chan), BF16),
            pltpu.VMEM((side + 2, wide, 3 * chan), BF16),
            pltpu.VMEM((side, wide, chan), F32),
            pltpu.VMEM((3, 3 * chan, chan), BF16),
            pltpu.VMEM((4, 3 * chan, chan), BF16),
            pltpu.VMEM((n_sp * size, chan), F32),
            pltpu.VMEM((n_sp * size, chan), F32),
            pltpu.VMEM((chips * size, chan), F32),
            pltpu.VMEM((wide, chan), F32),
            pltpu.VMEM((wide, chan), F32),
            pltpu.VMEM((wide, chan), F32),
            pltpu.VMEM((wide, chan), F32),
            pltpu.VMEM((n_sp, 8, wide, chan), BF16),
            pltpu.VMEM((4, group * wide, chan), BF16),
            pltpu.VMEM((4, group * wide, 3 * chan), BF16),
            pltpu.VMEM((chips, size + 16, chan), CODE),
            pltpu.VMEM((chips, size + 16, chan), CODE),
            pltpu.VMEM((n_dp, size + 16, chan), CODE),
            pltpu.VMEM((n_sp, size, chan), BF16),
            sem((6,)),
            sem((n_sp,)), sem((n_sp,)), sem((n_sp,)), sem((n_sp,)), sem((1,)), sem((1,)),
            sem((chips,)), sem((chips,)), sem((n_dp,)), sem((n_dp,)), sem((n_sp,)), sem((n_sp,)),
        ],
        compiler_params=pltpu.CompilerParams(
            collective_id=0, has_side_effects=True, vmem_limit_bytes=48 * 2**20),
    )(
        adjacency.transpose(0, 2, 1), block_in[0, 0], weights.reshape(3, 3 * chan, chan), out_bias.reshape(1, chan),
        cotangent[0, 0],
    )
    result, wgrad, grad_in = pl.pallas_call(
        hand_on,
        out_shape=(
            jax.ShapeDtypeStruct(tile, BF16), jax.ShapeDtypeStruct((9 * chan, chan), F32), jax.ShapeDtypeStruct(tile, BF16)),
        in_specs=[vmem, vmem, vmem],
        out_specs=(hbm, hbm, hbm),
        scratch_shapes=[sem((3,))],
        compiler_params=pltpu.CompilerParams(vmem_limit_bytes=4 * 2**20),
    )(*held)
    return (result[None, None], wgrad.reshape(weights.shape), grad_in[None, None])


def solution(mesh):
    placed = (
        P("dp", "space", None, None, None),
        P(),
        P(),
        P("space", None, None),
        P("dp", "space", None, None, None),
    )
    return jax.shard_map(
        functools.partial(per_device, mesh.shape["space"], mesh.shape["dp"]),
        mesh=mesh,
        in_specs=placed,
        out_specs=(P("dp", "space", None, None, None), P(), P("dp", "space", None, None, None)),
        check_vma=False,
    )
```

```python
import functools

import jax
import jax.numpy as jnp
from jax import lax
from jax.experimental import pallas as pl
from jax.experimental.pallas import tpu as pltpu
from jax.sharding import PartitionSpec as P

MESH = pl.DeviceIdType.MESH
ROWS = 8
PAIRS = 7
F32 = jnp.float32
BF16 = jnp.bfloat16
CODE = jnp.int16


def silu(v):
    return v / (1.0 + jnp.exp(-v))


def encode(v):
    top = jnp.maximum(jnp.max(jnp.abs(v), axis=0, keepdims=True), 1e-30)
    power = jnp.ceil(jnp.log2(top))
    code = jnp.clip(jnp.round(v * jnp.exp2(15.0 - power)), -32767.0, 32767.0)
    rows = jnp.concatenate([code, jnp.broadcast_to(power, (16, v.shape[1]))], axis=0)
    return rows.astype(jnp.int32).astype(CODE)


def decode(rows):
    v = rows.astype(jnp.int32).astype(F32)
    size = v.shape[0] - 16
    return v[:size] * jnp.exp2(v[size:size + 1] - 15.0)


def wide_of(side):
    return -(-(side + 4) // 16) * 16


def block_kernel(
    n_sp, n_dp, side,
    adj_hbm, x_hbm, w_hbm, bias_hbm, g_hbm,
    out, wg_out, gin_out,
    x_in, g_in, w_in, bias, adj, adj_all, adj_row,
    taps, gtaps, flat, pad_grad, wt, vt, pair_w, pair_t, wgf, corr, half_in, col_a, col_b, col_c, col_d,
    ends, gends, la, lg, sent, parts, dps, full,
    in_sem, es, er, cs, cr, js, jr, hs, hr, ss, sr, ds_, dr, gs, gr,
):
    wide = wide_of(side)
    chan = 128
    chunks = side // ROWS
    me = lax.axis_index("space")
    my_dp = lax.axis_index("dp")
    core = lax.rem(me, 2)
    chip = me // 2
    chips = n_sp // 2
    partner = me + 1 - 2 * core

    barrier = pltpu.get_barrier_semaphore()

    def greet_sp(k, c):
        pl.semaphore_signal(barrier, inc=1, device_id=(lax.rem(me + k, n_sp), my_dp), device_id_type=MESH)
        return c

    def greet_dp(k, c):
        pl.semaphore_signal(barrier, inc=1, device_id=(me, lax.rem(my_dp + k, n_dp)), device_id_type=MESH)
        return c

    loads = [
        pltpu.make_async_copy(x_hbm, x_in, in_sem.at[0]),
        pltpu.make_async_copy(g_hbm, g_in, in_sem.at[1]),
        pltpu.make_async_copy(adj_hbm, adj, in_sem.at[2]),
        pltpu.make_async_copy(w_hbm, w_in, in_sem.at[3]),
        pltpu.make_async_copy(bias_hbm, bias, in_sem.at[4]),
    ]
    for one in loads:
        one.start()
    lax.fori_loop(1, n_sp, greet_sp, 0)
    lax.fori_loop(1, n_dp, greet_dp, 0)

    def alike(k):
        return lax.rem(me + 2 * k, n_sp)

    def beside(tile):
        return tile + 1 - 2 * lax.rem(tile, 2)

    def remote(src, dst, send, recv, peer, dp=None):
        return pltpu.make_async_remote_copy(
            src_ref=src, dst_ref=dst, send_sem=send, recv_sem=recv,
            device_id=(peer, my_dp if dp is None else dp), device_id_type=MESH)

    def push(buf, slot, peer, send, recv):
        return remote(buf.at[slot], buf.at[slot], send, recv.at[slot], peer)

    def pair_begin(buf, send, recv):
        def go(k, c):
            push(buf, me, alike(k), send.at[alike(k)], recv).start()
            return c
        lax.fori_loop(1, chips, go, 0)
        push(buf, me, partner, send.at[partner], recv).start()

    def pair_relay(buf, send, recv):
        def go(k, c):
            tile = alike(k)
            push(buf, tile, partner, send.at[beside(tile)], recv).wait_recv()
            push(buf, tile, partner, send.at[beside(tile)], recv).start()
            return c
        lax.fori_loop(1, chips, go, 0)

    def pair_finish(buf, send, recv):
        push(buf, partner, partner, send.at[partner], recv).wait()
        def go(k, c):
            tile = alike(k)
            push(buf, me, tile, send.at[tile], recv).wait_send()
            push(buf, beside(tile), partner, send.at[beside(tile)], recv).wait()
            return c
        lax.fori_loop(1, chips, go, 0)

    r64 = lax.broadcasted_iota(jnp.int32, (wide, chan), 0)
    ra = lax.broadcasted_iota(jnp.int32, (wide, wide), 0)
    rb = lax.broadcasted_iota(jnp.int32, (wide, wide), 1)
    mirror = jnp.where(ra + rb == side - 1, 1.0, 0.0).astype(BF16)

    def flip(v):
        return jnp.dot(mirror, v, preferred_element_type=F32)

    s8 = lax.broadcasted_iota(jnp.int32, (ROWS, 8, chan), 1)

    def column(block, at):
        return jnp.sum(jnp.where(s8 == at, block, 0.0), axis=1)

    tail = jnp.zeros((wide - side, chan), F32)

    def widen(v):
        return jnp.concatenate([v, tail], axis=0)

    loads[0].wait()
    for c in range(chunks):
        lo = c * ROWS
        col_a[lo:lo + ROWS, :] = silu(column(x_in[lo:lo + ROWS, 0:8, :].astype(F32), 0))
        col_b[lo:lo + ROWS, :] = silu(column(x_in[lo:lo + ROWS, side - 8:side, :].astype(F32), 7))
    for col in (col_a, col_b, col_c, col_d):
        col[side:wide, :] = tail
    ends[me, 0] = widen(silu(x_in[0].astype(F32))).astype(BF16)
    ends[me, 1] = col_b[...].astype(BF16)
    ends[me, 2] = flip(widen(silu(x_in[side - 1].astype(F32))).astype(BF16)).astype(BF16)
    ends[me, 3] = flip(col_a[...].astype(BF16)).astype(BF16)
    pl.semaphore_wait(barrier, n_sp + n_dp - 2)
    pair_begin(ends, es, er)
    loads[1].wait()
    for c in range(chunks):
        lo = c * ROWS
        col_c[lo:lo + ROWS, :] = column(g_in[lo:lo + ROWS, 0:8, :].astype(F32), 0)
        col_d[lo:lo + ROWS, :] = column(g_in[lo:lo + ROWS, side - 8:side, :].astype(F32), 7)
    gends[me, 0] = flip(widen(g_in[0].astype(F32)).astype(BF16)).astype(BF16)
    gends[me, 1] = flip(col_d[...].astype(BF16)).astype(BF16)
    gends[me, 2] = widen(g_in[side - 1].astype(F32)).astype(BF16)
    gends[me, 3] = col_c[...].astype(BF16)
    loads[2].wait()
    lane = lax.broadcasted_iota(jnp.int32, (1, chan), 1)
    row = jnp.zeros((1, chan), jnp.int32)
    for k in range(8):
        for part in range(2):
            row = jnp.where(lane == 2 * k + part, adj[0, part, k], row)
    adj_row[me] = row
    pair_begin(adj_row, js, jr)
    pair_begin(gends, cs, cr)

    three = 3 * chan
    pairs = side // 2
    zero_row = jnp.zeros((wide, three), BF16)
    for buf in (taps, gtaps):
        buf[0, :, three:] = zero_row
        buf[pairs + 1, :, 0:three] = zero_row

    def shifts(v):
        return jnp.concatenate(
            [pltpu.roll(v, 1, 0).astype(BF16), v.astype(BF16), pltpu.roll(v, wide - 1, 0).astype(BF16)], axis=1)

    def spread(c, carry):
        for part in range(2):
            rows = []
            for k in range(ROWS // 2):
                i = c * ROWS + 2 * k + part
                p = c * (ROWS // 2) + k + 1
                a = widen(silu(x_in[i].astype(F32)))
                rows.append(a.astype(BF16))
                taps[p, :, part * three:(part + 1) * three] = shifts(a)
                gtaps[p, :, part * three:(part + 1) * three] = shifts(widen(g_in[i].astype(F32)))
            n = ROWS // 2 * wide
            flat[part * chan:(part + 1) * chan, pl.ds(pl.multiple_of(c * n, n), n)] = jnp.concatenate(rows, axis=0).T
        return carry

    lax.fori_loop(0, chunks, spread, 0)

    def grads(first, part):
        return gtaps[first:first + pairs, :, part * three:(part + 1) * three].reshape(pairs * wide, three)

    odd = jnp.dot(flat[...], grads(1, 1), preferred_element_type=F32)
    even = jnp.dot(flat[...], grads(1, 0), preferred_element_type=F32)
    below = jnp.dot(flat[0:chan], grads(0, 1), preferred_element_type=F32)
    above = jnp.dot(flat[chan:2 * chan], grads(2, 0), preferred_element_type=F32)
    for r, v in enumerate((odd[:chan] + above, odd[chan:] + even[:chan], even[chan:] + below)):
        for b in range(3):
            at = (3 * r + 2 - b) * chan
            wgf[at:at + chan, :] = v[:, b * chan:(b + 1) * chan]
    used = 9 * chan
    if wgf.shape[0] > used:
        wgf[used:, :] = jnp.zeros((wgf.shape[0] - used, chan), F32)

    size = full.shape[1]
    half = chips * size
    swap = remote(
        wgf.at[pl.ds(pl.multiple_of((1 - core) * half, 16), half)], half_in, hs.at[0], hr.at[0], partner)
    swap.start()

    loads[3].wait()
    loads[4].wait()
    for r in range(3):
        for c in range(3):
            block = w_in[2 - r, (2 - c) * chan:(3 - c) * chan, :].astype(F32)
            wt[r, c * chan:(c + 1) * chan, :] = block.T.astype(BF16)
    for k in range(3):
        to = slice(k * chan, (k + 1) * chan)
        for e, (r, c) in enumerate(((2, 2 - k), (2 - k, 0), (0, k), (k, 2))):
            vt[e, to, :] = wt[r, c * chan:(c + 1) * chan, :]
    blank = jnp.zeros((three, chan), BF16)
    for buf, one in ((pair_w, w_in), (pair_t, wt)):
        for k in range(4):
            at = slice(k * three, (k + 1) * three)
            buf[at, 0:chan] = one[k] if k < 3 else blank
            buf[at, chan:] = one[k - 1] if k > 0 else blank
    swap.wait()

    def half_rows(h):
        at = pl.multiple_of(h * size, 16)
        return wgf[pl.ds(pl.multiple_of(core * half + h * size, 16), size), :] + half_in[pl.ds(at, size), :]

    def scatter_copy(k):
        peer = alike(k)
        start = remote(sent.at[peer // 2], parts.at[chip], ss.at[peer // 2], sr.at[chip], peer)
        wait = remote(sent.at[peer // 2], parts.at[peer // 2], ss.at[peer // 2], sr.at[peer // 2], peer)
        return start, wait

    def scatter_start(k, c):
        h = alike(k) // 2
        sent[h] = encode(half_rows(h))
        scatter_copy(k)[0].start()
        return c

    lax.fori_loop(1, chips, scatter_start, 0)

    pair_relay(adj_row, js, jr)
    pair_relay(ends, es, er)

    def two_rows(buf, first, w):
        rows = jnp.concatenate([
            buf[pl.ds(first, PAIRS), :, three:].reshape(PAIRS * wide, three),
            buf[pl.ds(first + 1, PAIRS)].reshape(PAIRS * wide, 2 * three),
            buf[pl.ds(first + 2, PAIRS), :, 0:three].reshape(PAIRS * wide, three)], axis=1)
        return jnp.dot(rows, w[...], preferred_element_type=F32).reshape(PAIRS, wide, 2 * chan)

    def grad_chunk(c, carry):
        pad_grad[pl.ds(c * PAIRS, PAIRS)] = two_rows(gtaps, c * PAIRS, pair_t)
        return carry

    lax.fori_loop(0, pairs // PAIRS, grad_chunk, 0)

    pair_finish(adj_row, js, jr)
    spill = pltpu.make_async_copy(adj_row, adj_all, in_sem.at[5])
    spill.start()
    pair_relay(gends, cs, cr)
    pair_finish(ends, es, er)
    spill.wait()

    group = la.shape[1] // wide
    corr[...] = jnp.zeros_like(corr)

    def rim_groups(parity):
        def rim_group(n, carry):
            def fill(j, c2):
                t = 2 * (n * group + j) + parity
                at = pl.ds(pl.multiple_of(j * wide, 16), wide)
                for e in range(4):
                    v = ends[adj_all[t, 0, 2 * e], adj_all[t, 0, 2 * e + 1]].astype(F32)
                    k = ends[adj_all[t, 0, 8 + 2 * e], adj_all[t, 0, 9 + 2 * e]].astype(F32)[0:1]
                    la[e, at, :] = jnp.where(r64 < side, v, jnp.where(r64 == side, k, 0.0)).astype(BF16)
                    lg[e, at, :] = shifts(gends[t, e].astype(F32))
                return c2

            lax.fori_loop(0, group, fill, 0)
            for e in range(4):
                res = jnp.dot(la[e].T, lg[e], preferred_element_type=F32)
                for k in range(3):
                    r, c = ((0, k), (k, 2), (2, 2 - k), (2 - k, 0))[e]
                    at = (3 * r + c) * chan
                    corr[at:at + chan, :] += res[:, k * chan:(k + 1) * chan]
            return carry

        lax.fori_loop(0, chips // group, rim_group, 0)

    rim_groups(core)
    pair_finish(gends, cs, cr)
    rim_groups(1 - core)

    def scatter_wait(k, c):
        scatter_copy(k)[1].wait()
        return c

    lax.fori_loop(1, chips, scatter_wait, 0)
    slot = core * chips + chip
    mine = half_rows(chip) + corr[pl.ds(pl.multiple_of(slot * size, 16), size), :]
    mine = lax.fori_loop(1, chips, lambda k, t: t + decode(parts[alike(k) // 2]), mine)
    dps[my_dp] = encode(mine)

    def sample_copy(k):
        peer = lax.rem(my_dp + k, n_dp)
        start = remote(dps.at[my_dp], dps.at[my_dp], ds_.at[peer], dr.at[my_dp], me, peer)
        wait = remote(dps.at[my_dp], dps.at[peer], ds_.at[peer], dr.at[peer], me, peer)
        return start, wait

    def sample_start(k, c):
        sample_copy(k)[0].start()
        return c

    def sample_wait(k, c):
        sample_copy(k)[1].wait()
        return c

    lax.fori_loop(1, n_dp, sample_start, 0)

    def near(buf, e):
        return buf[adj[0, 0, e], adj[0, 1, e]]

    corner = [ends[adj[0, 0, 4 + k], adj[0, 1, 4 + k]].astype(F32)[0:1] for k in range(4)]

    def rim_row(v, behind, ahead):
        return jnp.where(r64 < side, v, jnp.where(r64 == side, behind, jnp.where(r64 == wide - 1, ahead, 0.0)))

    taps[0, :, three:] = shifts(rim_row(flip(near(ends, 0)), corner[1], corner[0]))
    taps[pairs + 1, :, 0:three] = shifts(rim_row(near(ends, 2).astype(F32), corner[2], corner[3]))
    col_a[...] = near(ends, 3).astype(F32)
    col_b[...] = flip(near(ends, 1))
    some = ROWS // 2
    s16 = lax.broadcasted_iota(jnp.int32, (some, 16, chan), 1)
    at_right = (side - 1) // 16 * 16
    for c in range(chunks):
        p = slice(c * some + 1, (c + 1) * some + 1)
        for part in range(2):
            rows = pl.ds(c * ROWS + part, some, stride=2)
            at = slice(part * three, part * three + chan)
            v = jnp.where(s16 == 0, col_a[rows, :][:, None, :], taps[p, 0:16, at].astype(F32))
            taps[p, 0:16, at] = v.astype(BF16)
            at = slice(part * three + 2 * chan, (part + 1) * three)
            v = taps[p, at_right:at_right + 16, at].astype(F32)
            v = jnp.where(s16 == side - 1 - at_right, col_b[rows, :][:, None, :], v)
            taps[p, at_right:at_right + 16, at] = v.astype(BF16)

    def conv_chunk(c, carry):
        conv = two_rows(taps, c * PAIRS, pair_w)
        for k in range(2 * PAIRS):
            i = 2 * PAIRS * c + k
            at = k % 2 * chan
            out[i] = (x_in[i].astype(F32) + conv[k // 2, 0:side, at:at + chan] + bias[...]).astype(BF16)
        return carry

    lax.fori_loop(0, pairs // PAIRS, conv_chunk, 0)

    lax.fori_loop(1, n_dp, sample_wait, 0)
    total = decode(dps[0])
    for d in range(1, n_dp):
        total = total + decode(dps[d])
    full[me] = total.astype(BF16)
    pair_begin(full, gs, gr)

    def rim_grad(e):
        at = adj[0, 1, e]
        v = jnp.dot(shifts(gends[adj[0, 0, e], at].astype(F32)), vt[at], preferred_element_type=F32)
        return jnp.where(r64 < side, v, 0.0).astype(BF16)

    def rim_corner(k):
        at = adj[0, 1, 4 + k]
        v = jnp.dot(gends[adj[0, 0, 4 + k], at], vt[at, 0:chan, :], preferred_element_type=F32)
        return v[side - 1:side].astype(BF16).astype(F32)

    add = [rim_corner(k) for k in range(4)]
    pad_grad[0, :, 0:chan] += rim_grad(0).astype(F32)
    pad_grad[pairs - 1, :, chan:] += flip(rim_grad(2))
    col_a[...] = flip(rim_grad(3)) + jnp.where(r64 == 0, add[0], jnp.where(r64 == side - 1, add[3], 0.0))
    col_b[...] = rim_grad(1).astype(F32) + jnp.where(r64 == 0, add[1], jnp.where(r64 == side - 1, add[2], 0.0))

    r56 = lax.broadcasted_iota(jnp.int32, (side, chan), 0)

    def finish_rows(c, carry):
        for k in range(ROWS):
            i = c * ROWS + k
            p = pad_grad[c * (ROWS // 2) + k // 2, 0:side, k % 2 * chan:(k % 2 + 1) * chan]
            p = p + jnp.where(r56 == 0, col_a[pl.ds(i, 1), :], jnp.where(r56 == side - 1, col_b[pl.ds(i, 1), :], 0.0))
            v = x_in[i].astype(F32)
            s = 1.0 / (1.0 + jnp.exp(-v))
            gin_out[i] = (g_in[i].astype(F32) + p * s * (1.0 + v * (1.0 - s))).astype(BF16)
        return carry

    lax.fori_loop(0, chunks, finish_rows, 0)

    pair_relay(full, gs, gr)
    pair_finish(full, gs, gr)

    def open_rows(t, carry):
        at = (lax.rem(t, 2) * chips + t // 2) * size
        wg_out[pl.ds(pl.multiple_of(at, 16), size), :] = full[t].astype(F32)
        return carry

    lax.fori_loop(0, n_sp, open_rows, 0)


def hand_on(a, wg, c, a_out, wg_out, c_out, sems):
    used = wg_out.shape[0]
    copies = [
        pltpu.make_async_copy(a, a_out, sems.at[0]),
        pltpu.make_async_copy(c, c_out, sems.at[1]),
        pltpu.make_async_copy(wg.at[pl.ds(0, used)], wg_out, sems.at[2]),
    ]
    for one in copies:
        one.start()
    for one in copies:
        one.wait()


def per_device(n_sp, n_dp, block_in, weights, out_bias, adjacency, cotangent):
    side, chan = block_in.shape[2], block_in.shape[4]
    wide = wide_of(side)
    chips = n_sp // 2
    size = -(-9 * chan // (16 * n_sp)) * 16
    group = min(chips, 4)
    vmem = pl.BlockSpec(memory_space=pltpu.VMEM)
    hbm = pl.BlockSpec(memory_space=pltpu.HBM)
    sem = pltpu.SemaphoreType.DMA
    tile = (side, side, chan)
    held = pl.pallas_call(
        functools.partial(block_kernel, n_sp, n_dp, side),
        out_shape=(pltpu.VMEM(tile, BF16), pltpu.VMEM((n_sp * size, chan), F32), pltpu.VMEM(tile, BF16)),
        in_specs=[hbm] * 5,
        out_specs=(vmem, vmem, vmem),
        scratch_shapes=[
            pltpu.VMEM(tile, BF16),
            pltpu.VMEM(tile, BF16),
            pltpu.VMEM((3, 3 * chan, chan), BF16),
            pltpu.VMEM((1, chan), F32),
            pltpu.SMEM((1, 2, 8), jnp.int32),
            pltpu.SMEM((n_sp, 1, chan), jnp.int32),
            pltpu.VMEM((n_sp, 1, chan), jnp.int32),
            pltpu.VMEM((side // 2 + 2, wide, 6 * chan), BF16),
            pltpu.VMEM((side // 2 + 2, wide, 6 * chan), BF16),
            pltpu.VMEM((2 * chan, side // 2 * wide), BF16),
            pltpu.VMEM((side // 2, wide, 2 * chan), F32),
            pltpu.VMEM((3, 3 * chan, chan), BF16),
            pltpu.VMEM((4, 3 * chan, chan), BF16),
            pltpu.VMEM((12 * chan, 2 * chan), BF16),
            pltpu.VMEM((12 * chan, 2 * chan), BF16),
            pltpu.VMEM((n_sp * size, chan), F32),
            pltpu.VMEM((n_sp * size, chan), F32),
            pltpu.VMEM((chips * size, chan), F32),
            pltpu.VMEM((wide, chan), F32),
            pltpu.VMEM((wide, chan), F32),
            pltpu.VMEM((wide, chan), F32),
            pltpu.VMEM((wide, chan), F32),
            pltpu.VMEM((n_sp, 4, wide, chan), BF16),
            pltpu.VMEM((n_sp, 4, wide, chan), BF16),
            pltpu.VMEM((4, group * wide, chan), BF16),
            pltpu.VMEM((4, group * wide, 3 * chan), BF16),
            pltpu.VMEM((chips, size + 16, chan), CODE),
            pltpu.VMEM((chips, size + 16, chan), CODE),
            pltpu.VMEM((n_dp, size + 16, chan), CODE),
            pltpu.VMEM((n_sp, size, chan), BF16),
            sem((6,)), sem((n_sp,)), sem((n_sp,)),
            sem((n_sp,)), sem((n_sp,)), sem((n_sp,)), sem((n_sp,)), sem((1,)), sem((1,)),
            sem((chips,)), sem((chips,)), sem((n_dp,)), sem((n_dp,)), sem((n_sp,)), sem((n_sp,)),
        ],
        compiler_params=pltpu.CompilerParams(
            collective_id=0, has_side_effects=True, vmem_limit_bytes=58 * 2**20),
    )(
        adjacency.transpose(0, 2, 1), block_in[0, 0], weights.reshape(3, 3 * chan, chan), out_bias.reshape(1, chan),
        cotangent[0, 0],
    )
    result, wgrad, grad_in = pl.pallas_call(
        hand_on,
        out_shape=(
            jax.ShapeDtypeStruct(tile, BF16), jax.ShapeDtypeStruct((9 * chan, chan), F32), jax.ShapeDtypeStruct(tile, BF16)),
        in_specs=[vmem, vmem, vmem],
        out_specs=(hbm, hbm, hbm),
        scratch_shapes=[sem((3,))],
        compiler_params=pltpu.CompilerParams(vmem_limit_bytes=4 * 2**20),
    )(*held)
    return (result[None, None], wgrad.reshape(weights.shape), grad_in[None, None])


def solution(mesh):
    placed = (
        P("dp", "space", None, None, None),
        P(),
        P(),
        P("space", None, None),
        P("dp", "space", None, None, None),
    )
    return jax.shard_map(
        functools.partial(per_device, mesh.shape["space"], mesh.shape["dp"]),
        mesh=mesh,
        in_specs=placed,
        out_specs=(P("dp", "space", None, None, None), P(), P("dp", "space", None, None, None)),
        check_vma=False,
    )
```

```python
import functools

import jax
import jax.numpy as jnp
from jax import lax
from jax.experimental import pallas as pl
from jax.experimental.pallas import tpu as pltpu
from jax.sharding import PartitionSpec as P

MESH = pl.DeviceIdType.MESH
ROWS = 8
PAIRS = 7
F32 = jnp.float32
BF16 = jnp.bfloat16
CODE = jnp.int16


def silu(v):
    h = 0.5 * v
    return h + h * jnp.tanh(h)


def encode(v):
    top = jnp.maximum(jnp.max(jnp.abs(v), axis=0, keepdims=True), 1e-30)
    power = jnp.ceil(jnp.log2(top))
    code = jnp.clip(jnp.round(v * jnp.exp2(15.0 - power)), -32767.0, 32767.0)
    rows = jnp.concatenate([code, jnp.broadcast_to(power, (16, v.shape[1]))], axis=0)
    return rows.astype(jnp.int32).astype(CODE)


def decode(rows):
    v = rows.astype(jnp.int32).astype(F32)
    size = v.shape[0] - 16
    return v[:size] * jnp.exp2(v[size:size + 1] - 15.0)


def wide_of(side):
    return -(-(side + 4) // 16) * 16


def block_kernel(
    n_sp, n_dp, side,
    adj_hbm, x_hbm, w_hbm, bias_hbm, g_hbm,
    out, wg_out, gin_out,
    x_in, g_in, w_in, bias, adj, adj_all, adj_row,
    taps, gtaps, flat, pad_grad, wt, vt, pair_w, pair_t, wgf, corr, half_in, col_a, col_b, col_c, col_d,
    ends, packed, gends, la, lg, sent, parts, dps, full,
    in_sem, edge_sem, pack_sem, adj_sem, swap_sem, share_sem, sample_sem, full_sem, near_sem,
):
    wide = wide_of(side)
    chan = 128
    chunks = side // ROWS
    me = lax.axis_index("space")
    my_dp = lax.axis_index("dp")
    core = lax.rem(me, 2)
    chip = me // 2
    chips = n_sp // 2
    partner = me + 1 - 2 * core

    barrier = pltpu.get_barrier_semaphore()

    def greet_sp(k, c):
        pl.semaphore_signal(barrier, inc=1, device_id=(lax.rem(me + k, n_sp), my_dp), device_id_type=MESH)
        return c

    def greet_dp(k, c):
        pl.semaphore_signal(barrier, inc=1, device_id=(me, lax.rem(my_dp + k, n_dp)), device_id_type=MESH)
        return c

    loads = [
        pltpu.make_async_copy(adj_hbm, adj, in_sem.at[2]),
        pltpu.make_async_copy(x_hbm, x_in, in_sem.at[0]),
        pltpu.make_async_copy(g_hbm, g_in, in_sem.at[1]),
        pltpu.make_async_copy(w_hbm, w_in, in_sem.at[3]),
        pltpu.make_async_copy(bias_hbm, bias, in_sem.at[4]),
    ]
    for one in loads:
        one.start()
    lax.fori_loop(1, n_sp, greet_sp, 0)
    lax.fori_loop(1, n_dp, greet_dp, 0)

    def alike(k):
        return lax.rem(me + 2 * k, n_sp)

    def remote(src, dst, send, recv, peer, dp=None):
        return pltpu.make_async_remote_copy(
            src_ref=src, dst_ref=dst, send_sem=send, recv_sem=recv,
            device_id=(peer, my_dp if dp is None else dp), device_id_type=MESH)

    def take(buf, count, sem):
        some = buf.at[pl.ds(0, count)]
        pltpu.make_async_copy(some, some, sem).wait()

    def pair_begin(buf, sems):
        mine = buf.at[me]
        def go(k, c):
            remote(mine, mine, sems.at[0], sems.at[2], alike(k)).start()
            return c
        lax.fori_loop(1, chips, go, 0)
        remote(mine, mine, sems.at[0], sems.at[1], partner).start()

    def pair_relay(buf, sems):
        take(buf, chips - 1, sems.at[2])
        def go(k, c):
            other = buf.at[alike(k)]
            remote(other, other, sems.at[0], sems.at[1], partner).start()
            return c
        lax.fori_loop(1, chips, go, 0)

    def pair_finish(buf, sems):
        take(buf, chips, sems.at[1])
        take(buf, n_sp - 1, sems.at[0])

    r64 = lax.broadcasted_iota(jnp.int32, (wide, chan), 0)
    ra = lax.broadcasted_iota(jnp.int32, (wide, wide), 0)
    rb = lax.broadcasted_iota(jnp.int32, (wide, wide), 1)
    mirror = jnp.where(ra + rb == side - 1, 1.0, 0.0).astype(BF16)

    def flip(v):
        return jnp.dot(mirror, v, preferred_element_type=F32)

    s8 = lax.broadcasted_iota(jnp.int32, (ROWS, 8, chan), 1)

    def column(block, at):
        return jnp.sum(jnp.where(s8 == at, block, 0.0), axis=1)

    tail = jnp.zeros((wide - side, chan), F32)

    def widen(v):
        return jnp.concatenate([v, tail], axis=0)

    loads[0].wait()
    lane = lax.broadcasted_iota(jnp.int32, (1, chan), 1)
    row = jnp.zeros((1, chan), jnp.int32)
    for k in range(8):
        for part in range(2):
            row = jnp.where(lane == 2 * k + part, adj[0, part, k], row)
    adj_row[me] = row
    loads[1].wait()
    for c in range(chunks):
        lo = c * ROWS
        col_a[lo:lo + ROWS, :] = silu(column(x_in[lo:lo + ROWS, 0:8, :].astype(F32), 0))
        col_b[lo:lo + ROWS, :] = silu(column(x_in[lo:lo + ROWS, side - 8:side, :].astype(F32), 7))
    for col in (col_a, col_b, col_c, col_d):
        col[side:wide, :] = tail
    loads[2].wait()
    for c in range(chunks):
        lo = c * ROWS
        col_c[lo:lo + ROWS, :] = column(g_in[lo:lo + ROWS, 0:8, :].astype(F32), 0)
    spare = wide - side

    def fill_up(v, at):
        return jnp.concatenate([v[0:side], col_c[at * spare:(at + 1) * spare, :]], axis=0).astype(BF16)

    ends[me, 0] = fill_up(silu(x_in[0].astype(F32)), 0)
    ends[me, 1] = fill_up(col_b[...], 1)
    ends[me, 2] = fill_up(flip(widen(silu(x_in[side - 1].astype(F32))).astype(BF16)), 2)
    ends[me, 3] = fill_up(flip(col_a[...].astype(BF16)), 3)
    pl.semaphore_wait(barrier, n_sp + n_dp - 2)
    pair_begin(adj_row, adj_sem)
    pair_begin(ends, edge_sem)
    for c in range(chunks):
        lo = c * ROWS
        col_d[lo:lo + ROWS, :] = column(g_in[lo:lo + ROWS, side - 8:side, :].astype(F32), 7)
    packed[me, 0] = fill_up(flip(widen(g_in[0].astype(F32)).astype(BF16)), 4)
    packed[me, 1] = fill_up(flip(col_d[...].astype(BF16)), 5)
    packed[me, 2] = fill_up(g_in[side - 1].astype(F32), 6)
    pair_begin(packed, pack_sem)

    three = 3 * chan
    pairs = side // 2
    zero_row = jnp.zeros((wide, three), BF16)
    for buf in (taps, gtaps):
        buf[0, :, three:] = zero_row
        buf[pairs + 1, :, 0:three] = zero_row

    def shifts(v):
        return jnp.concatenate(
            [pltpu.roll(v, 1, 0).astype(BF16), v.astype(BF16), pltpu.roll(v, wide - 1, 0).astype(BF16)], axis=1)

    def spread(c, carry):
        for part in range(2):
            rows = []
            for k in range(ROWS // 2):
                i = c * ROWS + 2 * k + part
                p = c * (ROWS // 2) + k + 1
                a = widen(silu(x_in[i].astype(F32)))
                rows.append(a.astype(BF16))
                taps[p, :, part * three + chan:part * three + 2 * chan] = rows[-1]
                gtaps[p, :, part * three:(part + 1) * three] = shifts(widen(g_in[i].astype(F32)))
            n = ROWS // 2 * wide
            flat[part * chan:(part + 1) * chan, pl.ds(pl.multiple_of(c * n, n), n)] = jnp.concatenate(rows, axis=0).T
        return carry

    lax.fori_loop(0, chunks, spread, 0)

    def grads(first, part):
        return gtaps[first:first + pairs, :, part * three:(part + 1) * three].reshape(pairs * wide, three)

    odd = jnp.dot(flat[...], grads(1, 1), preferred_element_type=F32)
    even = jnp.dot(flat[...], grads(1, 0), preferred_element_type=F32)
    below = jnp.dot(flat[0:chan], grads(0, 1), preferred_element_type=F32)
    above = jnp.dot(flat[chan:2 * chan], grads(2, 0), preferred_element_type=F32)
    for r, v in enumerate((odd[:chan] + above, odd[chan:] + even[:chan], even[chan:] + below)):
        for b in range(3):
            at = (3 * r + 2 - b) * chan
            wgf[at:at + chan, :] = v[:, b * chan:(b + 1) * chan]
    used = 9 * chan
    if wgf.shape[0] > used:
        wgf[used:, :] = jnp.zeros((wgf.shape[0] - used, chan), F32)

    size = full.shape[1]
    half = chips * size
    swap = remote(
        wgf.at[pl.ds(pl.multiple_of((1 - core) * half, 16), half)], half_in, swap_sem.at[0], swap_sem.at[1], partner)
    swap.start()

    loads[3].wait()
    loads[4].wait()
    for r in range(3):
        for c in range(3):
            block = w_in[2 - r, (2 - c) * chan:(3 - c) * chan, :].astype(F32)
            wt[r, c * chan:(c + 1) * chan, :] = block.T.astype(BF16)
    for k in range(3):
        to = slice(k * chan, (k + 1) * chan)
        for e, (r, c) in enumerate(((2, 2 - k), (2 - k, 0), (0, k), (k, 2))):
            vt[e, to, :] = wt[r, c * chan:(c + 1) * chan, :]
    blank = jnp.zeros((three, chan), BF16)
    for buf, one in ((pair_w, w_in), (pair_t, wt)):
        for k in range(4):
            at = slice(k * three, (k + 1) * three)
            buf[at, 0:chan] = one[k] if k < 3 else blank
            buf[at, chan:] = one[k - 1] if k > 0 else blank
    swap.wait()

    def half_rows(h):
        at = pl.multiple_of(h * size, 16)
        return wgf[pl.ds(pl.multiple_of(core * half + h * size, 16), size), :] + half_in[pl.ds(at, size), :]

    def scatter_copy(k):
        h = alike(k) // 2
        return remote(sent.at[h], parts.at[chip], share_sem.at[0], share_sem.at[1], alike(k))

    def scatter_start(k, c):
        h = alike(k) // 2
        sent[h] = encode(half_rows(h))
        scatter_copy(k).start()
        return c

    lax.fori_loop(1, chips, scatter_start, 0)

    pair_relay(adj_row, adj_sem)
    pair_relay(ends, edge_sem)

    def two_rows(buf, first, w):
        rows = jnp.concatenate([
            buf[pl.ds(first, PAIRS), :, three:].reshape(PAIRS * wide, three),
            buf[pl.ds(first + 1, PAIRS)].reshape(PAIRS * wide, 2 * three),
            buf[pl.ds(first + 2, PAIRS), :, 0:three].reshape(PAIRS * wide, three)], axis=1)
        return jnp.dot(rows, w[...], preferred_element_type=F32).reshape(PAIRS, wide, 2 * chan)

    def grad_chunk(c, carry):
        pad_grad[pl.ds(c * PAIRS, PAIRS)] = two_rows(gtaps, c * PAIRS, pair_t)
        return carry

    early = pairs // PAIRS // 2
    lax.fori_loop(0, early, grad_chunk, 0)

    pair_finish(adj_row, adj_sem)
    spill = pltpu.make_async_copy(adj_row, adj_all, in_sem.at[5])
    spill.start()
    pair_relay(packed, pack_sem)
    pair_finish(ends, edge_sem)
    spill.wait()

    group = la.shape[1] // wide
    corr[...] = jnp.zeros_like(corr)

    def rim_groups(parity):
        def rim_group(n, carry):
            def fill(j, c2):
                t = 2 * (n * group + j) + parity
                at = pl.ds(pl.multiple_of(j * wide, 16), wide)
                over = [ends[t, e].astype(F32)[side:wide] for e in range(4)]
                for e in range(4):
                    if e < 3:
                        g = packed[t, e].astype(F32)
                        over.append(g[side:wide])
                        g = jnp.where(r64 < side, g, 0.0)
                    else:
                        g = widen(jnp.concatenate(over, axis=0))
                    gends[t, e] = g.astype(BF16)
                    lg[e, at, :] = shifts(g)
                    v = ends[adj_all[t, 0, 2 * e], adj_all[t, 0, 2 * e + 1]].astype(F32)
                    k = ends[adj_all[t, 0, 8 + 2 * e], adj_all[t, 0, 9 + 2 * e]].astype(F32)[0:1]
                    la[e, at, :] = jnp.where(r64 < side, v, jnp.where(r64 == side, k, 0.0)).astype(BF16)
                return c2

            lax.fori_loop(0, group, fill, 0)
            for e in range(4):
                res = jnp.dot(la[e].T, lg[e], preferred_element_type=F32)
                for k in range(3):
                    r, c = ((0, k), (k, 2), (2, 2 - k), (2 - k, 0))[e]
                    at = (3 * r + c) * chan
                    corr[at:at + chan, :] += res[:, k * chan:(k + 1) * chan]
            return carry

        lax.fori_loop(0, chips // group, rim_group, 0)

    rim_groups(core)
    pair_finish(packed, pack_sem)
    rim_groups(1 - core)

    take(parts, chips - 1, share_sem.at[1])
    take(sent, chips - 1, share_sem.at[0])
    slot = core * chips + chip
    mine = half_rows(chip) + corr[pl.ds(pl.multiple_of(slot * size, 16), size), :]
    mine = lax.fori_loop(1, chips, lambda k, t: t + decode(parts[alike(k) // 2]), mine)
    dps[my_dp] = encode(mine)

    def sample_start(k, c):
        one = dps.at[my_dp]
        remote(one, one, sample_sem.at[0], sample_sem.at[1], me, lax.rem(my_dp + k, n_dp)).start()
        return c

    lax.fori_loop(1, n_dp, sample_start, 0)

    def near(buf, e):
        return buf[adj[0, 0, e], adj[0, 1, e]]

    corner = [ends[adj[0, 0, 4 + k], adj[0, 1, 4 + k]].astype(F32)[0:1] for k in range(4)]

    def rim_row(v, behind, ahead):
        return jnp.where(r64 < side, v, jnp.where(r64 == side, behind, jnp.where(r64 == wide - 1, ahead, 0.0)))

    taps[0, :, three:] = shifts(rim_row(flip(near(ends, 0)), corner[1], corner[0]))
    taps[pairs + 1, :, 0:three] = shifts(rim_row(near(ends, 2).astype(F32), corner[2], corner[3]))
    col_a[...] = near(ends, 3).astype(F32)
    col_b[...] = flip(near(ends, 1))

    def spread_act(c, carry):
        for part in range(2):
            at = part * three
            for k in range(ROWS // 2):
                p = c * (ROWS // 2) + k + 1
                i = pl.ds(c * ROWS + 2 * k + part, 1)
                v = taps[p, :, at + chan:at + 2 * chan].astype(F32)
                taps[p, :, at:at + chan] = jnp.where(r64 == 0, col_a[i, :], pltpu.roll(v, 1, 0)).astype(BF16)
                taps[p, :, at + 2 * chan:at + three] = jnp.where(
                    r64 == side - 1, col_b[i, :], pltpu.roll(v, wide - 1, 0)).astype(BF16)
        return carry

    lax.fori_loop(0, chunks, spread_act, 0)
    lax.fori_loop(early, pairs // PAIRS, grad_chunk, 0)

    def conv_chunk(c, carry):
        conv = two_rows(taps, c * PAIRS, pair_w)
        for k in range(2 * PAIRS):
            i = 2 * PAIRS * c + k
            at = k % 2 * chan
            out[i] = (x_in[i].astype(F32) + conv[k // 2, 0:side, at:at + chan] + bias[...]).astype(BF16)
        return carry

    lax.fori_loop(0, pairs // PAIRS, conv_chunk, 0)

    take(dps, n_dp - 1, sample_sem.at[1])
    take(dps, n_dp - 1, sample_sem.at[0])
    total = decode(dps[0])
    for d in range(1, n_dp):
        total = total + decode(dps[d])
    full[me] = total.astype(BF16)

    def share_copy(k):
        one = full.at[me]
        return remote(one, one, full_sem.at[0], near_sem.at[k], alike(k))

    def share_start(k, c):
        share_copy(k).start()
        return c

    lax.fori_loop(1, chips, share_start, 0)
    remote(full.at[me], full.at[me], full_sem.at[0], full_sem.at[1], partner).start()

    def rim_grad(e):
        at = adj[0, 1, e]
        v = jnp.dot(shifts(gends[adj[0, 0, e], at].astype(F32)), vt[at], preferred_element_type=F32)
        return jnp.where(r64 < side, v, 0.0).astype(BF16)

    def rim_corner(k):
        at = adj[0, 1, 4 + k]
        v = jnp.dot(gends[adj[0, 0, 4 + k], at], vt[at, 0:chan, :], preferred_element_type=F32)
        return v[side - 1:side].astype(BF16).astype(F32)

    add = [rim_corner(k) for k in range(4)]
    pad_grad[0, :, 0:chan] += rim_grad(0).astype(F32)
    pad_grad[pairs - 1, :, chan:] += flip(rim_grad(2))
    col_a[...] = flip(rim_grad(3)) + jnp.where(r64 == 0, add[0], jnp.where(r64 == side - 1, add[3], 0.0))
    col_b[...] = rim_grad(1).astype(F32) + jnp.where(r64 == 0, add[1], jnp.where(r64 == side - 1, add[2], 0.0))

    r56 = lax.broadcasted_iota(jnp.int32, (side, chan), 0)

    def finish_rows(c, carry):
        for k in range(ROWS):
            i = c * ROWS + k
            p = pad_grad[c * (ROWS // 2) + k // 2, 0:side, k % 2 * chan:(k % 2 + 1) * chan]
            p = p + jnp.where(r56 == 0, col_a[pl.ds(i, 1), :], jnp.where(r56 == side - 1, col_b[pl.ds(i, 1), :], 0.0))
            v = x_in[i].astype(F32)
            s = 0.5 + 0.5 * jnp.tanh(0.5 * v)
            gin_out[i] = (g_in[i].astype(F32) + p * s * (1.0 + v * (1.0 - s))).astype(BF16)
        return carry

    lax.fori_loop(0, chunks, finish_rows, 0)

    def share_relay(n, c):
        k = chips - n
        take(full, 1, near_sem.at[k])
        other = full.at[alike(chips - k)]
        remote(other, other, full_sem.at[0], full_sem.at[1], partner).start()
        return c

    lax.fori_loop(1, chips, share_relay, 0)
    pair_finish(full, full_sem)

    def open_rows(t, carry):
        at = (lax.rem(t, 2) * chips + t // 2) * size
        wg_out[pl.ds(pl.multiple_of(at, 16), size), :] = full[t].astype(F32)
        return carry

    lax.fori_loop(0, n_sp, open_rows, 0)


def hand_on(a, wg, c, a_out, wg_out, c_out, sems):
    used = wg_out.shape[0]
    copies = [
        pltpu.make_async_copy(a, a_out, sems.at[0]),
        pltpu.make_async_copy(c, c_out, sems.at[1]),
        pltpu.make_async_copy(wg.at[pl.ds(0, used)], wg_out, sems.at[2]),
    ]
    for one in copies:
        one.start()
    for one in copies:
        one.wait()


def per_device(n_sp, n_dp, block_in, weights, out_bias, adjacency, cotangent):
    side, chan = block_in.shape[2], block_in.shape[4]
    wide = wide_of(side)
    chips = n_sp // 2
    size = -(-9 * chan // (16 * n_sp)) * 16
    group = min(chips, 4)
    vmem = pl.BlockSpec(memory_space=pltpu.VMEM)
    hbm = pl.BlockSpec(memory_space=pltpu.HBM)
    sem = pltpu.SemaphoreType.DMA
    tile = (side, side, chan)
    held = pl.pallas_call(
        functools.partial(block_kernel, n_sp, n_dp, side),
        out_shape=(pltpu.VMEM(tile, BF16), pltpu.VMEM((n_sp * size, chan), F32), pltpu.VMEM(tile, BF16)),
        in_specs=[hbm] * 5,
        out_specs=(vmem, vmem, vmem),
        scratch_shapes=[
            pltpu.VMEM(tile, BF16),
            pltpu.VMEM(tile, BF16),
            pltpu.VMEM((3, 3 * chan, chan), BF16),
            pltpu.VMEM((1, chan), F32),
            pltpu.SMEM((1, 2, 8), jnp.int32),
            pltpu.SMEM((n_sp, 1, chan), jnp.int32),
            pltpu.VMEM((n_sp, 1, chan), jnp.int32),
            pltpu.VMEM((side // 2 + 2, wide, 6 * chan), BF16),
            pltpu.VMEM((side // 2 + 2, wide, 6 * chan), BF16),
            pltpu.VMEM((2 * chan, side // 2 * wide), BF16),
            pltpu.VMEM((side // 2, wide, 2 * chan), F32),
            pltpu.VMEM((3, 3 * chan, chan), BF16),
            pltpu.VMEM((4, 3 * chan, chan), BF16),
            pltpu.VMEM((12 * chan, 2 * chan), BF16),
            pltpu.VMEM((12 * chan, 2 * chan), BF16),
            pltpu.VMEM((n_sp * size, chan), F32),
            pltpu.VMEM((n_sp * size, chan), F32),
            pltpu.VMEM((chips * size, chan), F32),
            pltpu.VMEM((wide, chan), F32),
            pltpu.VMEM((wide, chan), F32),
            pltpu.VMEM((wide, chan), F32),
            pltpu.VMEM((wide, chan), F32),
            pltpu.VMEM((n_sp, 4, wide, chan), BF16),
            pltpu.VMEM((n_sp, 3, wide, chan), BF16),
            pltpu.VMEM((n_sp, 4, wide, chan), BF16),
            pltpu.VMEM((4, group * wide, chan), BF16),
            pltpu.VMEM((4, group * wide, 3 * chan), BF16),
            pltpu.VMEM((chips, size + 16, chan), CODE),
            pltpu.VMEM((chips, size + 16, chan), CODE),
            pltpu.VMEM((n_dp, size + 16, chan), CODE),
            pltpu.VMEM((n_sp, size, chan), BF16),
            sem((6,)), sem((3,)), sem((3,)), sem((3,)), sem((2,)), sem((2,)), sem((2,)), sem((2,)), sem((chips,)),
        ],
        compiler_params=pltpu.CompilerParams(
            collective_id=0, has_side_effects=True, vmem_limit_bytes=58 * 2**20),
    )(
        adjacency.transpose(0, 2, 1), block_in[0, 0], weights.reshape(3, 3 * chan, chan), out_bias.reshape(1, chan),
        cotangent[0, 0],
    )
    result, wgrad, grad_in = pl.pallas_call(
        hand_on,
        out_shape=(
            jax.ShapeDtypeStruct(tile, BF16), jax.ShapeDtypeStruct((9 * chan, chan), F32), jax.ShapeDtypeStruct(tile, BF16)),
        in_specs=[vmem, vmem, vmem],
        out_specs=(hbm, hbm, hbm),
        scratch_shapes=[sem((3,))],
        compiler_params=pltpu.CompilerParams(vmem_limit_bytes=4 * 2**20),
    )(*held)
    return (result[None, None], wgrad.reshape(weights.shape), grad_in[None, None])


def solution(mesh):
    placed = (
        P("dp", "space", None, None, None),
        P(),
        P(),
        P("space", None, None),
        P("dp", "space", None, None, None),
    )
    return jax.shard_map(
        functools.partial(per_device, mesh.shape["space"], mesh.shape["dp"]),
        mesh=mesh,
        in_specs=placed,
        out_specs=(P("dp", "space", None, None, None), P(), P("dp", "space", None, None, None)),
        check_vma=False,
    )
```

```python
import functools

import jax
import jax.numpy as jnp
from jax import lax
from jax.experimental import pallas as pl
from jax.experimental.pallas import tpu as pltpu
from jax.sharding import PartitionSpec as P

MESH = pl.DeviceIdType.MESH
ROWS = 8
PAIRS = 7
F32 = jnp.float32
BF16 = jnp.bfloat16
CODE = jnp.int16


def silu(v):
    h = 0.5 * v
    return h + h * jnp.tanh(h)


def encode(v):
    top = jnp.maximum(jnp.max(jnp.abs(v), axis=0, keepdims=True), 1e-30)
    power = jnp.ceil(jnp.log2(top))
    code = jnp.clip(jnp.round(v * jnp.exp2(15.0 - power)), -32767.0, 32767.0)
    return code.astype(jnp.int32).astype(CODE), jnp.exp2(power - 15.0)


def decode(rows, scale):
    return rows.astype(jnp.int32).astype(F32) * scale


def wide_of(side):
    return -(-(side + 4) // 16) * 16


def block_kernel(
    n_sp, n_dp, side,
    adj_hbm, x_hbm, w_hbm, bias_hbm, g_hbm,
    out, wg_out, gin_out,
    x_in, g_in, w_in, bias, adj, adj_all, adj_row,
    taps, gtaps, flat, pad_grad, wt, vt, pair_w, pair_t, wgf, corr, half_in, col_a, col_b, col_c, col_d,
    ends, packed, gends, la, lat, lg, sent, sent_s, parts, parts_s, dps, dps_s, full,
    in_sem, edge_sem, pack_sem, adj_sem, swap_sem, share_sem, sample_sem, scale_sem, full_sem, near_sem,
):
    wide = wide_of(side)
    chan = 128
    chunks = side // ROWS
    me = lax.axis_index("space")
    my_dp = lax.axis_index("dp")
    core = lax.rem(me, 2)
    chip = me // 2
    chips = n_sp // 2
    partner = me + 1 - 2 * core

    barrier = pltpu.get_barrier_semaphore()

    def greet_sp(k, c):
        pl.semaphore_signal(barrier, inc=1, device_id=(lax.rem(me + k, n_sp), my_dp), device_id_type=MESH)
        return c

    def greet_dp(k, c):
        pl.semaphore_signal(barrier, inc=1, device_id=(me, lax.rem(my_dp + k, n_dp)), device_id_type=MESH)
        return c

    loads = [
        pltpu.make_async_copy(adj_hbm, adj, in_sem.at[2]),
        pltpu.make_async_copy(x_hbm, x_in, in_sem.at[0]),
        pltpu.make_async_copy(g_hbm, g_in, in_sem.at[1]),
        pltpu.make_async_copy(w_hbm, w_in, in_sem.at[3]),
        pltpu.make_async_copy(bias_hbm, bias, in_sem.at[4]),
    ]
    for one in loads:
        one.start()
    lax.fori_loop(1, n_sp, greet_sp, 0)
    lax.fori_loop(1, n_dp, greet_dp, 0)

    def each_chip(do):
        if chips == 4:
            for other in (3 - chip, lax.rem(chip + 2, 4), chip + 1 - 2 * lax.rem(chip, 2)):
                do(other)
        else:
            def go(k, c):
                do(lax.rem(chip + k, chips))
                return c
            lax.fori_loop(1, chips, go, 0)

    low = 1 - (2 * my_dp) // n_dp
    first_dp = low * (n_dp - 1 - my_dp) + (1 - low) * my_dp

    def each_dp(do):
        for j in range(n_dp - 1):
            at = j + (j - first_dp + n_dp) // n_dp
            do(low * (n_dp - 1 - at) + (1 - low) * at)

    def remote(src, dst, send, recv, peer, dp=None):
        return pltpu.make_async_remote_copy(
            src_ref=src, dst_ref=dst, send_sem=send, recv_sem=recv,
            device_id=(peer, my_dp if dp is None else dp), device_id_type=MESH)

    def take(buf, count, sem):
        some = buf.at[pl.ds(0, count)]
        pltpu.make_async_copy(some, some, sem).wait()

    def take_rows(buf, count, first, rows, sem):
        some = buf.at[pl.ds(0, count), pl.ds(first, rows)]
        pltpu.make_async_copy(some, some, sem).wait()

    def pair_begin(buf, sems):
        mine = buf.at[me]
        each_chip(lambda h: remote(mine, mine, sems.at[0], sems.at[2], 2 * h + core).start())
        remote(mine, mine, sems.at[0], sems.at[1], partner).start()

    def pair_relay(buf, sems):
        take(buf, chips - 1, sems.at[2])
        def go(h):
            other = buf.at[2 * h + core]
            remote(other, other, sems.at[0], sems.at[1], partner).start()
        each_chip(go)

    def pair_finish(buf, sems):
        take(buf, chips, sems.at[1])
        take(buf, n_sp - 1, sems.at[0])

    r64 = lax.broadcasted_iota(jnp.int32, (wide, chan), 0)
    ra = lax.broadcasted_iota(jnp.int32, (wide, wide), 0)
    rb = lax.broadcasted_iota(jnp.int32, (wide, wide), 1)
    mirror = jnp.where(ra + rb == side - 1, 1.0, 0.0).astype(BF16)

    def flip(v):
        return jnp.dot(mirror, v, preferred_element_type=F32)

    s8 = lax.broadcasted_iota(jnp.int32, (ROWS, 8, chan), 1)

    def column(block, at):
        return jnp.sum(jnp.where(s8 == at, block, 0.0), axis=1)

    tail = jnp.zeros((wide - side, chan), F32)

    def widen(v):
        return jnp.concatenate([v, tail], axis=0)

    loads[0].wait()
    lane = lax.broadcasted_iota(jnp.int32, (1, chan), 1)
    row = jnp.zeros((1, chan), jnp.int32)
    for k in range(8):
        for part in range(2):
            row = jnp.where(lane == 2 * k + part, adj[0, part, k], row)
    adj_row[me] = row
    loads[1].wait()
    for c in range(chunks):
        lo = c * ROWS
        col_a[lo:lo + ROWS, :] = silu(column(x_in[lo:lo + ROWS, 0:8, :].astype(F32), 0))
        col_b[lo:lo + ROWS, :] = silu(column(x_in[lo:lo + ROWS, side - 8:side, :].astype(F32), 7))
    for col in (col_a, col_b, col_c, col_d):
        col[side:wide, :] = tail
    loads[2].wait()
    for c in range(chunks):
        lo = c * ROWS
        col_c[lo:lo + ROWS, :] = column(g_in[lo:lo + ROWS, 0:8, :].astype(F32), 0)
    spare = wide - side

    def fill_up(v, at):
        return jnp.concatenate([v[0:side], col_c[at * spare:(at + 1) * spare, :]], axis=0).astype(BF16)

    ends[me, 0] = fill_up(silu(x_in[0].astype(F32)), 0)
    ends[me, 1] = fill_up(col_b[...], 1)
    ends[me, 2] = fill_up(flip(widen(silu(x_in[side - 1].astype(F32))).astype(BF16)), 2)
    ends[me, 3] = fill_up(flip(col_a[...].astype(BF16)), 3)
    pl.semaphore_wait(barrier, n_sp + n_dp - 2)
    def tell(k, c):
        mine = adj_row.at[me]
        remote(mine, mine, adj_sem.at[0], adj_sem.at[1], lax.rem(me + k, n_sp)).start()
        return c

    lax.fori_loop(1, n_sp, tell, 0)
    pair_begin(ends, edge_sem)
    three = 3 * chan
    pairs = side // 2
    zero_row = jnp.zeros((wide, three), BF16)
    for buf in (taps, gtaps):
        buf[0, :, three:] = zero_row
        buf[pairs + 1, :, 0:three] = zero_row

    def shifts(v):
        return jnp.concatenate(
            [pltpu.roll(v, 1, 0).astype(BF16), v.astype(BF16), pltpu.roll(v, wide - 1, 0).astype(BF16)], axis=1)

    def spread(c, carry):
        for part in range(2):
            rows = []
            for k in range(ROWS // 2):
                i = c * ROWS + 2 * k + part
                p = c * (ROWS // 2) + k + 1
                a = widen(silu(x_in[i].astype(F32)))
                rows.append(a.astype(BF16))
                taps[p, :, part * three + chan:part * three + 2 * chan] = rows[-1]
                gtaps[p, :, part * three:(part + 1) * three] = shifts(widen(g_in[i].astype(F32)))
            n = ROWS // 2 * wide
            flat[part * chan:(part + 1) * chan, pl.ds(pl.multiple_of(c * n, n), n)] = jnp.concatenate(rows, axis=0).T
        return carry

    lax.fori_loop(0, chunks, spread, 0)

    for c in range(chunks):
        lo = c * ROWS
        col_d[lo:lo + ROWS, :] = column(g_in[lo:lo + ROWS, side - 8:side, :].astype(F32), 7)
    packed[me, 0] = fill_up(flip(widen(g_in[0].astype(F32)).astype(BF16)), 4)
    packed[me, 1] = fill_up(flip(col_d[...].astype(BF16)), 5)
    packed[me, 2] = fill_up(g_in[side - 1].astype(F32), 6)
    pair_begin(packed, pack_sem)

    def grads(first, part):
        return gtaps[first:first + pairs, :, part * three:(part + 1) * three].reshape(pairs * wide, three)

    odd = jnp.dot(flat[...], grads(1, 1), preferred_element_type=F32)
    even = jnp.dot(flat[...], grads(1, 0), preferred_element_type=F32)
    below = jnp.dot(flat[0:chan], grads(0, 1), preferred_element_type=F32)
    above = jnp.dot(flat[chan:2 * chan], grads(2, 0), preferred_element_type=F32)
    for r, v in enumerate((odd[:chan] + above, odd[chan:] + even[:chan], even[chan:] + below)):
        for b in range(3):
            at = (3 * r + 2 - b) * chan
            wgf[at:at + chan, :] = v[:, b * chan:(b + 1) * chan]
    used = 9 * chan
    if wgf.shape[0] > used:
        wgf[used:, :] = jnp.zeros((wgf.shape[0] - used, chan), F32)

    size = full.shape[1]
    half = chips * size
    swap = remote(
        wgf.at[pl.ds(pl.multiple_of((1 - core) * half, 16), half)], half_in, swap_sem.at[0], swap_sem.at[1], partner)
    swap.start()
    take(adj_row, n_sp - 1, adj_sem.at[1])
    take(adj_row, n_sp - 1, adj_sem.at[0])
    spill = pltpu.make_async_copy(adj_row, adj_all, in_sem.at[5])
    spill.start()

    loads[3].wait()
    loads[4].wait()
    for r in range(3):
        for c in range(3):
            block = w_in[2 - r, (2 - c) * chan:(3 - c) * chan, :].astype(F32)
            wt[r, c * chan:(c + 1) * chan, :] = block.T.astype(BF16)
    for k in range(3):
        to = slice(k * chan, (k + 1) * chan)
        for e, (r, c) in enumerate(((2, 2 - k), (2 - k, 0), (0, k), (k, 2))):
            vt[e, to, :] = wt[r, c * chan:(c + 1) * chan, :]
    blank = jnp.zeros((three, chan), BF16)
    for buf, one in ((pair_w, w_in), (pair_t, wt)):
        for k in range(4):
            at = slice(k * three, (k + 1) * three)
            buf[at, 0:chan] = one[k] if k < 3 else blank
            buf[at, chan:] = one[k - 1] if k > 0 else blank
    swap.wait()

    def half_rows(h):
        at = pl.multiple_of(h * size, 16)
        return wgf[pl.ds(pl.multiple_of(core * half + h * size, 16), size), :] + half_in[pl.ds(at, size), :]

    def scatter(h):
        sent[h], sent_s[h] = encode(half_rows(h))
        to = 2 * h + core
        remote(sent.at[h], parts.at[chip], share_sem.at[0], share_sem.at[1], to).start()
        remote(sent_s.at[h], parts_s.at[chip], scale_sem.at[0], scale_sem.at[1], to).start()

    each_chip(scatter)

    pair_relay(ends, edge_sem)

    def two_rows(buf, first, w):
        rows = jnp.concatenate([
            buf[pl.ds(first, PAIRS), :, three:].reshape(PAIRS * wide, three),
            buf[pl.ds(first + 1, PAIRS)].reshape(PAIRS * wide, 2 * three),
            buf[pl.ds(first + 2, PAIRS), :, 0:three].reshape(PAIRS * wide, three)], axis=1)
        return jnp.dot(rows, w[...], preferred_element_type=F32).reshape(PAIRS, wide, 2 * chan)

    def grad_chunk(c, carry):
        pad_grad[pl.ds(c * PAIRS, PAIRS)] = two_rows(gtaps, c * PAIRS, pair_t)
        return carry

    early = pairs // PAIRS // 2
    lax.fori_loop(0, early, grad_chunk, 0)
    pair_relay(packed, pack_sem)
    pair_finish(ends, edge_sem)
    spill.wait()

    group = la.shape[1] // wide
    groups = chips // group
    corr[...] = jnp.zeros_like(corr)

    def turn_edges(n, carry):
        def fill(j, c2):
            t = 2 * (lax.rem(n, groups) * group + j) + n // groups
            at = pl.ds(pl.multiple_of(j * wide, 16), wide)
            for e in range(4):
                v = ends[adj_all[t, 0, 2 * e], adj_all[t, 0, 2 * e + 1]].astype(F32)
                k = ends[adj_all[t, 0, 8 + 2 * e], adj_all[t, 0, 9 + 2 * e]].astype(F32)[0:1]
                la[e, at, :] = jnp.where(r64 < side, v, jnp.where(r64 == side, k, 0.0)).astype(BF16)
            return c2

        lax.fori_loop(0, group, fill, 0)
        for e in range(4):
            lat[n, e] = la[e].T
        return carry

    lax.fori_loop(0, 2 * groups, turn_edges, 0)

    def rim_groups(parity):
        def rim_group(n, carry):
            def fill(j, c2):
                t = 2 * (n * group + j) + parity
                at = pl.ds(pl.multiple_of(j * wide, 16), wide)
                over = [ends[t, e].astype(F32)[side:wide] for e in range(4)]
                for e in range(4):
                    if e < 3:
                        g = packed[t, e].astype(F32)
                        over.append(g[side:wide])
                        g = jnp.where(r64 < side, g, 0.0)
                    else:
                        g = widen(jnp.concatenate(over, axis=0))
                    gends[t, e] = g.astype(BF16)
                    lg[e, at, :] = shifts(g)
                return c2

            lax.fori_loop(0, group, fill, 0)
            for e in range(4):
                res = jnp.dot(lat[parity * groups + n, e], lg[e], preferred_element_type=F32)
                for k in range(3):
                    r, c = ((0, k), (k, 2), (2, 2 - k), (2 - k, 0))[e]
                    at = (3 * r + c) * chan
                    corr[at:at + chan, :] += res[:, k * chan:(k + 1) * chan]
            return carry

        lax.fori_loop(0, groups, rim_group, 0)

    rim_groups(core)
    pair_finish(packed, pack_sem)
    rim_groups(1 - core)

    take(parts, chips - 1, share_sem.at[1])
    take(sent, chips - 1, share_sem.at[0])
    take(parts_s, chips - 1, scale_sem.at[1])
    take(sent_s, chips - 1, scale_sem.at[0])
    slot = core * chips + chip
    mine = half_rows(chip) + corr[pl.ds(pl.multiple_of(slot * size, 16), size), :]
    def add_part(k, t):
        h = lax.rem(chip + k, chips)
        return t + decode(parts[h], parts_s[h])

    mine = lax.fori_loop(1, chips, add_part, mine)
    dps[my_dp], dps_s[my_dp] = encode(mine)

    steps = 3 if size % 48 == 0 else 1
    step = size // steps
    scales = dps_s.at[my_dp]
    each_dp(lambda z: remote(scales, scales, scale_sem.at[2], scale_sem.at[3], me, z).start())
    for n in range(steps):
        one = dps.at[my_dp, pl.ds(n * step, step)]
        each_dp(lambda z, one=one, n=n: remote(one, one, sample_sem.at[0], sample_sem.at[1 + n], me, z).start())

    def near(buf, e):
        return buf[adj[0, 0, e], adj[0, 1, e]]

    corner = [ends[adj[0, 0, 4 + k], adj[0, 1, 4 + k]].astype(F32)[0:1] for k in range(4)]

    def rim_row(v, behind, ahead):
        return jnp.where(r64 < side, v, jnp.where(r64 == side, behind, jnp.where(r64 == wide - 1, ahead, 0.0)))

    taps[0, :, three:] = shifts(rim_row(flip(near(ends, 0)), corner[1], corner[0]))
    taps[pairs + 1, :, 0:three] = shifts(rim_row(near(ends, 2).astype(F32), corner[2], corner[3]))
    col_a[...] = near(ends, 3).astype(F32)
    col_b[...] = flip(near(ends, 1))

    def spread_act(c, carry):
        for part in range(2):
            at = part * three
            for k in range(ROWS // 2):
                p = c * (ROWS // 2) + k + 1
                i = pl.ds(c * ROWS + 2 * k + part, 1)
                v = taps[p, :, at + chan:at + 2 * chan].astype(F32)
                taps[p, :, at:at + chan] = jnp.where(r64 == 0, col_a[i, :], pltpu.roll(v, 1, 0)).astype(BF16)
                taps[p, :, at + 2 * chan:at + three] = jnp.where(
                    r64 == side - 1, col_b[i, :], pltpu.roll(v, wide - 1, 0)).astype(BF16)
        return carry

    lax.fori_loop(0, chunks, spread_act, 0)
    lax.fori_loop(early, pairs // PAIRS, grad_chunk, 0)

    def conv_chunk(c, carry):
        conv = two_rows(taps, c * PAIRS, pair_w)
        for k in range(2 * PAIRS):
            i = 2 * PAIRS * c + k
            at = k % 2 * chan
            out[i] = (x_in[i].astype(F32) + conv[k // 2, 0:side, at:at + chan] + bias[...]).astype(BF16)
        return carry

    lax.fori_loop(0, early, conv_chunk, 0)

    take(dps_s, n_dp - 1, scale_sem.at[3])
    for n in range(steps):
        take_rows(dps, n_dp - 1, n * step, step, sample_sem.at[1 + n])
        at = pl.ds(n * step, step)
        total = decode(dps[0, at], dps_s[0])
        for d in range(1, n_dp):
            total = total + decode(dps[d, at], dps_s[d])
        one = full.at[me, pl.ds(n * step, step)]
        one[...] = total.astype(BF16)

        each_chip(lambda h, one=one, n=n: remote(one, one, full_sem.at[0], near_sem.at[n], 2 * h + core).start())
        remote(one, one, full_sem.at[0], full_sem.at[1], partner).start()
    take(dps, n_dp - 1, sample_sem.at[0])
    take(dps_s, n_dp - 1, scale_sem.at[2])
    lax.fori_loop(early, pairs // PAIRS, conv_chunk, 0)

    def rim_grad(e):
        at = adj[0, 1, e]
        v = jnp.dot(shifts(gends[adj[0, 0, e], at].astype(F32)), vt[at], preferred_element_type=F32)
        return jnp.where(r64 < side, v, 0.0).astype(BF16)

    def rim_corner(k):
        at = adj[0, 1, 4 + k]
        v = jnp.dot(gends[adj[0, 0, 4 + k], at], vt[at, 0:chan, :], preferred_element_type=F32)
        return v[side - 1:side].astype(BF16).astype(F32)

    add = [rim_corner(k) for k in range(4)]
    pad_grad[0, :, 0:chan] += rim_grad(0).astype(F32)
    pad_grad[pairs - 1, :, chan:] += flip(rim_grad(2))
    col_a[...] = flip(rim_grad(3)) + jnp.where(r64 == 0, add[0], jnp.where(r64 == side - 1, add[3], 0.0))
    col_b[...] = rim_grad(1).astype(F32) + jnp.where(r64 == 0, add[1], jnp.where(r64 == side - 1, add[2], 0.0))

    r56 = lax.broadcasted_iota(jnp.int32, (side, chan), 0)

    def finish_rows(c, carry):
        for k in range(ROWS):
            i = c * ROWS + k
            p = pad_grad[c * (ROWS // 2) + k // 2, 0:side, k % 2 * chan:(k % 2 + 1) * chan]
            p = p + jnp.where(r56 == 0, col_a[pl.ds(i, 1), :], jnp.where(r56 == side - 1, col_b[pl.ds(i, 1), :], 0.0))
            v = x_in[i].astype(F32)
            s = 0.5 + 0.5 * jnp.tanh(0.5 * v)
            gin_out[i] = (g_in[i].astype(F32) + p * s * (1.0 + v * (1.0 - s))).astype(BF16)
        return carry

    lax.fori_loop(0, chunks, finish_rows, 0)

    for n in range(steps):
        take_rows(full, chips - 1, n * step, step, near_sem.at[n])

        def share_relay(h, n=n):
            one = full.at[2 * h + core, pl.ds(n * step, step)]
            remote(one, one, full_sem.at[0], full_sem.at[1], partner).start()

        each_chip(share_relay)
    pair_finish(full, full_sem)

    def open_rows(t, carry):
        at = (lax.rem(t, 2) * chips + t // 2) * size
        wg_out[pl.ds(pl.multiple_of(at, 16), size), :] = full[t].astype(F32)
        return carry

    lax.fori_loop(0, n_sp, open_rows, 0)


def hand_on(a, wg, c, a_out, wg_out, c_out, sems):
    used = wg_out.shape[0]
    copies = [
        pltpu.make_async_copy(a, a_out, sems.at[0]),
        pltpu.make_async_copy(c, c_out, sems.at[1]),
        pltpu.make_async_copy(wg.at[pl.ds(0, used)], wg_out, sems.at[2]),
    ]
    for one in copies:
        one.start()
    for one in copies:
        one.wait()


def per_device(n_sp, n_dp, block_in, weights, out_bias, adjacency, cotangent):
    side, chan = block_in.shape[2], block_in.shape[4]
    wide = wide_of(side)
    chips = n_sp // 2
    size = -(-9 * chan // (16 * n_sp)) * 16
    group = min(chips, 4)
    vmem = pl.BlockSpec(memory_space=pltpu.VMEM)
    hbm = pl.BlockSpec(memory_space=pltpu.HBM)
    sem = pltpu.SemaphoreType.DMA
    tile = (side, side, chan)
    held = pl.pallas_call(
        functools.partial(block_kernel, n_sp, n_dp, side),
        out_shape=(pltpu.VMEM(tile, BF16), pltpu.VMEM((n_sp * size, chan), F32), pltpu.VMEM(tile, BF16)),
        in_specs=[hbm] * 5,
        out_specs=(vmem, vmem, vmem),
        scratch_shapes=[
            pltpu.VMEM(tile, BF16),
            pltpu.VMEM(tile, BF16),
            pltpu.VMEM((3, 3 * chan, chan), BF16),
            pltpu.VMEM((1, chan), F32),
            pltpu.SMEM((1, 2, 8), jnp.int32),
            pltpu.SMEM((n_sp, 1, chan), jnp.int32),
            pltpu.VMEM((n_sp, 1, chan), jnp.int32),
            pltpu.VMEM((side // 2 + 2, wide, 6 * chan), BF16),
            pltpu.VMEM((side // 2 + 2, wide, 6 * chan), BF16),
            pltpu.VMEM((2 * chan, side // 2 * wide), BF16),
            pltpu.VMEM((side // 2, wide, 2 * chan), F32),
            pltpu.VMEM((3, 3 * chan, chan), BF16),
            pltpu.VMEM((4, 3 * chan, chan), BF16),
            pltpu.VMEM((12 * chan, 2 * chan), BF16),
            pltpu.VMEM((12 * chan, 2 * chan), BF16),
            pltpu.VMEM((n_sp * size, chan), F32),
            pltpu.VMEM((n_sp * size, chan), F32),
            pltpu.VMEM((chips * size, chan), F32),
            pltpu.VMEM((wide, chan), F32),
            pltpu.VMEM((wide, chan), F32),
            pltpu.VMEM((wide, chan), F32),
            pltpu.VMEM((wide, chan), F32),
            pltpu.VMEM((n_sp, 4, wide, chan), BF16),
            pltpu.VMEM((n_sp, 3, wide, chan), BF16),
            pltpu.VMEM((n_sp, 4, wide, chan), BF16),
            pltpu.VMEM((4, group * wide, chan), BF16),
            pltpu.VMEM((n_sp // group, 4, chan, group * wide), BF16),
            pltpu.VMEM((4, group * wide, 3 * chan), BF16),
            pltpu.VMEM((chips, size, chan), CODE),
            pltpu.VMEM((chips, 1, chan), F32),
            pltpu.VMEM((chips, size, chan), CODE),
            pltpu.VMEM((chips, 1, chan), F32),
            pltpu.VMEM((n_dp, size, chan), CODE),
            pltpu.VMEM((n_dp, 1, chan), F32),
            pltpu.VMEM((n_sp, size, chan), BF16),
            sem((6,)), sem((3,)), sem((3,)), sem((2,)), sem((2,)), sem((2,)), sem((4,)), sem((4,)), sem((2,)), sem((3,)),
        ],
        compiler_params=pltpu.CompilerParams(
            collective_id=0, has_side_effects=True, vmem_limit_bytes=58 * 2**20),
    )(
        adjacency.transpose(0, 2, 1), block_in[0, 0], weights.reshape(3, 3 * chan, chan), out_bias.reshape(1, chan),
        cotangent[0, 0],
    )
    result, wgrad, grad_in = pl.pallas_call(
        hand_on,
        out_shape=(
            jax.ShapeDtypeStruct(tile, BF16), jax.ShapeDtypeStruct((9 * chan, chan), F32), jax.ShapeDtypeStruct(tile, BF16)),
        in_specs=[vmem, vmem, vmem],
        out_specs=(hbm, hbm, hbm),
        scratch_shapes=[sem((3,))],
        compiler_params=pltpu.CompilerParams(vmem_limit_bytes=4 * 2**20),
    )(*held)
    return (result[None, None], wgrad.reshape(weights.shape), grad_in[None, None])


def solution(mesh):
    placed = (
        P("dp", "space", None, None, None),
        P(),
        P(),
        P("space", None, None),
        P("dp", "space", None, None, None),
    )
    return jax.shard_map(
        functools.partial(per_device, mesh.shape["space"], mesh.shape["dp"]),
        mesh=mesh,
        in_specs=placed,
        out_specs=(P("dp", "space", None, None, None), P(), P("dp", "space", None, None, None)),
        check_vma=False,
    )
```

```python
import functools

import jax
import jax.numpy as jnp
from jax import lax
from jax.experimental import pallas as pl
from jax.experimental.pallas import tpu as pltpu
from jax.sharding import PartitionSpec as P

MESH = pl.DeviceIdType.MESH
ROWS = 8
PAIRS = 7
CORNERS = ((0, 0), (0, 2), (2, 2), (2, 0))
SIDES = ((0, 1), (1, 2), (2, 1), (1, 0))
F32 = jnp.float32
BF16 = jnp.bfloat16
CODE = jnp.int16


def silu(v):
    h = 0.5 * v
    return h + h * jnp.tanh(h)


def encode(v):
    top = jnp.maximum(jnp.max(jnp.abs(v), axis=0, keepdims=True), 1e-30)
    power = jnp.ceil(jnp.log2(top))
    code = jnp.clip(jnp.round(v * jnp.exp2(15.0 - power)), -32767.0, 32767.0)
    return code.astype(jnp.int32).astype(CODE), jnp.exp2(power - 15.0)


def decode(rows, scale):
    return rows.astype(jnp.int32).astype(F32) * scale


def wide_of(side):
    return -(-(side + 4) // 16) * 16


def block_kernel(
    n_sp, n_dp, side,
    adj_hbm, x_hbm, w_hbm, bias_hbm, g_hbm,
    out, wg_out, gin_out,
    x_in, g_in, w_in, bias, adj, adj_all, adj_row,
    taps, gtaps, flat, pad_grad, wt, vt, pair_w, pair_t, wgf, corr, half_in, col_a, col_b, col_c, col_d,
    ends, turned, gends, la, lat, lg, sent, sent_s, parts, parts_s, dps, dps_s, full,
    in_sem, edge_sem, near_g_sem, far_g_sem, adj_sem, swap_sem, share_sem, sample_sem, scale_sem, full_sem, near_sem,
):
    wide = wide_of(side)
    chan = 128
    chunks = side // ROWS
    me = lax.axis_index("space")
    my_dp = lax.axis_index("dp")
    core = lax.rem(me, 2)
    chip = me // 2
    chips = n_sp // 2
    partner = me + 1 - 2 * core
    size = full.shape[1]
    corners = chips == 4 and size == chan + 16
    near_count = 2 if corners else 4
    turn = chip if corners else 0

    barrier = pltpu.get_barrier_semaphore()

    def greet_sp(k, c):
        pl.semaphore_signal(barrier, inc=1, device_id=(lax.rem(me + k, n_sp), my_dp), device_id_type=MESH)
        return c

    def greet_dp(k, c):
        pl.semaphore_signal(barrier, inc=1, device_id=(me, lax.rem(my_dp + k, n_dp)), device_id_type=MESH)
        return c

    def load(src, dst, sem, parts=1):
        n = dst.shape[0] // parts
        for k in range(parts):
            rows = pl.ds(k * n, n)
            pltpu.make_async_copy(src.at[rows], dst.at[rows], sem).start()
        return pltpu.make_async_copy(src, dst, sem)

    loads = [
        load(adj_hbm, adj, in_sem.at[2]),
        load(x_hbm, x_in, in_sem.at[0], 4),
        load(g_hbm, g_in, in_sem.at[1], 4),
        load(w_hbm, w_in, in_sem.at[3]),
        load(bias_hbm, bias, in_sem.at[4]),
    ]
    lax.fori_loop(1, n_sp, greet_sp, 0)
    lax.fori_loop(1, n_dp, greet_dp, 0)

    def each_chip(do):
        if chips == 4:
            for other in (3 - chip, lax.rem(chip + 2, 4), chip + 1 - 2 * lax.rem(chip, 2)):
                do(other)
        else:
            def go(k, c):
                do(lax.rem(chip + k, chips))
                return c
            lax.fori_loop(1, chips, go, 0)

    low = 1 - (2 * my_dp) // n_dp
    first_dp = low * (n_dp - 1 - my_dp) + (1 - low) * my_dp

    def each_dp(do):
        for j in range(n_dp - 1):
            at = j + (j - first_dp + n_dp) // n_dp
            do(low * (n_dp - 1 - at) + (1 - low) * at)

    def remote(src, dst, send, recv, peer, dp=None):
        return pltpu.make_async_remote_copy(
            src_ref=src, dst_ref=dst, send_sem=send, recv_sem=recv,
            device_id=(peer, my_dp if dp is None else dp), device_id_type=MESH)

    def take(buf, count, sem):
        some = buf.at[pl.ds(0, count)]
        pltpu.make_async_copy(some, some, sem).wait()

    def take_rows(buf, count, first, rows, sem):
        some = buf.at[pl.ds(0, count), pl.ds(first, rows)]
        pltpu.make_async_copy(some, some, sem).wait()

    def pair_begin(buf, sems):
        mine = buf.at[me]
        each_chip(lambda h: remote(mine, mine, sems.at[0], sems.at[2], 2 * h + core).start())
        remote(mine, mine, sems.at[0], sems.at[1], partner).start()

    def pair_relay(buf, sems):
        take(buf, chips - 1, sems.at[2])
        def go(h):
            other = buf.at[2 * h + core]
            remote(other, other, sems.at[0], sems.at[1], partner).start()
        each_chip(go)

    def pair_finish(buf, sems):
        take(buf, chips, sems.at[1])
        take(buf, n_sp - 1, sems.at[0])

    def stretch_begin(src, buf, first, count, sems):
        to = buf.at[me, pl.ds(first, count)]

        def one(h, peer, sem):
            at = pl.ds((h if corners else 0) + first, count)
            remote(src.at[at], to, sems.at[0], sem, peer).start()

        each_chip(lambda h: one(h, 2 * h + core, sems.at[2]))
        one(chip, partner, sems.at[1])

    def stretch_relay(buf, first, count, sems):
        take_rows(buf, chips - 1, first, count, sems.at[2])

        def go(h):
            other = buf.at[2 * h + core, pl.ds(first, count)]
            remote(other, other, sems.at[0], sems.at[1], partner).start()

        each_chip(go)

    def stretch_finish(buf, first, count, sems):
        take_rows(buf, chips, first, count, sems.at[1])
        take_rows(buf, n_sp - 1, first, count, sems.at[0])

    r64 = lax.broadcasted_iota(jnp.int32, (wide, chan), 0)
    ra = lax.broadcasted_iota(jnp.int32, (wide, wide), 0)
    rb = lax.broadcasted_iota(jnp.int32, (wide, wide), 1)
    mirror = jnp.where(ra + rb == side - 1, 1.0, 0.0).astype(BF16)

    def flip(v):
        return jnp.dot(mirror, v, preferred_element_type=F32)

    s8 = lax.broadcasted_iota(jnp.int32, (8, chan), 0)

    def column(block, at):
        rows = block[0] if at == 0 else pltpu.roll(block[0], 8 - at, 0)
        for k in range(1, ROWS):
            one = block[k] if k == at else pltpu.roll(block[k], (k - at) % 8, 0)
            rows = jnp.where(s8 == k, one, rows)
        return rows

    tail = jnp.zeros((wide - side, chan), F32)

    def widen(v):
        return jnp.concatenate([v, tail], axis=0)

    loads[0].wait()
    lane = lax.broadcasted_iota(jnp.int32, (1, chan), 1)
    row = jnp.zeros((1, chan), jnp.int32)
    for k in range(8):
        for part in range(2):
            row = jnp.where(lane == 2 * k + part, adj[0, part, k], row)
    adj_row[me] = row
    loads[1].wait()
    for c in range(chunks):
        lo = c * ROWS
        col_a[lo:lo + ROWS, :] = silu(column(x_in[lo:lo + ROWS, 0:8, :].astype(F32), 0))
        col_b[lo:lo + ROWS, :] = silu(column(x_in[lo:lo + ROWS, side - 8:side, :].astype(F32), 7))
    for col in (col_a, col_b, col_c, col_d):
        col[side:wide, :] = tail
    ends[me, 0] = widen(silu(x_in[0].astype(F32))).astype(BF16)
    ends[me, 1] = col_b[...].astype(BF16)
    ends[me, 2] = flip(widen(silu(x_in[side - 1].astype(F32))).astype(BF16)).astype(BF16)
    ends[me, 3] = flip(col_a[...].astype(BF16)).astype(BF16)

    three = 3 * chan
    pairs = side // 2
    zero_row = jnp.zeros((wide, three), BF16)
    for buf in (taps, gtaps):
        buf[0, :, three:] = zero_row
        buf[pairs + 1, :, 0:three] = zero_row

    def shifts(v):
        return jnp.concatenate(
            [pltpu.roll(v, 1, 0).astype(BF16), v.astype(BF16), pltpu.roll(v, wide - 1, 0).astype(BF16)], axis=1)

    def spread(c, carry):
        for part in range(2):
            rows = []
            for k in range(ROWS // 2):
                i = c * ROWS + 2 * k + part
                p = c * (ROWS // 2) + k + 1
                a = widen(silu(x_in[i].astype(F32)))
                rows.append(a.astype(BF16))
                taps[p, :, part * three + chan:part * three + 2 * chan] = rows[-1]
                gtaps[p, :, part * three:(part + 1) * three] = shifts(widen(g_in[i].astype(F32)))
            n = ROWS // 2 * wide
            flat[part * chan:(part + 1) * chan, pl.ds(pl.multiple_of(c * n, n), n)] = jnp.concatenate(rows, axis=0).T
        return carry

    ahead = chunks * (1 - (2 * my_dp) // n_dp)
    loads[2].wait()
    lax.fori_loop(0, ahead, spread, 0)

    pl.semaphore_wait(barrier, n_sp + n_dp - 2)
    def tell(k, c):
        mine = adj_row.at[me]
        remote(mine, mine, adj_sem.at[0], adj_sem.at[1], lax.rem(me + k, n_sp)).start()
        return c

    lax.fori_loop(1, n_sp, tell, 0)
    pair_begin(ends, edge_sem)
    for c in range(chunks):
        lo = c * ROWS
        col_c[lo:lo + ROWS, :] = column(g_in[lo:lo + ROWS, 0:8, :].astype(F32), 0)
        col_d[lo:lo + ROWS, :] = column(g_in[lo:lo + ROWS, side - 8:side, :].astype(F32), 7)
    around = (
        flip(widen(g_in[0].astype(F32)).astype(BF16)).astype(BF16), flip(col_d[...].astype(BF16)).astype(BF16),
        widen(g_in[side - 1].astype(F32)).astype(BF16), col_c[...].astype(BF16))
    for k in range(7):
        turned[k] = around[(k + 3) % 4]
    for k in range(4):
        gends[me, k] = turned[turn + k]
    stretch_begin(turned, gends, 0, near_count, near_g_sem)

    lax.fori_loop(ahead, chunks, spread, 0)

    def grads(first, part):
        return gtaps[first:first + pairs, :, part * three:(part + 1) * three].reshape(pairs * wide, three)

    odd = jnp.dot(flat[...], grads(1, 1), preferred_element_type=F32)
    even = jnp.dot(flat[...], grads(1, 0), preferred_element_type=F32)
    below = jnp.dot(flat[0:chan], grads(0, 1), preferred_element_type=F32)
    above = jnp.dot(flat[chan:2 * chan], grads(2, 0), preferred_element_type=F32)
    for r, v in enumerate((odd[:chan] + above, odd[chan:] + even[:chan], even[chan:] + below)):
        for b in range(3):
            block = v[:, b * chan:(b + 1) * chan]
            if not corners:
                wgf[(3 * r + 2 - b) * chan:(3 * r + 3 - b) * chan, :] = block
            elif (r, b) == (1, 1):
                for k in range(n_sp):
                    wgf[k * size + chan:(k + 1) * size, :] = block[16 * k:16 * k + 16]
            else:
                kind = SIDES if (r + b) % 2 else CORNERS
                at = (kind.index((r, 2 - b)) + chips * ((r + b) % 2)) * size
                wgf[at:at + chan, :] = block
    used = 9 * chan
    if wgf.shape[0] > used:
        wgf[used:, :] = jnp.zeros((wgf.shape[0] - used, chan), F32)

    half = chips * size
    swap = remote(
        wgf.at[pl.ds(pl.multiple_of((1 - core) * half, 16), half)], half_in, swap_sem.at[0], swap_sem.at[1], partner)
    swap.start()
    take(adj_row, n_sp - 1, adj_sem.at[1])
    take(adj_row, n_sp - 1, adj_sem.at[0])
    spill = pltpu.make_async_copy(adj_row, adj_all, in_sem.at[5])
    spill.start()

    loads[3].wait()
    loads[4].wait()
    for r in range(3):
        for c in range(3):
            block = w_in[2 - r, (2 - c) * chan:(3 - c) * chan, :].astype(F32)
            wt[r, c * chan:(c + 1) * chan, :] = block.T.astype(BF16)
    for k in range(3):
        to = slice(k * chan, (k + 1) * chan)
        for e, (r, c) in enumerate(((2, 2 - k), (2 - k, 0), (0, k), (k, 2))):
            vt[e, to, :] = wt[r, c * chan:(c + 1) * chan, :]
    blank = jnp.zeros((three, chan), BF16)
    for buf, one in ((pair_w, w_in), (pair_t, wt)):
        for k in range(4):
            at = slice(k * three, (k + 1) * three)
            buf[at, 0:chan] = one[k] if k < 3 else blank
            buf[at, chan:] = one[k - 1] if k > 0 else blank
    def two_rows(buf, first, w):
        rows = jnp.concatenate([
            buf[pl.ds(first, PAIRS), :, three:].reshape(PAIRS * wide, three),
            buf[pl.ds(first + 1, PAIRS)].reshape(PAIRS * wide, 2 * three),
            buf[pl.ds(first + 2, PAIRS), :, 0:three].reshape(PAIRS * wide, three)], axis=1)
        return jnp.dot(rows, w[...], preferred_element_type=F32).reshape(PAIRS, wide, 2 * chan)

    def grad_chunk(c, carry):
        pad_grad[pl.ds(c * PAIRS, PAIRS)] = two_rows(gtaps, c * PAIRS, pair_t)
        return carry

    early = pairs // PAIRS // 2
    none = my_dp // n_dp
    lax.fori_loop(none, none + early // 2, grad_chunk, 0)
    swap.wait()

    def half_rows(h):
        at = pl.multiple_of(h * size, 16)
        return wgf[pl.ds(pl.multiple_of(core * half + h * size, 16), size), :] + half_in[pl.ds(at, size), :]

    def scatter(h):
        sent[h], sent_s[h] = encode(half_rows(h))
        remote(sent_s.at[h], parts_s.at[chip], scale_sem.at[0], scale_sem.at[1], 2 * h + core).start()

    each_chip(scatter)
    steps = 3 if size % 48 == 0 else 1
    step = size // steps
    for n in range(steps):
        rows = pl.ds(n * step, step)
        each_chip(lambda h, n=n, rows=rows: remote(
            sent.at[h, rows], parts.at[chip, rows], share_sem.at[0], share_sem.at[1 + n], 2 * h + core).start())

    pair_relay(ends, edge_sem)

    lax.fori_loop(none + early // 2, none + early, grad_chunk, 0)
    stretch_relay(gends, 0, near_count, near_g_sem)
    pair_finish(ends, edge_sem)
    spill.wait()

    def rim_cells(t, e):
        v = ends[adj_all[t, 0, 2 * e], adj_all[t, 0, 2 * e + 1]].astype(F32)
        k = ends[adj_all[t, 0, 8 + 2 * e], adj_all[t, 0, 9 + 2 * e]].astype(F32)[0:1]
        return jnp.where(r64 < side, v, jnp.where(r64 == side, k, 0.0)).astype(BF16)

    slot = core * chips + chip
    if corners:
        def tile_rows(t):
            return pl.ds(pl.multiple_of(t * wide, 16), wide)

        def turn_edges(t, carry):
            la[0, tile_rows(t), :] = rim_cells(t, chip)
            la[1, tile_rows(t), :] = rim_cells(t, lax.rem(chip + 3, 4))
            return carry

        def shift_edges(parity):
            def go(k, carry):
                t = 2 * k + parity
                g = gends[t, 1].astype(F32)
                lg[0, tile_rows(t), 0:chan] = pltpu.roll(g, 1, 0).astype(BF16)
                lg[0, tile_rows(t), chan:2 * chan] = gends[t, 1]
                lg[1, tile_rows(t), 0:chan] = pltpu.roll(gends[t, 0].astype(F32), wide - 1, 0).astype(BF16)
                return carry
            lax.fori_loop(0, chips, go, 0)

        lax.fori_loop(0, n_sp, turn_edges, 0)
        for k in range(2):
            lat[k] = la[k].T
        shift_edges(core)
        stretch_finish(gends, 0, near_count, near_g_sem)
        shift_edges(1 - core)
        here = jnp.dot(lat[0], lg[0, :, 0:2 * chan], preferred_element_type=F32)
        before = jnp.dot(lat[1], lg[1, :, 0:chan], preferred_element_type=F32)
        mine = half_rows(chip)
        rim = jnp.where(core == 0, here[:, 0:chan] + before, here[:, chan:])
        mine = jnp.concatenate([mine[0:chan] + rim, mine[chan:]], axis=0)
    else:
        stretch_finish(gends, 0, near_count, near_g_sem)
        group = la.shape[1] // wide
        corr[...] = jnp.zeros_like(corr)

        def rim_group(n, carry):
            def fill(j, c2):
                t = n * group + j
                at = pl.ds(pl.multiple_of(j * wide, 16), wide)
                for e in range(4):
                    la[e, at, :] = rim_cells(t, e)
                    lg[e, at, :] = shifts(gends[t, (e + 1) % 4].astype(F32))
                return c2

            lax.fori_loop(0, group, fill, 0)
            for e in range(4):
                res = jnp.dot(la[e].T, lg[e], preferred_element_type=F32)
                for k in range(3):
                    r, c = ((0, k), (k, 2), (2, 2 - k), (2 - k, 0))[e]
                    at = (3 * r + c) * chan
                    corr[at:at + chan, :] += res[:, k * chan:(k + 1) * chan]
            return carry

        lax.fori_loop(0, n_sp // group, rim_group, 0)
        mine = half_rows(chip) + corr[pl.ds(pl.multiple_of(slot * size, 16), size), :]

    take(parts_s, chips - 1, scale_sem.at[1])
    for n in range(steps):
        rows = pl.ds(n * step, step)
        take_rows(parts, chips - 1, n * step, step, share_sem.at[1 + n])

        def add_part(k, t, rows=rows):
            h = lax.rem(chip + k, chips)
            return t + decode(parts[h, rows], parts_s[h])

        some = lax.fori_loop(1, chips, add_part, mine[n * step:(n + 1) * step])
        dps[my_dp, rows], dps_s[my_dp, n] = encode(some)
        one, scale = dps.at[my_dp, rows], dps_s.at[my_dp, n]
        each_dp(lambda z, scale=scale, n=n: remote(scale, scale, scale_sem.at[2], scale_sem.at[3 + n], me, z).start())
        each_dp(lambda z, one=one, n=n: remote(one, one, sample_sem.at[0], sample_sem.at[1 + n], me, z).start())
    take(sent, chips - 1, share_sem.at[0])
    take(sent_s, chips - 1, scale_sem.at[0])
    if corners:
        stretch_begin(turned, gends, 2, 2, far_g_sem)

    def near(buf, e):
        return buf[adj[0, 0, e], adj[0, 1, e]]

    corner = [ends[adj[0, 0, 4 + k], adj[0, 1, 4 + k]].astype(F32)[0:1] for k in range(4)]

    def rim_row(v, behind, ahead):
        return jnp.where(r64 < side, v, jnp.where(r64 == side, behind, jnp.where(r64 == wide - 1, ahead, 0.0)))

    taps[0, :, three:] = shifts(rim_row(flip(near(ends, 0)), corner[1], corner[0]))
    taps[pairs + 1, :, 0:three] = shifts(rim_row(near(ends, 2).astype(F32), corner[2], corner[3]))
    col_a[...] = near(ends, 3).astype(F32)
    col_b[...] = flip(near(ends, 1))

    def spread_act(c, carry):
        for part in range(2):
            at = part * three
            for k in range(ROWS // 2):
                p = c * (ROWS // 2) + k + 1
                i = pl.ds(c * ROWS + 2 * k + part, 1)
                v = taps[p, :, at + chan:at + 2 * chan].astype(F32)
                taps[p, :, at:at + chan] = jnp.where(r64 == 0, col_a[i, :], pltpu.roll(v, 1, 0)).astype(BF16)
                taps[p, :, at + 2 * chan:at + three] = jnp.where(
                    r64 == side - 1, col_b[i, :], pltpu.roll(v, wide - 1, 0)).astype(BF16)
        return carry

    lax.fori_loop(0, chunks, spread_act, 0)
    lax.fori_loop(early, pairs // PAIRS, grad_chunk, 0)

    def conv_chunk(c, carry):
        conv = two_rows(taps, c * PAIRS, pair_w)
        for k in range(2 * PAIRS):
            i = 2 * PAIRS * c + k
            at = k % 2 * chan
            out[i] = (x_in[i].astype(F32) + conv[k // 2, 0:side, at:at + chan] + bias[...]).astype(BF16)
        return carry

    most = pairs // PAIRS - 1
    lax.fori_loop(0, most, conv_chunk, 0)

    for n in range(steps):
        take_rows(dps_s, n_dp - 1, n, 1, scale_sem.at[3 + n])
        take_rows(dps, n_dp - 1, n * step, step, sample_sem.at[1 + n])
        at = pl.ds(n * step, step)
        total = decode(dps[0, at], dps_s[0, n])
        for d in range(1, n_dp):
            total = total + decode(dps[d, at], dps_s[d, n])
        one = full.at[me, pl.ds(n * step, step)]
        one[...] = total.astype(BF16)

        last = n == steps - 1

        def share(h, one=one, n=n, last=last):
            remote(one, one, full_sem.at[0], near_sem.at[n], 2 * h + core).start()
            if last:
                remote(one, one, full_sem.at[0], near_sem.at[n], 2 * h + 1 - core).start()

        each_chip(share)
        remote(one, one, full_sem.at[0], near_sem.at[n] if last else full_sem.at[1], partner).start()
    take(dps, n_dp - 1, sample_sem.at[0])
    take_rows(dps_s, n_dp - 1, 0, steps, scale_sem.at[2])
    if corners:
        stretch_relay(gends, 2, 2, far_g_sem)
    lax.fori_loop(most, pairs // PAIRS, conv_chunk, 0)

    if corners:
        stretch_finish(gends, 2, 2, far_g_sem)

    def rim_grad(e):
        at = adj[0, 1, e]
        g = gends[adj[0, 0, e], lax.rem(at + 5 - turn, 4)]
        v = jnp.dot(shifts(g.astype(F32)), vt[at], preferred_element_type=F32)
        return jnp.where(r64 < side, v, 0.0).astype(BF16)

    def rim_corner(k):
        at = adj[0, 1, 4 + k]
        v = jnp.dot(gends[adj[0, 0, 4 + k], lax.rem(at + 5 - turn, 4)], vt[at, 0:chan, :], preferred_element_type=F32)
        return v[side - 1:side].astype(BF16).astype(F32)

    add = [rim_corner(k) for k in range(4)]
    pad_grad[0, :, 0:chan] += rim_grad(0).astype(F32)
    pad_grad[pairs - 1, :, chan:] += flip(rim_grad(2))
    col_a[...] = flip(rim_grad(3)) + jnp.where(r64 == 0, add[0], jnp.where(r64 == side - 1, add[3], 0.0))
    col_b[...] = rim_grad(1).astype(F32) + jnp.where(r64 == 0, add[1], jnp.where(r64 == side - 1, add[2], 0.0))

    r56 = lax.broadcasted_iota(jnp.int32, (side, chan), 0)

    def finish_rows(c, carry):
        for k in range(ROWS):
            i = c * ROWS + k
            p = pad_grad[c * (ROWS // 2) + k // 2, 0:side, k % 2 * chan:(k % 2 + 1) * chan]
            p = p + jnp.where(r56 == 0, col_a[pl.ds(i, 1), :], jnp.where(r56 == side - 1, col_b[pl.ds(i, 1), :], 0.0))
            v = x_in[i].astype(F32)
            s = 0.5 + 0.5 * jnp.tanh(0.5 * v)
            gin_out[i] = (g_in[i].astype(F32) + p * s * (1.0 + v * (1.0 - s))).astype(BF16)
        return carry

    lax.fori_loop(0, chunks, finish_rows, 0)

    for n in range(steps - 1):
        take_rows(full, chips - 1, n * step, step, near_sem.at[n])

        def share_relay(h, n=n):
            one = full.at[2 * h + core, pl.ds(n * step, step)]
            remote(one, one, full_sem.at[0], full_sem.at[1], partner).start()

        each_chip(share_relay)
    take_rows(full, n_sp - 1, (steps - 1) * step, step, near_sem.at[steps - 1])
    if steps > 1:
        take_rows(full, chips, 0, (steps - 1) * step, full_sem.at[1])
    take(full, n_sp - 1, full_sem.at[0])

    if corners:
        for t in range(n_sp):
            v = full[t].astype(F32)
            r, c = (SIDES if t % 2 else CORNERS)[t // 2]
            wg_out[(3 * r + c) * chan:(3 * r + c + 1) * chan, :] = v[0:chan]
            at = 4 * chan + 16 * (t % 2 * chips + t // 2)
            wg_out[at:at + 16, :] = v[chan:]
    else:
        def open_rows(t, carry):
            at = (lax.rem(t, 2) * chips + t // 2) * size
            wg_out[pl.ds(pl.multiple_of(at, 16), size), :] = full[t].astype(F32)
            return carry

        lax.fori_loop(0, n_sp, open_rows, 0)


def hand_on(a, wg, c, a_out, wg_out, c_out, sems):
    def begin(src, dst, sem, parts=4):
        n = dst.shape[0] // parts
        for k in range(parts):
            rows = pl.ds(k * n, n)
            pltpu.make_async_copy(src.at[rows], dst.at[rows], sem).start()
        return pltpu.make_async_copy(dst, dst, sem)

    for one in [begin(a, a_out, sems.at[0]), begin(c, c_out, sems.at[1]), begin(wg, wg_out, sems.at[2])]:
        one.wait()


def per_device(n_sp, n_dp, block_in, weights, out_bias, adjacency, cotangent):
    side, chan = block_in.shape[2], block_in.shape[4]
    wide = wide_of(side)
    chips = n_sp // 2
    size = -(-9 * chan // (16 * n_sp)) * 16
    corners = chips == 4 and size == chan + 16
    group = n_sp if corners else 4
    edges = 2 if corners else 4
    vmem = pl.BlockSpec(memory_space=pltpu.VMEM)
    hbm = pl.BlockSpec(memory_space=pltpu.HBM)
    sem = pltpu.SemaphoreType.DMA
    tile = (side, side, chan)
    held = pl.pallas_call(
        functools.partial(block_kernel, n_sp, n_dp, side),
        out_shape=(pltpu.VMEM(tile, BF16), pltpu.VMEM((n_sp * size, chan), F32), pltpu.VMEM(tile, BF16)),
        in_specs=[hbm] * 5,
        out_specs=(vmem, vmem, vmem),
        scratch_shapes=[
            pltpu.VMEM(tile, BF16),
            pltpu.VMEM(tile, BF16),
            pltpu.VMEM((3, 3 * chan, chan), BF16),
            pltpu.VMEM((1, chan), F32),
            pltpu.SMEM((1, 2, 8), jnp.int32),
            pltpu.SMEM((n_sp, 1, chan), jnp.int32),
            pltpu.VMEM((n_sp, 1, chan), jnp.int32),
            pltpu.VMEM((side // 2 + 2, wide, 6 * chan), BF16),
            pltpu.VMEM((side // 2 + 2, wide, 6 * chan), BF16),
            pltpu.VMEM((2 * chan, side // 2 * wide), BF16),
            pltpu.VMEM((side // 2, wide, 2 * chan), F32),
            pltpu.VMEM((3, 3 * chan, chan), BF16),
            pltpu.VMEM((4, 3 * chan, chan), BF16),
            pltpu.VMEM((12 * chan, 2 * chan), BF16),
            pltpu.VMEM((12 * chan, 2 * chan), BF16),
            pltpu.VMEM((n_sp * size, chan), F32),
            pltpu.VMEM((n_sp * size, chan), F32),
            pltpu.VMEM((chips * size, chan), F32),
            pltpu.VMEM((wide, chan), F32),
            pltpu.VMEM((wide, chan), F32),
            pltpu.VMEM((wide, chan), F32),
            pltpu.VMEM((wide, chan), F32),
            pltpu.VMEM((n_sp, 4, wide, chan), BF16),
            pltpu.VMEM((7, wide, chan), BF16),
            pltpu.VMEM((n_sp, 4, wide, chan), BF16),
            pltpu.VMEM((edges, group * wide, chan), BF16),
            pltpu.VMEM((edges, chan, group * wide), BF16),
            pltpu.VMEM((edges, group * wide, 3 * chan), BF16),
            pltpu.VMEM((chips, size, chan), CODE),
            pltpu.VMEM((chips, 1, chan), F32),
            pltpu.VMEM((chips, size, chan), CODE),
            pltpu.VMEM((chips, 1, chan), F32),
            pltpu.VMEM((n_dp, size, chan), CODE),
            pltpu.VMEM((n_dp, 3, 1, chan), F32),
            pltpu.VMEM((n_sp, size, chan), BF16),
            sem((6,)), sem((3,)), sem((3,)), sem((3,)), sem((2,)), sem((2,)), sem((4,)), sem((4,)), sem((6,)), sem((2,)), sem((3,)),
        ],
        compiler_params=pltpu.CompilerParams(
            collective_id=0, has_side_effects=True, vmem_limit_bytes=58 * 2**20),
    )(
        adjacency.transpose(0, 2, 1), block_in[0, 0], weights.reshape(3, 3 * chan, chan), out_bias.reshape(1, chan),
        cotangent[0, 0],
    )
    result, wgrad, grad_in = pl.pallas_call(
        hand_on,
        out_shape=(
            jax.ShapeDtypeStruct(tile, BF16), jax.ShapeDtypeStruct((9 * chan, chan), F32), jax.ShapeDtypeStruct(tile, BF16)),
        in_specs=[vmem, vmem, vmem],
        out_specs=(hbm, hbm, hbm),
        scratch_shapes=[sem((3,))],
        compiler_params=pltpu.CompilerParams(vmem_limit_bytes=4 * 2**20),
    )(*held)
    return (result[None, None], wgrad.reshape(weights.shape), grad_in[None, None])


def solution(mesh):
    placed = (
        P("dp", "space", None, None, None),
        P(),
        P(),
        P("space", None, None),
        P("dp", "space", None, None, None),
    )
    return jax.shard_map(
        functools.partial(per_device, mesh.shape["space"], mesh.shape["dp"]),
        mesh=mesh,
        in_specs=placed,
        out_specs=(P("dp", "space", None, None, None), P(), P("dp", "space", None, None, None)),
        check_vma=False,
    )
```

```python
import functools

import jax
import jax.numpy as jnp
from jax import lax
from jax.experimental import pallas as pl
from jax.experimental.pallas import tpu as pltpu
from jax.sharding import PartitionSpec as P

MESH = pl.DeviceIdType.MESH
ROWS = 8
PAIRS = 7
CORNERS = ((0, 0), (0, 2), (2, 2), (2, 0))
SIDES = ((0, 1), (1, 2), (2, 1), (1, 0))
F32 = jnp.float32
BF16 = jnp.bfloat16
CODE = jnp.int16


def silu(v):
    h = 0.5 * v
    return h + h * jnp.tanh(h)


def encode(v):
    top = jnp.maximum(jnp.max(jnp.abs(v), axis=0, keepdims=True), 1e-30)
    power = jnp.ceil(jnp.log2(top))
    code = jnp.clip(jnp.round(v * jnp.exp2(15.0 - power)), -32767.0, 32767.0)
    return code.astype(jnp.int32).astype(CODE), jnp.exp2(power - 15.0)


def decode(rows, scale):
    return rows.astype(jnp.int32).astype(F32) * scale


def wide_of(side):
    return -(-(side + 4) // 16) * 16


def block_kernel(
    n_sp, n_dp, side,
    adj_hbm, x_hbm, w_hbm, bias_hbm, g_hbm,
    out, wg_out, gin_out,
    x_in, g_in, w_in, bias, adj, adj_all, adj_row,
    taps, gtaps, flat, pad_grad, wt, vt, pair_w, pair_t, wgf, corr, half_in, col_a, col_b, col_c, col_d,
    ends, turned, gends, la, lat, lg, sent, sent_s, parts, parts_s, dps, dps_s, full,
    in_sem, edge_sem, near_g_sem, far_g_sem, adj_sem, swap_sem, share_sem, sample_sem, scale_sem, full_sem, near_sem,
):
    wide = wide_of(side)
    chan = 128
    chunks = side // ROWS
    me = lax.axis_index("space")
    my_dp = lax.axis_index("dp")
    core = lax.rem(me, 2)
    chip = me // 2
    chips = n_sp // 2
    partner = me + 1 - 2 * core
    size = full.shape[1]
    corners = chips == 4 and size == chan + 16
    near_count = 2 if corners else 4
    turn = chip if corners else 0

    barrier = pltpu.get_barrier_semaphore()

    def greet_sp(k, c):
        pl.semaphore_signal(barrier, inc=1, device_id=(lax.rem(me + k, n_sp), my_dp), device_id_type=MESH)
        return c

    def greet_dp(k, c):
        pl.semaphore_signal(barrier, inc=1, device_id=(me, lax.rem(my_dp + k, n_dp)), device_id_type=MESH)
        return c

    def load(src, dst, sem, parts=1):
        n = dst.shape[0] // parts
        for k in range(parts):
            rows = pl.ds(k * n, n)
            pltpu.make_async_copy(src.at[rows], dst.at[rows], sem).start()
        return pltpu.make_async_copy(src, dst, sem)

    loads = [
        load(adj_hbm, adj, in_sem.at[2]),
        load(x_hbm, x_in, in_sem.at[0], 4),
        load(g_hbm, g_in, in_sem.at[1], 4),
        load(w_hbm, w_in, in_sem.at[3]),
        load(bias_hbm, bias, in_sem.at[4]),
    ]
    lax.fori_loop(1, n_sp, greet_sp, 0)
    lax.fori_loop(1, n_dp, greet_dp, 0)

    def each_chip(do):
        if chips == 4:
            for other in (3 - chip, lax.rem(chip + 2, 4), chip + 1 - 2 * lax.rem(chip, 2)):
                do(other)
        else:
            def go(k, c):
                do(lax.rem(chip + k, chips))
                return c
            lax.fori_loop(1, chips, go, 0)

    def other_dp(j):
        return j + (j - my_dp + n_dp) // n_dp

    def remote(src, dst, send, recv, peer, dp=None):
        return pltpu.make_async_remote_copy(
            src_ref=src, dst_ref=dst, send_sem=send, recv_sem=recv,
            device_id=(peer, my_dp if dp is None else dp), device_id_type=MESH)

    def take(buf, count, sem):
        some = buf.at[pl.ds(0, count)]
        pltpu.make_async_copy(some, some, sem).wait()

    def take_rows(buf, count, first, rows, sem):
        some = buf.at[pl.ds(0, count), pl.ds(first, rows)]
        pltpu.make_async_copy(some, some, sem).wait()

    def pair_begin(buf, sems):
        mine = buf.at[me]
        each_chip(lambda h: remote(mine, mine, sems.at[0], sems.at[2], 2 * h + core).start())
        remote(mine, mine, sems.at[0], sems.at[1], partner).start()

    def pair_relay(buf, sems):
        take(buf, chips - 1, sems.at[2])
        def go(h):
            other = buf.at[2 * h + core]
            remote(other, other, sems.at[0], sems.at[1], partner).start()
        each_chip(go)

    def pair_finish(buf, sems):
        take(buf, chips, sems.at[1])
        take(buf, n_sp - 1, sems.at[0])

    def stretch_begin(src, buf, first, count, sems):
        to = buf.at[me, pl.ds(first, count)]

        def one(h, peer, sem):
            at = pl.ds((h if corners else 0) + first, count)
            remote(src.at[at], to, sems.at[0], sem, peer).start()

        each_chip(lambda h: one(h, 2 * h + core, sems.at[2]))
        one(chip, partner, sems.at[1])

    def stretch_relay(buf, first, count, sems):
        take_rows(buf, chips - 1, first, count, sems.at[2])

        def go(h):
            other = buf.at[2 * h + core, pl.ds(first, count)]
            remote(other, other, sems.at[0], sems.at[1], partner).start()

        each_chip(go)

    def stretch_finish(buf, first, count, sems):
        take_rows(buf, chips, first, count, sems.at[1])
        take_rows(buf, n_sp - 1, first, count, sems.at[0])

    r64 = lax.broadcasted_iota(jnp.int32, (wide, chan), 0)
    ra = lax.broadcasted_iota(jnp.int32, (wide, wide), 0)
    rb = lax.broadcasted_iota(jnp.int32, (wide, wide), 1)
    mirror = jnp.where(ra + rb == side - 1, 1.0, 0.0).astype(BF16)

    def flip(v):
        return jnp.dot(mirror, v, preferred_element_type=F32)

    s8 = lax.broadcasted_iota(jnp.int32, (8, chan), 0)

    def column(block, at):
        rows = block[0] if at == 0 else pltpu.roll(block[0], 8 - at, 0)
        for k in range(1, ROWS):
            one = block[k] if k == at else pltpu.roll(block[k], (k - at) % 8, 0)
            rows = jnp.where(s8 == k, one, rows)
        return rows

    tail = jnp.zeros((wide - side, chan), F32)

    def widen(v):
        return jnp.concatenate([v, tail], axis=0)

    loads[0].wait()
    lane = lax.broadcasted_iota(jnp.int32, (1, chan), 1)
    row = jnp.zeros((1, chan), jnp.int32)
    for k in range(8):
        for part in range(2):
            row = jnp.where(lane == 2 * k + part, adj[0, part, k], row)
    adj_row[me] = row
    loads[1].wait()
    for c in range(chunks):
        lo = c * ROWS
        col_a[lo:lo + ROWS, :] = silu(column(x_in[lo:lo + ROWS, 0:8, :].astype(F32), 0))
        col_b[lo:lo + ROWS, :] = silu(column(x_in[lo:lo + ROWS, side - 8:side, :].astype(F32), 7))
    for col in (col_a, col_b, col_c, col_d):
        col[side:wide, :] = tail
    ends[me, 0] = widen(silu(x_in[0].astype(F32))).astype(BF16)
    ends[me, 1] = col_b[...].astype(BF16)
    ends[me, 2] = flip(widen(silu(x_in[side - 1].astype(F32))).astype(BF16)).astype(BF16)
    ends[me, 3] = flip(col_a[...].astype(BF16)).astype(BF16)

    three = 3 * chan
    pairs = side // 2
    zero_row = jnp.zeros((wide, three), BF16)
    for buf in (taps, gtaps):
        buf[0, :, three:] = zero_row
        buf[pairs + 1, :, 0:three] = zero_row

    def shifts(v):
        return jnp.concatenate(
            [pltpu.roll(v, 1, 0).astype(BF16), v.astype(BF16), pltpu.roll(v, wide - 1, 0).astype(BF16)], axis=1)

    def spread(c, carry):
        for part in range(2):
            rows = []
            for k in range(ROWS // 2):
                i = c * ROWS + 2 * k + part
                p = c * (ROWS // 2) + k + 1
                a = widen(silu(x_in[i].astype(F32)))
                rows.append(a.astype(BF16))
                taps[p, :, part * three + chan:part * three + 2 * chan] = rows[-1]
                gtaps[p, :, part * three:(part + 1) * three] = shifts(widen(g_in[i].astype(F32)))
            n = ROWS // 2 * wide
            flat[part * chan:(part + 1) * chan, pl.ds(pl.multiple_of(c * n, n), n)] = jnp.concatenate(rows, axis=0).T
        return carry

    ahead = chunks * (1 - (2 * my_dp) // n_dp)
    loads[2].wait()
    lax.fori_loop(0, ahead, spread, 0)

    pl.semaphore_wait(barrier, n_sp + n_dp - 2)
    def tell(k, c):
        mine = adj_row.at[me]
        remote(mine, mine, adj_sem.at[0], adj_sem.at[1], lax.rem(me + k, n_sp)).start()
        return c

    lax.fori_loop(1, n_sp, tell, 0)
    pair_begin(ends, edge_sem)
    for c in range(chunks):
        lo = c * ROWS
        col_c[lo:lo + ROWS, :] = column(g_in[lo:lo + ROWS, 0:8, :].astype(F32), 0)
        col_d[lo:lo + ROWS, :] = column(g_in[lo:lo + ROWS, side - 8:side, :].astype(F32), 7)
    around = (
        flip(widen(g_in[0].astype(F32)).astype(BF16)).astype(BF16), flip(col_d[...].astype(BF16)).astype(BF16),
        widen(g_in[side - 1].astype(F32)).astype(BF16), col_c[...].astype(BF16))
    for k in range(7):
        turned[k] = around[(k + 3) % 4]
    for k in range(4):
        gends[me, k] = turned[turn + k]
    stretch_begin(turned, gends, 0, near_count, near_g_sem)

    lax.fori_loop(ahead, chunks, spread, 0)

    def grads(first, part):
        return gtaps[first:first + pairs, :, part * three:(part + 1) * three].reshape(pairs * wide, three)

    odd = jnp.dot(flat[...], grads(1, 1), preferred_element_type=F32)
    even = jnp.dot(flat[...], grads(1, 0), preferred_element_type=F32)
    below = jnp.dot(flat[0:chan], grads(0, 1), preferred_element_type=F32)
    above = jnp.dot(flat[chan:2 * chan], grads(2, 0), preferred_element_type=F32)
    for r, v in enumerate((odd[:chan] + above, odd[chan:] + even[:chan], even[chan:] + below)):
        for b in range(3):
            block = v[:, b * chan:(b + 1) * chan]
            if not corners:
                wgf[(3 * r + 2 - b) * chan:(3 * r + 3 - b) * chan, :] = block
            elif (r, b) == (1, 1):
                for k in range(n_sp):
                    wgf[k * size + chan:(k + 1) * size, :] = block[16 * k:16 * k + 16]
            else:
                kind = SIDES if (r + b) % 2 else CORNERS
                at = (kind.index((r, 2 - b)) + chips * ((r + b) % 2)) * size
                wgf[at:at + chan, :] = block
    used = 9 * chan
    if wgf.shape[0] > used:
        wgf[used:, :] = jnp.zeros((wgf.shape[0] - used, chan), F32)

    half = chips * size
    swap = remote(
        wgf.at[pl.ds(pl.multiple_of((1 - core) * half, 16), half)], half_in, swap_sem.at[0], swap_sem.at[1], partner)
    swap.start()
    take(adj_row, n_sp - 1, adj_sem.at[1])
    take(adj_row, n_sp - 1, adj_sem.at[0])
    spill = pltpu.make_async_copy(adj_row, adj_all, in_sem.at[5])
    spill.start()

    loads[3].wait()
    loads[4].wait()
    for r in range(3):
        for c in range(3):
            block = w_in[2 - r, (2 - c) * chan:(3 - c) * chan, :].astype(F32)
            wt[r, c * chan:(c + 1) * chan, :] = block.T.astype(BF16)
    for k in range(3):
        to = slice(k * chan, (k + 1) * chan)
        for e, (r, c) in enumerate(((2, 2 - k), (2 - k, 0), (0, k), (k, 2))):
            vt[e, to, :] = wt[r, c * chan:(c + 1) * chan, :]
    blank = jnp.zeros((three, chan), BF16)
    for buf, one in ((pair_w, w_in), (pair_t, wt)):
        for k in range(4):
            at = slice(k * three, (k + 1) * three)
            buf[at, 0:chan] = one[k] if k < 3 else blank
            buf[at, chan:] = one[k - 1] if k > 0 else blank
    def two_rows(buf, first, w):
        rows = jnp.concatenate([
            buf[pl.ds(first, PAIRS), :, three:].reshape(PAIRS * wide, three),
            buf[pl.ds(first + 1, PAIRS)].reshape(PAIRS * wide, 2 * three),
            buf[pl.ds(first + 2, PAIRS), :, 0:three].reshape(PAIRS * wide, three)], axis=1)
        return jnp.dot(rows, w[...], preferred_element_type=F32).reshape(PAIRS, wide, 2 * chan)

    def grad_chunk(c, carry):
        pad_grad[pl.ds(c * PAIRS, PAIRS)] = two_rows(gtaps, c * PAIRS, pair_t)
        return carry

    early = pairs // PAIRS // 2
    none = my_dp // n_dp
    lax.fori_loop(none, none + early // 2, grad_chunk, 0)
    swap.wait()

    def half_rows(h):
        at = pl.multiple_of(h * size, 16)
        return wgf[pl.ds(pl.multiple_of(core * half + h * size, 16), size), :] + half_in[pl.ds(at, size), :]

    def scatter(h):
        sent[h], sent_s[h] = encode(half_rows(h))
        remote(sent_s.at[h], parts_s.at[chip], scale_sem.at[0], scale_sem.at[1], 2 * h + core).start()

    each_chip(scatter)
    steps = 3 if size % 48 == 0 else 1
    step = size // steps
    for n in range(steps):
        rows = pl.ds(n * step, step)
        each_chip(lambda h, n=n, rows=rows: remote(
            sent.at[h, rows], parts.at[chip, rows], share_sem.at[0], share_sem.at[1 + n], 2 * h + core).start())

    pair_relay(ends, edge_sem)

    lax.fori_loop(none + early // 2, none + early, grad_chunk, 0)
    stretch_relay(gends, 0, near_count, near_g_sem)
    pair_finish(ends, edge_sem)
    spill.wait()

    def rim_cells(t, e):
        v = ends[adj_all[t, 0, 2 * e], adj_all[t, 0, 2 * e + 1]].astype(F32)
        k = ends[adj_all[t, 0, 8 + 2 * e], adj_all[t, 0, 9 + 2 * e]].astype(F32)[0:1]
        return jnp.where(r64 < side, v, jnp.where(r64 == side, k, 0.0)).astype(BF16)

    slot = core * chips + chip
    if corners:
        def tile_rows(t):
            return pl.ds(pl.multiple_of(t * wide, 16), wide)

        def turn_edges(t, carry):
            la[0, tile_rows(t), :] = rim_cells(t, chip)
            la[1, tile_rows(t), :] = rim_cells(t, lax.rem(chip + 3, 4))
            return carry

        def shift_edges(parity):
            def go(k, carry):
                t = 2 * k + parity
                g = gends[t, 1].astype(F32)
                lg[0, tile_rows(t), 0:chan] = pltpu.roll(g, 1, 0).astype(BF16)
                lg[0, tile_rows(t), chan:2 * chan] = gends[t, 1]
                lg[1, tile_rows(t), 0:chan] = pltpu.roll(gends[t, 0].astype(F32), wide - 1, 0).astype(BF16)
                return carry
            lax.fori_loop(0, chips, go, 0)

        lax.fori_loop(0, n_sp, turn_edges, 0)
        for k in range(2):
            lat[k] = la[k].T
        shift_edges(core)
        stretch_finish(gends, 0, near_count, near_g_sem)
        shift_edges(1 - core)
        here = jnp.dot(lat[0], lg[0, :, 0:2 * chan], preferred_element_type=F32)
        before = jnp.dot(lat[1], lg[1, :, 0:chan], preferred_element_type=F32)
        mine = half_rows(chip)
        rim = jnp.where(core == 0, here[:, 0:chan] + before, here[:, chan:])
        mine = jnp.concatenate([mine[0:chan] + rim, mine[chan:]], axis=0)
    else:
        stretch_finish(gends, 0, near_count, near_g_sem)
        group = la.shape[1] // wide
        corr[...] = jnp.zeros_like(corr)

        def rim_group(n, carry):
            def fill(j, c2):
                t = n * group + j
                at = pl.ds(pl.multiple_of(j * wide, 16), wide)
                for e in range(4):
                    la[e, at, :] = rim_cells(t, e)
                    lg[e, at, :] = shifts(gends[t, (e + 1) % 4].astype(F32))
                return c2

            lax.fori_loop(0, group, fill, 0)
            for e in range(4):
                res = jnp.dot(la[e].T, lg[e], preferred_element_type=F32)
                for k in range(3):
                    r, c = ((0, k), (k, 2), (2, 2 - k), (2 - k, 0))[e]
                    at = (3 * r + c) * chan
                    corr[at:at + chan, :] += res[:, k * chan:(k + 1) * chan]
            return carry

        lax.fori_loop(0, n_sp // group, rim_group, 0)
        mine = half_rows(chip) + corr[pl.ds(pl.multiple_of(slot * size, 16), size), :]

    def to_sample(n, j):
        one, scale = dps.at[my_dp, pl.ds(n * step, step)], dps_s.at[my_dp, n]
        remote(scale, scale, scale_sem.at[2], scale_sem.at[3 + n], me, other_dp(j)).start()
        remote(one, one, sample_sem.at[0], sample_sem.at[1 + n], me, other_dp(j)).start()

    take(parts_s, chips - 1, scale_sem.at[1])
    for n in range(steps):
        rows = pl.ds(n * step, step)
        take_rows(parts, chips - 1, n * step, step, share_sem.at[1 + n])

        def add_part(k, t, rows=rows):
            h = lax.rem(chip + k, chips)
            return t + decode(parts[h, rows], parts_s[h])

        some = lax.fori_loop(1, chips, add_part, mine[n * step:(n + 1) * step])
        dps[my_dp, rows], dps_s[my_dp, n] = encode(some)
        to_sample(n, 0)
    for n in range(steps):
        for j in range(1, n_dp - 1):
            to_sample(n, j)
    take(sent, chips - 1, share_sem.at[0])
    take(sent_s, chips - 1, scale_sem.at[0])
    if corners:
        stretch_begin(turned, gends, 2, 2, far_g_sem)

    def near(buf, e):
        return buf[adj[0, 0, e], adj[0, 1, e]]

    corner = [ends[adj[0, 0, 4 + k], adj[0, 1, 4 + k]].astype(F32)[0:1] for k in range(4)]

    def rim_row(v, behind, ahead):
        return jnp.where(r64 < side, v, jnp.where(r64 == side, behind, jnp.where(r64 == wide - 1, ahead, 0.0)))

    taps[0, :, three:] = shifts(rim_row(flip(near(ends, 0)), corner[1], corner[0]))
    taps[pairs + 1, :, 0:three] = shifts(rim_row(near(ends, 2).astype(F32), corner[2], corner[3]))
    col_a[...] = near(ends, 3).astype(F32)
    col_b[...] = flip(near(ends, 1))

    def spread_act(c, carry):
        for part in range(2):
            at = part * three
            for k in range(ROWS // 2):
                p = c * (ROWS // 2) + k + 1
                i = pl.ds(c * ROWS + 2 * k + part, 1)
                v = taps[p, :, at + chan:at + 2 * chan].astype(F32)
                taps[p, :, at:at + chan] = jnp.where(r64 == 0, col_a[i, :], pltpu.roll(v, 1, 0)).astype(BF16)
                taps[p, :, at + 2 * chan:at + three] = jnp.where(
                    r64 == side - 1, col_b[i, :], pltpu.roll(v, wide - 1, 0)).astype(BF16)
        return carry

    lax.fori_loop(0, chunks, spread_act, 0)
    lax.fori_loop(early, pairs // PAIRS, grad_chunk, 0)

    def conv_chunk(c, carry):
        conv = two_rows(taps, c * PAIRS, pair_w)
        for k in range(2 * PAIRS):
            i = 2 * PAIRS * c + k
            at = k % 2 * chan
            out[i] = (x_in[i].astype(F32) + conv[k // 2, 0:side, at:at + chan] + bias[...]).astype(BF16)
        return carry

    most = pairs // PAIRS - 1
    lax.fori_loop(0, most, conv_chunk, 0)

    for n in range(steps):
        take_rows(dps_s, n_dp - 1, n, 1, scale_sem.at[3 + n])
        take_rows(dps, n_dp - 1, n * step, step, sample_sem.at[1 + n])
        at = pl.ds(n * step, step)
        total = decode(dps[0, at], dps_s[0, n])
        for d in range(1, n_dp):
            total = total + decode(dps[d, at], dps_s[d, n])
        one = full.at[me, pl.ds(n * step, step)]
        one[...] = total.astype(BF16)

        last = n == steps - 1

        def share(h, one=one, n=n, last=last):
            remote(one, one, full_sem.at[0], near_sem.at[n], 2 * h + core).start()
            if last:
                remote(one, one, full_sem.at[0], near_sem.at[n], 2 * h + 1 - core).start()

        if chips == 4:
            for j in range(3):
                share(j + (j - chip + 4) // 4)
        else:
            each_chip(share)
        remote(one, one, full_sem.at[0], near_sem.at[n] if last else full_sem.at[1], partner).start()
    take(dps, n_dp - 1, sample_sem.at[0])
    take_rows(dps_s, n_dp - 1, 0, steps, scale_sem.at[2])
    if corners:
        stretch_relay(gends, 2, 2, far_g_sem)
    lax.fori_loop(most, pairs // PAIRS, conv_chunk, 0)

    if corners:
        stretch_finish(gends, 2, 2, far_g_sem)

    def rim_grad(e):
        at = adj[0, 1, e]
        g = gends[adj[0, 0, e], lax.rem(at + 5 - turn, 4)]
        v = jnp.dot(shifts(g.astype(F32)), vt[at], preferred_element_type=F32)
        return jnp.where(r64 < side, v, 0.0).astype(BF16)

    def rim_corner(k):
        at = adj[0, 1, 4 + k]
        v = jnp.dot(gends[adj[0, 0, 4 + k], lax.rem(at + 5 - turn, 4)], vt[at, 0:chan, :], preferred_element_type=F32)
        return v[side - 1:side].astype(BF16).astype(F32)

    add = [rim_corner(k) for k in range(4)]
    pad_grad[0, :, 0:chan] += rim_grad(0).astype(F32)
    pad_grad[pairs - 1, :, chan:] += flip(rim_grad(2))
    col_a[...] = flip(rim_grad(3)) + jnp.where(r64 == 0, add[0], jnp.where(r64 == side - 1, add[3], 0.0))
    col_b[...] = rim_grad(1).astype(F32) + jnp.where(r64 == 0, add[1], jnp.where(r64 == side - 1, add[2], 0.0))

    r56 = lax.broadcasted_iota(jnp.int32, (side, chan), 0)

    def finish_rows(c, carry):
        for k in range(ROWS):
            i = c * ROWS + k
            p = pad_grad[c * (ROWS // 2) + k // 2, 0:side, k % 2 * chan:(k % 2 + 1) * chan]
            p = p + jnp.where(r56 == 0, col_a[pl.ds(i, 1), :], jnp.where(r56 == side - 1, col_b[pl.ds(i, 1), :], 0.0))
            v = x_in[i].astype(F32)
            s = 0.5 + 0.5 * jnp.tanh(0.5 * v)
            gin_out[i] = (g_in[i].astype(F32) + p * s * (1.0 + v * (1.0 - s))).astype(BF16)
        return carry

    def share_relay(n):
        take_rows(full, chips - 1, n * step, step, near_sem.at[n])

        def go(h):
            one = full.at[2 * h + core, pl.ds(n * step, step)]
            remote(one, one, full_sem.at[0], full_sem.at[1], partner).start()

        each_chip(go)

    done = 0
    for n in range(steps - 1):
        share_relay(n)
        upto = chunks * (n + 1) // steps
        lax.fori_loop(done, upto, finish_rows, 0)
        done = upto
    lax.fori_loop(done, chunks, finish_rows, 0)
    take_rows(full, n_sp - 1, (steps - 1) * step, step, near_sem.at[steps - 1])
    if steps > 1:
        take_rows(full, chips, 0, (steps - 1) * step, full_sem.at[1])
    take(full, n_sp - 1, full_sem.at[0])

    if corners:
        for t in range(n_sp):
            v = full[t].astype(F32)
            r, c = (SIDES if t % 2 else CORNERS)[t // 2]
            wg_out[(3 * r + c) * chan:(3 * r + c + 1) * chan, :] = v[0:chan]
            at = 4 * chan + 16 * (t % 2 * chips + t // 2)
            wg_out[at:at + 16, :] = v[chan:]
    else:
        def open_rows(t, carry):
            at = (lax.rem(t, 2) * chips + t // 2) * size
            wg_out[pl.ds(pl.multiple_of(at, 16), size), :] = full[t].astype(F32)
            return carry

        lax.fori_loop(0, n_sp, open_rows, 0)


def hand_on(a, wg, c, a_out, wg_out, c_out, sems):
    def begin(src, dst, sem, parts=4):
        n = dst.shape[0] // parts
        for k in range(parts):
            rows = pl.ds(k * n, n)
            pltpu.make_async_copy(src.at[rows], dst.at[rows], sem).start()
        return pltpu.make_async_copy(dst, dst, sem)

    for one in [begin(a, a_out, sems.at[0]), begin(c, c_out, sems.at[1]), begin(wg, wg_out, sems.at[2])]:
        one.wait()


def per_device(n_sp, n_dp, block_in, weights, out_bias, adjacency, cotangent):
    side, chan = block_in.shape[2], block_in.shape[4]
    wide = wide_of(side)
    chips = n_sp // 2
    size = -(-9 * chan // (16 * n_sp)) * 16
    corners = chips == 4 and size == chan + 16
    group = n_sp if corners else 4
    edges = 2 if corners else 4
    vmem = pl.BlockSpec(memory_space=pltpu.VMEM)
    hbm = pl.BlockSpec(memory_space=pltpu.HBM)
    sem = pltpu.SemaphoreType.DMA
    tile = (side, side, chan)
    held = pl.pallas_call(
        functools.partial(block_kernel, n_sp, n_dp, side),
        out_shape=(pltpu.VMEM(tile, BF16), pltpu.VMEM((n_sp * size, chan), F32), pltpu.VMEM(tile, BF16)),
        in_specs=[hbm] * 5,
        out_specs=(vmem, vmem, vmem),
        scratch_shapes=[
            pltpu.VMEM(tile, BF16),
            pltpu.VMEM(tile, BF16),
            pltpu.VMEM((3, 3 * chan, chan), BF16),
            pltpu.VMEM((1, chan), F32),
            pltpu.SMEM((1, 2, 8), jnp.int32),
            pltpu.SMEM((n_sp, 1, chan), jnp.int32),
            pltpu.VMEM((n_sp, 1, chan), jnp.int32),
            pltpu.VMEM((side // 2 + 2, wide, 6 * chan), BF16),
            pltpu.VMEM((side // 2 + 2, wide, 6 * chan), BF16),
            pltpu.VMEM((2 * chan, side // 2 * wide), BF16),
            pltpu.VMEM((side // 2, wide, 2 * chan), F32),
            pltpu.VMEM((3, 3 * chan, chan), BF16),
            pltpu.VMEM((4, 3 * chan, chan), BF16),
            pltpu.VMEM((12 * chan, 2 * chan), BF16),
            pltpu.VMEM((12 * chan, 2 * chan), BF16),
            pltpu.VMEM((n_sp * size, chan), F32),
            pltpu.VMEM((n_sp * size, chan), F32),
            pltpu.VMEM((chips * size, chan), F32),
            pltpu.VMEM((wide, chan), F32),
            pltpu.VMEM((wide, chan), F32),
            pltpu.VMEM((wide, chan), F32),
            pltpu.VMEM((wide, chan), F32),
            pltpu.VMEM((n_sp, 4, wide, chan), BF16),
            pltpu.VMEM((7, wide, chan), BF16),
            pltpu.VMEM((n_sp, 4, wide, chan), BF16),
            pltpu.VMEM((edges, group * wide, chan), BF16),
            pltpu.VMEM((edges, chan, group * wide), BF16),
            pltpu.VMEM((edges, group * wide, 3 * chan), BF16),
            pltpu.VMEM((chips, size, chan), CODE),
            pltpu.VMEM((chips, 1, chan), F32),
            pltpu.VMEM((chips, size, chan), CODE),
            pltpu.VMEM((chips, 1, chan), F32),
            pltpu.VMEM((n_dp, size, chan), CODE),
            pltpu.VMEM((n_dp, 3, 1, chan), F32),
            pltpu.VMEM((n_sp, size, chan), BF16),
            sem((6,)), sem((3,)), sem((3,)), sem((3,)), sem((2,)), sem((2,)), sem((4,)), sem((4,)), sem((6,)), sem((2,)), sem((3,)),
        ],
        compiler_params=pltpu.CompilerParams(
            collective_id=0, has_side_effects=True, vmem_limit_bytes=58 * 2**20),
    )(
        adjacency.transpose(0, 2, 1), block_in[0, 0], weights.reshape(3, 3 * chan, chan), out_bias.reshape(1, chan),
        cotangent[0, 0],
    )
    result, wgrad, grad_in = pl.pallas_call(
        hand_on,
        out_shape=(
            jax.ShapeDtypeStruct(tile, BF16), jax.ShapeDtypeStruct((9 * chan, chan), F32), jax.ShapeDtypeStruct(tile, BF16)),
        in_specs=[vmem, vmem, vmem],
        out_specs=(hbm, hbm, hbm),
        scratch_shapes=[sem((3,))],
        compiler_params=pltpu.CompilerParams(vmem_limit_bytes=4 * 2**20),
    )(*held)
    return (result[None, None], wgrad.reshape(weights.shape), grad_in[None, None])


def solution(mesh):
    placed = (
        P("dp", "space", None, None, None),
        P(),
        P(),
        P("space", None, None),
        P("dp", "space", None, None, None),
    )
    return jax.shard_map(
        functools.partial(per_device, mesh.shape["space"], mesh.shape["dp"]),
        mesh=mesh,
        in_specs=placed,
        out_specs=(P("dp", "space", None, None, None), P(), P("dp", "space", None, None, None)),
        check_vma=False,
    )
```

```python
import functools

import jax
import jax.numpy as jnp
from jax import lax
from jax.experimental import pallas as pl
from jax.experimental.pallas import tpu as pltpu
from jax.sharding import PartitionSpec as P

MESH = pl.DeviceIdType.MESH
ROWS = 8
PAIRS = 7
CORNERS = ((0, 0), (0, 2), (2, 2), (2, 0))
SIDES = ((0, 1), (1, 2), (2, 1), (1, 0))
F32 = jnp.float32
BF16 = jnp.bfloat16
CODE = jnp.int16


def silu(v):
    h = 0.5 * v
    return h + h * jnp.tanh(h)


def encode(v):
    top = jnp.maximum(jnp.max(jnp.abs(v), axis=0, keepdims=True), 1e-30)
    power = jnp.ceil(jnp.log2(top))
    code = jnp.clip(jnp.round(v * jnp.exp2(15.0 - power)), -32767.0, 32767.0)
    return code.astype(jnp.int32).astype(CODE), jnp.exp2(power - 15.0)


def decode(rows, scale):
    return rows.astype(jnp.int32).astype(F32) * scale


def wide_of(side):
    return -(-(side + 4) // 16) * 16


def block_kernel(
    n_sp, n_dp, side,
    adj_hbm, x_hbm, w_hbm, bias_hbm, g_hbm,
    out, wg_out, gin_out,
    x_in, g_in, w_in, bias, adj, adj_all, adj_row,
    taps, gtaps, flat, pad_grad, wt, vt, pair_w, pair_t, wgf, corr, half_in, col_a, col_b, col_c, col_d,
    ends, packed, turned, gends, la, lat, lg, sent, sent_s, parts, parts_s, dps, dps_s, full,
    in_sem, edge_sem, near_g_sem, far_g_sem, adj_sem, swap_sem, share_sem, sample_sem, scale_sem, full_sem, near_sem,
):
    wide = wide_of(side)
    chan = 128
    chunks = side // ROWS
    me = lax.axis_index("space")
    my_dp = lax.axis_index("dp")
    core = lax.rem(me, 2)
    chip = me // 2
    chips = n_sp // 2
    partner = me + 1 - 2 * core
    size = full.shape[1]
    corners = chips == 4 and size == chan + 16
    near_count = 2 if corners else 4
    turn = chip if corners else 0

    barrier = pltpu.get_barrier_semaphore()

    def greet_sp(k, c):
        pl.semaphore_signal(barrier, inc=1, device_id=(lax.rem(me + k, n_sp), my_dp), device_id_type=MESH)
        return c

    def greet_dp(k, c):
        pl.semaphore_signal(barrier, inc=1, device_id=(me, lax.rem(my_dp + k, n_dp)), device_id_type=MESH)
        return c

    def load(src, dst, sem, parts=1):
        n = dst.shape[0] // parts
        for k in range(parts):
            rows = pl.ds(k * n, n)
            pltpu.make_async_copy(src.at[rows], dst.at[rows], sem).start()
        return pltpu.make_async_copy(src, dst, sem)

    loads = [
        load(adj_hbm, adj, in_sem.at[2]),
        load(x_hbm, x_in, in_sem.at[0], 4),
        load(g_hbm, g_in, in_sem.at[1], 4),
        load(w_hbm, w_in, in_sem.at[3]),
        load(bias_hbm, bias, in_sem.at[4]),
    ]
    lax.fori_loop(1, n_sp, greet_sp, 0)
    lax.fori_loop(1, n_dp, greet_dp, 0)

    def each_chip(do):
        if chips == 4:
            for other in (3 - chip, lax.rem(chip + 2, 4), chip + 1 - 2 * lax.rem(chip, 2)):
                do(other)
        else:
            def go(k, c):
                do(lax.rem(chip + k, chips))
                return c
            lax.fori_loop(1, chips, go, 0)

    def other_dp(j):
        return j + (j - my_dp + n_dp) // n_dp

    def remote(src, dst, send, recv, peer, dp=None):
        return pltpu.make_async_remote_copy(
            src_ref=src, dst_ref=dst, send_sem=send, recv_sem=recv,
            device_id=(peer, my_dp if dp is None else dp), device_id_type=MESH)

    def take(buf, count, sem):
        some = buf.at[pl.ds(0, count)]
        pltpu.make_async_copy(some, some, sem).wait()

    def take_rows(buf, count, first, rows, sem):
        some = buf.at[pl.ds(0, count), pl.ds(first, rows)]
        pltpu.make_async_copy(some, some, sem).wait()

    def pair_begin(buf, sems):
        mine = buf.at[me]
        each_chip(lambda h: remote(mine, mine, sems.at[0], sems.at[2], 2 * h + core).start())
        remote(mine, mine, sems.at[0], sems.at[1], partner).start()

    def pair_relay(buf, sems):
        take(buf, chips - 1, sems.at[2])
        def go(h):
            other = buf.at[2 * h + core]
            remote(other, other, sems.at[0], sems.at[1], partner).start()
        each_chip(go)

    def pair_finish(buf, sems):
        take(buf, chips, sems.at[1])
        take(buf, n_sp - 1, sems.at[0])

    def stretch_begin(src, buf, first, count, sems):
        to = buf.at[me, pl.ds(first, count)]

        def one(h, peer, sem):
            at = pl.ds((h if corners else 0) + first, count)
            remote(src.at[at], to, sems.at[0], sem, peer).start()

        each_chip(lambda h: one(h, 2 * h + core, sems.at[2]))
        one(chip, partner, sems.at[1])

    def stretch_relay(buf, first, count, sems):
        take_rows(buf, chips - 1, first, count, sems.at[2])

        def go(h):
            other = buf.at[2 * h + core, pl.ds(first, count)]
            remote(other, other, sems.at[0], sems.at[1], partner).start()

        each_chip(go)

    def stretch_finish(buf, first, count, sems):
        take_rows(buf, chips, first, count, sems.at[1])
        take_rows(buf, n_sp - 1, first, count, sems.at[0])

    r64 = lax.broadcasted_iota(jnp.int32, (wide, chan), 0)
    ra = lax.broadcasted_iota(jnp.int32, (wide, wide), 0)
    rb = lax.broadcasted_iota(jnp.int32, (wide, wide), 1)
    mirror = jnp.where(ra + rb == side - 1, 1.0, 0.0).astype(BF16)

    def flip(v):
        return jnp.dot(mirror, v, preferred_element_type=F32)

    s8 = lax.broadcasted_iota(jnp.int32, (8, chan), 0)

    def column(block, at):
        rows = block[0] if at == 0 else pltpu.roll(block[0], 8 - at, 0)
        for k in range(1, ROWS):
            one = block[k] if k == at else pltpu.roll(block[k], (k - at) % 8, 0)
            rows = jnp.where(s8 == k, one, rows)
        return rows

    tail = jnp.zeros((wide - side, chan), F32)

    def widen(v):
        return jnp.concatenate([v, tail], axis=0)

    loads[0].wait()
    lane = lax.broadcasted_iota(jnp.int32, (1, chan), 1)
    row = jnp.zeros((1, chan), jnp.int32)
    for k in range(8):
        for part in range(2):
            row = jnp.where(lane == 2 * k + part, adj[0, part, k], row)
    adj_row[me] = row
    loads[1].wait()
    for c in range(chunks):
        lo = c * ROWS
        col_a[lo:lo + ROWS, :] = silu(column(x_in[lo:lo + ROWS, 0:8, :].astype(F32), 0))
        col_b[lo:lo + ROWS, :] = silu(column(x_in[lo:lo + ROWS, side - 8:side, :].astype(F32), 7))
    for col in (col_a, col_b, col_c, col_d):
        col[side:wide, :] = tail
    for k, v in enumerate((
        silu(x_in[0].astype(F32)), col_b[0:side, :], flip(widen(silu(x_in[side - 1].astype(F32))).astype(BF16))[0:side],
        flip(col_a[...].astype(BF16))[0:side])):
        packed[me, k * side:(k + 1) * side, :] = v.astype(BF16)

    three = 3 * chan
    pairs = side // 2
    zero_row = jnp.zeros((wide, three), BF16)
    for buf in (taps, gtaps):
        buf[0, :, three:] = zero_row
        buf[pairs + 1, :, 0:three] = zero_row

    def shifts(v):
        return jnp.concatenate(
            [pltpu.roll(v, 1, 0).astype(BF16), v.astype(BF16), pltpu.roll(v, wide - 1, 0).astype(BF16)], axis=1)

    def spread(c, carry):
        for part in range(2):
            rows = []
            for k in range(ROWS // 2):
                i = c * ROWS + 2 * k + part
                p = c * (ROWS // 2) + k + 1
                a = widen(silu(x_in[i].astype(F32)))
                rows.append(a.astype(BF16))
                taps[p, :, part * three + chan:part * three + 2 * chan] = rows[-1]
                gtaps[p, :, part * three:(part + 1) * three] = shifts(widen(g_in[i].astype(F32)))
            n = ROWS // 2 * wide
            flat[part * chan:(part + 1) * chan, pl.ds(pl.multiple_of(c * n, n), n)] = jnp.concatenate(rows, axis=0).T
        return carry

    ahead = chunks * (1 - (2 * my_dp) // n_dp)
    loads[2].wait()
    lax.fori_loop(0, ahead, spread, 0)

    pl.semaphore_wait(barrier, n_sp + n_dp - 2)
    def tell(k, c):
        mine = adj_row.at[me]
        remote(mine, mine, adj_sem.at[0], adj_sem.at[1], lax.rem(me + k, n_sp)).start()
        return c

    lax.fori_loop(1, n_sp, tell, 0)
    pair_begin(packed, edge_sem)
    for c in range(chunks):
        lo = c * ROWS
        col_c[lo:lo + ROWS, :] = column(g_in[lo:lo + ROWS, 0:8, :].astype(F32), 0)
        col_d[lo:lo + ROWS, :] = column(g_in[lo:lo + ROWS, side - 8:side, :].astype(F32), 7)
    around = (
        flip(widen(g_in[0].astype(F32)).astype(BF16)).astype(BF16), flip(col_d[...].astype(BF16)).astype(BF16),
        widen(g_in[side - 1].astype(F32)).astype(BF16), col_c[...].astype(BF16))
    for k in range(7):
        turned[k] = around[(k + 3) % 4]
    for k in range(4):
        gends[me, k] = turned[turn + k]
    stretch_begin(turned, gends, 0, near_count, near_g_sem)

    lax.fori_loop(ahead, chunks, spread, 0)

    def grads(first, part):
        return gtaps[first:first + pairs, :, part * three:(part + 1) * three].reshape(pairs * wide, three)

    odd = jnp.dot(flat[...], grads(1, 1), preferred_element_type=F32)
    even = jnp.dot(flat[...], grads(1, 0), preferred_element_type=F32)
    below = jnp.dot(flat[0:chan], grads(0, 1), preferred_element_type=F32)
    above = jnp.dot(flat[chan:2 * chan], grads(2, 0), preferred_element_type=F32)
    for r, v in enumerate((odd[:chan] + above, odd[chan:] + even[:chan], even[chan:] + below)):
        for b in range(3):
            block = v[:, b * chan:(b + 1) * chan]
            if not corners:
                wgf[(3 * r + 2 - b) * chan:(3 * r + 3 - b) * chan, :] = block
            elif (r, b) == (1, 1):
                for k in range(n_sp):
                    wgf[k * size + chan:(k + 1) * size, :] = block[16 * k:16 * k + 16]
            else:
                kind = SIDES if (r + b) % 2 else CORNERS
                at = (kind.index((r, 2 - b)) + chips * ((r + b) % 2)) * size
                wgf[at:at + chan, :] = block
    used = 9 * chan
    if wgf.shape[0] > used:
        wgf[used:, :] = jnp.zeros((wgf.shape[0] - used, chan), F32)

    half = chips * size
    swap = remote(
        wgf.at[pl.ds(pl.multiple_of((1 - core) * half, 16), half)], half_in, swap_sem.at[0], swap_sem.at[1], partner)
    swap.start()
    take(adj_row, n_sp - 1, adj_sem.at[1])
    take(adj_row, n_sp - 1, adj_sem.at[0])
    spill = pltpu.make_async_copy(adj_row, adj_all, in_sem.at[5])
    spill.start()

    loads[3].wait()
    loads[4].wait()
    for r in range(3):
        for c in range(3):
            block = w_in[2 - r, (2 - c) * chan:(3 - c) * chan, :].astype(F32)
            wt[r, c * chan:(c + 1) * chan, :] = block.T.astype(BF16)
    for k in range(3):
        to = slice(k * chan, (k + 1) * chan)
        for e, (r, c) in enumerate(((2, 2 - k), (2 - k, 0), (0, k), (k, 2))):
            vt[e, to, :] = wt[r, c * chan:(c + 1) * chan, :]
    blank = jnp.zeros((three, chan), BF16)
    for buf, one in ((pair_w, w_in), (pair_t, wt)):
        for k in range(4):
            at = slice(k * three, (k + 1) * three)
            buf[at, 0:chan] = one[k] if k < 3 else blank
            buf[at, chan:] = one[k - 1] if k > 0 else blank
    def two_rows(buf, first, w):
        rows = jnp.concatenate([
            buf[pl.ds(first, PAIRS), :, three:].reshape(PAIRS * wide, three),
            buf[pl.ds(first + 1, PAIRS)].reshape(PAIRS * wide, 2 * three),
            buf[pl.ds(first + 2, PAIRS), :, 0:three].reshape(PAIRS * wide, three)], axis=1)
        return jnp.dot(rows, w[...], preferred_element_type=F32).reshape(PAIRS, wide, 2 * chan)

    def grad_chunk(c, carry):
        pad_grad[pl.ds(c * PAIRS, PAIRS)] = two_rows(gtaps, c * PAIRS, pair_t)
        return carry

    early = pairs // PAIRS // 2
    none = my_dp // n_dp
    lax.fori_loop(none, none + early // 2, grad_chunk, 0)
    swap.wait()

    def half_rows(h):
        at = pl.multiple_of(h * size, 16)
        return wgf[pl.ds(pl.multiple_of(core * half + h * size, 16), size), :] + half_in[pl.ds(at, size), :]

    def scatter(h):
        sent[h], sent_s[h] = encode(half_rows(h))
        remote(sent_s.at[h], parts_s.at[chip], scale_sem.at[0], scale_sem.at[1], 2 * h + core).start()

    each_chip(scatter)
    steps = 3 if size % 48 == 0 else 1
    step = size // steps
    for n in range(steps):
        rows = pl.ds(n * step, step)
        each_chip(lambda h, n=n, rows=rows: remote(
            sent.at[h, rows], parts.at[chip, rows], share_sem.at[0], share_sem.at[1 + n], 2 * h + core).start())

    pair_relay(packed, edge_sem)

    lax.fori_loop(none + early // 2, none + early, grad_chunk, 0)
    stretch_relay(gends, 0, near_count, near_g_sem)
    pair_finish(packed, edge_sem)

    def unpack(t, carry):
        for k in range(4):
            ends[t, k] = widen(packed[t, k * side:(k + 1) * side, :].astype(F32)).astype(BF16)
        return carry

    lax.fori_loop(0, n_sp, unpack, 0)
    spill.wait()

    def rim_cells(t, e):
        v = ends[adj_all[t, 0, 2 * e], adj_all[t, 0, 2 * e + 1]].astype(F32)
        k = ends[adj_all[t, 0, 8 + 2 * e], adj_all[t, 0, 9 + 2 * e]].astype(F32)[0:1]
        return jnp.where(r64 < side, v, jnp.where(r64 == side, k, 0.0)).astype(BF16)

    slot = core * chips + chip
    if corners:
        def tile_rows(t):
            return pl.ds(pl.multiple_of(t * wide, 16), wide)

        def turn_edges(t, carry):
            la[0, tile_rows(t), :] = rim_cells(t, chip)
            la[1, tile_rows(t), :] = rim_cells(t, lax.rem(chip + 3, 4))
            return carry

        def shift_edges(parity):
            def go(k, carry):
                t = 2 * k + parity
                g = gends[t, 1].astype(F32)
                lg[0, tile_rows(t), 0:chan] = pltpu.roll(g, 1, 0).astype(BF16)
                lg[0, tile_rows(t), chan:2 * chan] = gends[t, 1]
                lg[1, tile_rows(t), 0:chan] = pltpu.roll(gends[t, 0].astype(F32), wide - 1, 0).astype(BF16)
                return carry
            lax.fori_loop(0, chips, go, 0)

        lax.fori_loop(0, n_sp, turn_edges, 0)
        for k in range(2):
            lat[k] = la[k].T
        shift_edges(core)
        stretch_finish(gends, 0, near_count, near_g_sem)
        shift_edges(1 - core)
        here = jnp.dot(lat[0], lg[0, :, 0:2 * chan], preferred_element_type=F32)
        before = jnp.dot(lat[1], lg[1, :, 0:chan], preferred_element_type=F32)
        mine = half_rows(chip)
        rim = jnp.where(core == 0, here[:, 0:chan] + before, here[:, chan:])
        mine = jnp.concatenate([mine[0:chan] + rim, mine[chan:]], axis=0)
    else:
        stretch_finish(gends, 0, near_count, near_g_sem)
        group = la.shape[1] // wide
        corr[...] = jnp.zeros_like(corr)

        def rim_group(n, carry):
            def fill(j, c2):
                t = n * group + j
                at = pl.ds(pl.multiple_of(j * wide, 16), wide)
                for e in range(4):
                    la[e, at, :] = rim_cells(t, e)
                    lg[e, at, :] = shifts(gends[t, (e + 1) % 4].astype(F32))
                return c2

            lax.fori_loop(0, group, fill, 0)
            for e in range(4):
                res = jnp.dot(la[e].T, lg[e], preferred_element_type=F32)
                for k in range(3):
                    r, c = ((0, k), (k, 2), (2, 2 - k), (2 - k, 0))[e]
                    at = (3 * r + c) * chan
                    corr[at:at + chan, :] += res[:, k * chan:(k + 1) * chan]
            return carry

        lax.fori_loop(0, n_sp // group, rim_group, 0)
        mine = half_rows(chip) + corr[pl.ds(pl.multiple_of(slot * size, 16), size), :]

    def to_sample(n, j):
        one, scale = dps.at[my_dp, pl.ds(n * step, step)], dps_s.at[my_dp, n]
        remote(scale, scale, scale_sem.at[2], scale_sem.at[3 + n], me, other_dp(j)).start()
        remote(one, one, sample_sem.at[0], sample_sem.at[1 + n], me, other_dp(j)).start()

    take(parts_s, chips - 1, scale_sem.at[1])
    for n in range(steps):
        rows = pl.ds(n * step, step)
        take_rows(parts, chips - 1, n * step, step, share_sem.at[1 + n])

        def add_part(k, t, rows=rows):
            h = lax.rem(chip + k, chips)
            return t + decode(parts[h, rows], parts_s[h])

        some = lax.fori_loop(1, chips, add_part, mine[n * step:(n + 1) * step])
        dps[my_dp, rows], dps_s[my_dp, n] = encode(some)
        to_sample(n, 0)
    for n in range(steps):
        for j in range(1, n_dp - 1):
            to_sample(n, j)
    take(sent, chips - 1, share_sem.at[0])
    take(sent_s, chips - 1, scale_sem.at[0])
    if corners:
        stretch_begin(turned, gends, 2, 2, far_g_sem)

    def near(buf, e):
        return buf[adj[0, 0, e], adj[0, 1, e]]

    corner = [ends[adj[0, 0, 4 + k], adj[0, 1, 4 + k]].astype(F32)[0:1] for k in range(4)]

    def rim_row(v, behind, ahead):
        return jnp.where(r64 < side, v, jnp.where(r64 == side, behind, jnp.where(r64 == wide - 1, ahead, 0.0)))

    taps[0, :, three:] = shifts(rim_row(flip(near(ends, 0)), corner[1], corner[0]))
    taps[pairs + 1, :, 0:three] = shifts(rim_row(near(ends, 2).astype(F32), corner[2], corner[3]))
    col_a[...] = near(ends, 3).astype(F32)
    col_b[...] = flip(near(ends, 1))

    def spread_act(c, carry):
        for part in range(2):
            at = part * three
            for k in range(ROWS // 2):
                p = c * (ROWS // 2) + k + 1
                i = pl.ds(c * ROWS + 2 * k + part, 1)
                v = taps[p, :, at + chan:at + 2 * chan].astype(F32)
                taps[p, :, at:at + chan] = jnp.where(r64 == 0, col_a[i, :], pltpu.roll(v, 1, 0)).astype(BF16)
                taps[p, :, at + 2 * chan:at + three] = jnp.where(
                    r64 == side - 1, col_b[i, :], pltpu.roll(v, wide - 1, 0)).astype(BF16)
        return carry

    lax.fori_loop(0, chunks, spread_act, 0)
    lax.fori_loop(early, pairs // PAIRS, grad_chunk, 0)

    def conv_chunk(c, carry):
        conv = two_rows(taps, c * PAIRS, pair_w)
        for k in range(2 * PAIRS):
            i = 2 * PAIRS * c + k
            at = k % 2 * chan
            out[i] = (x_in[i].astype(F32) + conv[k // 2, 0:side, at:at + chan] + bias[...]).astype(BF16)
        return carry

    most = pairs // PAIRS - 1
    lax.fori_loop(0, most, conv_chunk, 0)

    for n in range(steps):
        take_rows(dps_s, n_dp - 1, n, 1, scale_sem.at[3 + n])
        take_rows(dps, n_dp - 1, n * step, step, sample_sem.at[1 + n])
        at = pl.ds(n * step, step)
        total = decode(dps[0, at], dps_s[0, n])
        for d in range(1, n_dp):
            total = total + decode(dps[d, at], dps_s[d, n])
        one = full.at[me, pl.ds(n * step, step)]
        one[...] = total.astype(BF16)

        last = n == steps - 1

        def share(h, one=one, n=n, last=last):
            remote(one, one, full_sem.at[0], near_sem.at[n], 2 * h + core).start()
            if last:
                remote(one, one, full_sem.at[0], near_sem.at[n], 2 * h + 1 - core).start()

        if chips == 4:
            for j in range(3):
                share(j + (j - chip + 4) // 4)
        else:
            each_chip(share)
        remote(one, one, full_sem.at[0], near_sem.at[n] if last else full_sem.at[1], partner).start()
    take(dps, n_dp - 1, sample_sem.at[0])
    take_rows(dps_s, n_dp - 1, 0, steps, scale_sem.at[2])
    if corners:
        stretch_relay(gends, 2, 2, far_g_sem)
    lax.fori_loop(most, pairs // PAIRS, conv_chunk, 0)

    if corners:
        stretch_finish(gends, 2, 2, far_g_sem)

    def rim_grad(e):
        at = adj[0, 1, e]
        g = gends[adj[0, 0, e], lax.rem(at + 5 - turn, 4)]
        v = jnp.dot(shifts(g.astype(F32)), vt[at], preferred_element_type=F32)
        return jnp.where(r64 < side, v, 0.0).astype(BF16)

    def rim_corner(k):
        at = adj[0, 1, 4 + k]
        v = jnp.dot(gends[adj[0, 0, 4 + k], lax.rem(at + 5 - turn, 4)], vt[at, 0:chan, :], preferred_element_type=F32)
        return v[side - 1:side].astype(BF16).astype(F32)

    add = [rim_corner(k) for k in range(4)]
    pad_grad[0, :, 0:chan] += rim_grad(0).astype(F32)
    pad_grad[pairs - 1, :, chan:] += flip(rim_grad(2))
    col_a[...] = flip(rim_grad(3)) + jnp.where(r64 == 0, add[0], jnp.where(r64 == side - 1, add[3], 0.0))
    col_b[...] = rim_grad(1).astype(F32) + jnp.where(r64 == 0, add[1], jnp.where(r64 == side - 1, add[2], 0.0))

    r56 = lax.broadcasted_iota(jnp.int32, (side, chan), 0)

    def finish_rows(c, carry):
        for k in range(ROWS):
            i = c * ROWS + k
            p = pad_grad[c * (ROWS // 2) + k // 2, 0:side, k % 2 * chan:(k % 2 + 1) * chan]
            p = p + jnp.where(r56 == 0, col_a[pl.ds(i, 1), :], jnp.where(r56 == side - 1, col_b[pl.ds(i, 1), :], 0.0))
            v = x_in[i].astype(F32)
            s = 0.5 + 0.5 * jnp.tanh(0.5 * v)
            gin_out[i] = (g_in[i].astype(F32) + p * s * (1.0 + v * (1.0 - s))).astype(BF16)
        return carry

    def share_relay(n):
        take_rows(full, chips - 1, n * step, step, near_sem.at[n])

        def go(h):
            one = full.at[2 * h + core, pl.ds(n * step, step)]
            remote(one, one, full_sem.at[0], full_sem.at[1], partner).start()

        each_chip(go)

    done = 0
    for n in range(steps - 1):
        share_relay(n)
        upto = chunks * (n + 1) // steps
        lax.fori_loop(done, upto, finish_rows, 0)
        done = upto
    lax.fori_loop(done, chunks, finish_rows, 0)
    take_rows(full, n_sp - 1, (steps - 1) * step, step, near_sem.at[steps - 1])
    if steps > 1:
        take_rows(full, chips, 0, (steps - 1) * step, full_sem.at[1])
    take(full, n_sp - 1, full_sem.at[0])

    if corners:
        for t in range(n_sp):
            v = full[t].astype(F32)
            r, c = (SIDES if t % 2 else CORNERS)[t // 2]
            wg_out[(3 * r + c) * chan:(3 * r + c + 1) * chan, :] = v[0:chan]
            at = 4 * chan + 16 * (t % 2 * chips + t // 2)
            wg_out[at:at + 16, :] = v[chan:]
    else:
        def open_rows(t, carry):
            at = (lax.rem(t, 2) * chips + t // 2) * size
            wg_out[pl.ds(pl.multiple_of(at, 16), size), :] = full[t].astype(F32)
            return carry

        lax.fori_loop(0, n_sp, open_rows, 0)


def hand_on(a, wg, c, a_out, wg_out, c_out, sems):
    def begin(src, dst, sem, parts=4):
        n = dst.shape[0] // parts
        for k in range(parts):
            rows = pl.ds(k * n, n)
            pltpu.make_async_copy(src.at[rows], dst.at[rows], sem).start()
        return pltpu.make_async_copy(dst, dst, sem)

    for one in [begin(a, a_out, sems.at[0]), begin(c, c_out, sems.at[1]), begin(wg, wg_out, sems.at[2])]:
        one.wait()


def per_device(n_sp, n_dp, block_in, weights, out_bias, adjacency, cotangent):
    side, chan = block_in.shape[2], block_in.shape[4]
    wide = wide_of(side)
    chips = n_sp // 2
    size = -(-9 * chan // (16 * n_sp)) * 16
    corners = chips == 4 and size == chan + 16
    group = n_sp if corners else 4
    edges = 2 if corners else 4
    vmem = pl.BlockSpec(memory_space=pltpu.VMEM)
    hbm = pl.BlockSpec(memory_space=pltpu.HBM)
    sem = pltpu.SemaphoreType.DMA
    tile = (side, side, chan)
    held = pl.pallas_call(
        functools.partial(block_kernel, n_sp, n_dp, side),
        out_shape=(pltpu.VMEM(tile, BF16), pltpu.VMEM((n_sp * size, chan), F32), pltpu.VMEM(tile, BF16)),
        in_specs=[hbm] * 5,
        out_specs=(vmem, vmem, vmem),
        scratch_shapes=[
            pltpu.VMEM(tile, BF16),
            pltpu.VMEM(tile, BF16),
            pltpu.VMEM((3, 3 * chan, chan), BF16),
            pltpu.VMEM((1, chan), F32),
            pltpu.SMEM((1, 2, 8), jnp.int32),
            pltpu.SMEM((n_sp, 1, chan), jnp.int32),
            pltpu.VMEM((n_sp, 1, chan), jnp.int32),
            pltpu.VMEM((side // 2 + 2, wide, 6 * chan), BF16),
            pltpu.VMEM((side // 2 + 2, wide, 6 * chan), BF16),
            pltpu.VMEM((2 * chan, side // 2 * wide), BF16),
            pltpu.VMEM((side // 2, wide, 2 * chan), F32),
            pltpu.VMEM((3, 3 * chan, chan), BF16),
            pltpu.VMEM((4, 3 * chan, chan), BF16),
            pltpu.VMEM((12 * chan, 2 * chan), BF16),
            pltpu.VMEM((12 * chan, 2 * chan), BF16),
            pltpu.VMEM((n_sp * size, chan), F32),
            pltpu.VMEM((n_sp * size, chan), F32),
            pltpu.VMEM((chips * size, chan), F32),
            pltpu.VMEM((wide, chan), F32),
            pltpu.VMEM((wide, chan), F32),
            pltpu.VMEM((wide, chan), F32),
            pltpu.VMEM((wide, chan), F32),
            pltpu.VMEM((n_sp, 4, wide, chan), BF16),
            pltpu.VMEM((n_sp, 4 * side, chan), BF16),
            pltpu.VMEM((7, wide, chan), BF16),
            pltpu.VMEM((n_sp, 4, wide, chan), BF16),
            pltpu.VMEM((edges, group * wide, chan), BF16),
            pltpu.VMEM((edges, chan, group * wide), BF16),
            pltpu.VMEM((edges, group * wide, 3 * chan), BF16),
            pltpu.VMEM((chips, size, chan), CODE),
            pltpu.VMEM((chips, 1, chan), F32),
            pltpu.VMEM((chips, size, chan), CODE),
            pltpu.VMEM((chips, 1, chan), F32),
            pltpu.VMEM((n_dp, size, chan), CODE),
            pltpu.VMEM((n_dp, 3, 1, chan), F32),
            pltpu.VMEM((n_sp, size, chan), BF16),
            sem((6,)), sem((3,)), sem((3,)), sem((3,)), sem((2,)), sem((2,)), sem((4,)), sem((4,)), sem((6,)), sem((2,)), sem((3,)),
        ],
        compiler_params=pltpu.CompilerParams(
            collective_id=0, has_side_effects=True, vmem_limit_bytes=58 * 2**20),
    )(
        adjacency.transpose(0, 2, 1), block_in[0, 0], weights.reshape(3, 3 * chan, chan), out_bias.reshape(1, chan),
        cotangent[0, 0],
    )
    result, wgrad, grad_in = pl.pallas_call(
        hand_on,
        out_shape=(
            jax.ShapeDtypeStruct(tile, BF16), jax.ShapeDtypeStruct((9 * chan, chan), F32), jax.ShapeDtypeStruct(tile, BF16)),
        in_specs=[vmem, vmem, vmem],
        out_specs=(hbm, hbm, hbm),
        scratch_shapes=[sem((3,))],
        compiler_params=pltpu.CompilerParams(vmem_limit_bytes=4 * 2**20),
    )(*held)
    return (result[None, None], wgrad.reshape(weights.shape), grad_in[None, None])


def solution(mesh):
    placed = (
        P("dp", "space", None, None, None),
        P(),
        P(),
        P("space", None, None),
        P("dp", "space", None, None, None),
    )
    return jax.shard_map(
        functools.partial(per_device, mesh.shape["space"], mesh.shape["dp"]),
        mesh=mesh,
        in_specs=placed,
        out_specs=(P("dp", "space", None, None, None), P(), P("dp", "space", None, None, None)),
        check_vma=False,
    )
```

```python
import functools

import jax
import jax.numpy as jnp
from jax import lax
from jax.experimental import pallas as pl
from jax.experimental.pallas import tpu as pltpu
from jax.sharding import PartitionSpec as P

MESH = pl.DeviceIdType.MESH
ROWS = 8
PAIRS = 7
CORNERS = ((0, 0), (0, 2), (2, 2), (2, 0))
SIDES = ((0, 1), (1, 2), (2, 1), (1, 0))
F32 = jnp.float32
BF16 = jnp.bfloat16
CODE = jnp.int16


def silu(v):
    h = 0.5 * v
    return h + h * jnp.tanh(h)


def encode(v):
    top = jnp.maximum(jnp.max(jnp.abs(v), axis=0, keepdims=True), 1e-30)
    power = jnp.ceil(jnp.log2(top))
    code = jnp.clip(jnp.round(v * jnp.exp2(15.0 - power)), -32767.0, 32767.0)
    return code.astype(jnp.int32).astype(CODE), jnp.exp2(power - 15.0)


def decode(rows, scale):
    return rows.astype(jnp.int32).astype(F32) * scale


def wide_of(side):
    return -(-(side + 4) // 16) * 16


def block_kernel(
    n_sp, n_dp, side,
    adj_hbm, x_hbm, w_hbm, bias_hbm, g_hbm,
    out, wg_out, gin_out,
    x_in, g_in, w_in, bias, adj, adj_all, adj_row,
    taps, gtaps, flat, pad_grad, wt, vt, pair_w, pair_t, wgf, corr, half_in, col_a, col_b, col_c, col_d,
    ends, packed, turned, gends, la, lat, lg, sent, sent_s, parts, parts_s, dps, dps_s, full,
    in_sem, edge_sem, near_g_sem, far_g_sem, adj_sem, swap_sem, share_sem, sample_sem, scale_sem, full_sem, near_sem,
):
    wide = wide_of(side)
    chan = 128
    chunks = side // ROWS
    me = lax.axis_index("space")
    my_dp = lax.axis_index("dp")
    core = lax.rem(me, 2)
    chip = me // 2
    chips = n_sp // 2
    partner = me + 1 - 2 * core
    size = full.shape[1]
    corners = chips == 4 and size == chan + 16
    near_count = 2 if corners else 4
    turn = chip if corners else 0

    barrier = pltpu.get_barrier_semaphore()

    def greet_sp(k, c):
        pl.semaphore_signal(barrier, inc=1, device_id=(lax.rem(me + k, n_sp), my_dp), device_id_type=MESH)
        return c

    def greet_dp(k, c):
        pl.semaphore_signal(barrier, inc=1, device_id=(me, lax.rem(my_dp + k, n_dp)), device_id_type=MESH)
        return c

    def load(src, dst, sem, parts=1):
        n = dst.shape[0] // parts
        for k in range(parts):
            rows = pl.ds(k * n, n)
            pltpu.make_async_copy(src.at[rows], dst.at[rows], sem).start()
        return pltpu.make_async_copy(src, dst, sem)

    loads = [
        load(adj_hbm, adj, in_sem.at[2]),
        load(x_hbm, x_in, in_sem.at[0], 4),
        load(g_hbm, g_in, in_sem.at[1], 4),
        load(w_hbm, w_in, in_sem.at[3]),
        load(bias_hbm, bias, in_sem.at[4]),
    ]
    lax.fori_loop(1, n_sp, greet_sp, 0)
    lax.fori_loop(1, n_dp, greet_dp, 0)

    def each_chip(do):
        if chips == 4:
            for other in (3 - chip, lax.rem(chip + 2, 4), chip + 1 - 2 * lax.rem(chip, 2)):
                do(other)
        else:
            def go(k, c):
                do(lax.rem(chip + k, chips))
                return c
            lax.fori_loop(1, chips, go, 0)

    def other_dp(j):
        return j + (j - my_dp + n_dp) // n_dp

    def remote(src, dst, send, recv, peer, dp=None):
        return pltpu.make_async_remote_copy(
            src_ref=src, dst_ref=dst, send_sem=send, recv_sem=recv,
            device_id=(peer, my_dp if dp is None else dp), device_id_type=MESH)

    def take(buf, count, sem):
        some = buf.at[pl.ds(0, count)]
        pltpu.make_async_copy(some, some, sem).wait()

    def take_rows(buf, count, first, rows, sem):
        some = buf.at[pl.ds(0, count), pl.ds(first, rows)]
        pltpu.make_async_copy(some, some, sem).wait()

    def pair_begin(buf, sems):
        mine = buf.at[me]
        each_chip(lambda h: remote(mine, mine, sems.at[0], sems.at[2], 2 * h + core).start())
        remote(mine, mine, sems.at[0], sems.at[1], partner).start()

    def pair_relay(buf, sems):
        take(buf, chips - 1, sems.at[2])
        def go(h):
            other = buf.at[2 * h + core]
            remote(other, other, sems.at[0], sems.at[1], partner).start()
        each_chip(go)

    def pair_finish(buf, sems):
        take(buf, chips, sems.at[1])
        take(buf, n_sp - 1, sems.at[0])

    def stretch_begin(src, buf, first, count, sems):
        to = buf.at[me, pl.ds(first, count)]

        def one(h, peer, sem):
            at = pl.ds((h if corners else 0) + first, count)
            remote(src.at[at], to, sems.at[0], sem, peer).start()

        each_chip(lambda h: one(h, 2 * h + core, sems.at[2]))
        one(chip, partner, sems.at[1])

    def stretch_relay(buf, first, count, sems):
        take_rows(buf, chips - 1, first, count, sems.at[2])

        def go(h):
            other = buf.at[2 * h + core, pl.ds(first, count)]
            remote(other, other, sems.at[0], sems.at[1], partner).start()

        each_chip(go)

    def stretch_finish(buf, first, count, sems):
        take_rows(buf, chips, first, count, sems.at[1])
        take_rows(buf, n_sp - 1, first, count, sems.at[0])

    r64 = lax.broadcasted_iota(jnp.int32, (wide, chan), 0)
    ra = lax.broadcasted_iota(jnp.int32, (wide, wide), 0)
    rb = lax.broadcasted_iota(jnp.int32, (wide, wide), 1)
    mirror = jnp.where(ra + rb == side - 1, 1.0, 0.0).astype(BF16)

    def flip(v):
        return jnp.dot(mirror, v, preferred_element_type=F32)

    s8 = lax.broadcasted_iota(jnp.int32, (8, chan), 0)

    def column(block, at):
        rows = block[0] if at == 0 else pltpu.roll(block[0], 8 - at, 0)
        for k in range(1, ROWS):
            one = block[k] if k == at else pltpu.roll(block[k], (k - at) % 8, 0)
            rows = jnp.where(s8 == k, one, rows)
        return rows

    tail = jnp.zeros((wide - side, chan), F32)

    def widen(v):
        return jnp.concatenate([v, tail], axis=0)

    loads[0].wait()
    lane = lax.broadcasted_iota(jnp.int32, (1, chan), 1)
    row = jnp.zeros((1, chan), jnp.int32)
    for k in range(8):
        for part in range(2):
            row = jnp.where(lane == 2 * k + part, adj[0, part, k], row)
    adj_row[me] = row
    loads[1].wait()
    for c in range(chunks):
        lo = c * ROWS
        col_a[lo:lo + ROWS, :] = silu(column(x_in[lo:lo + ROWS, 0:8, :].astype(F32), 0))
        col_b[lo:lo + ROWS, :] = silu(column(x_in[lo:lo + ROWS, side - 8:side, :].astype(F32), 7))
    for col in (col_a, col_b, col_c, col_d):
        col[side:wide, :] = tail
    for k, v in enumerate((
        silu(x_in[0].astype(F32)), col_b[0:side, :], flip(widen(silu(x_in[side - 1].astype(F32))).astype(BF16))[0:side],
        flip(col_a[...].astype(BF16))[0:side])):
        packed[me, k * side:(k + 1) * side, :] = v.astype(BF16)

    three = 3 * chan
    pairs = side // 2
    zero_row = jnp.zeros((wide, three), BF16)
    for buf in (taps, gtaps):
        buf[0, :, three:] = zero_row
        buf[pairs + 1, :, 0:three] = zero_row

    def shifts(v):
        return jnp.concatenate(
            [pltpu.roll(v, 1, 0).astype(BF16), v.astype(BF16), pltpu.roll(v, wide - 1, 0).astype(BF16)], axis=1)

    def spread(c, carry):
        for part in range(2):
            rows = []
            for k in range(ROWS // 2):
                i = c * ROWS + 2 * k + part
                p = c * (ROWS // 2) + k + 1
                a = widen(silu(x_in[i].astype(F32)))
                rows.append(a.astype(BF16))
                taps[p, :, part * three + chan:part * three + 2 * chan] = rows[-1]
                gtaps[p, :, part * three:(part + 1) * three] = shifts(widen(g_in[i].astype(F32)))
            n = ROWS // 2 * wide
            flat[part * chan:(part + 1) * chan, pl.ds(pl.multiple_of(c * n, n), n)] = jnp.concatenate(rows, axis=0).T
        return carry

    ahead = chunks * (1 - (2 * my_dp) // n_dp)
    loads[2].wait()
    lax.fori_loop(0, ahead, spread, 0)

    pl.semaphore_wait(barrier, n_sp + n_dp - 2)
    def tell(k, c):
        mine = adj_row.at[me]
        remote(mine, mine, adj_sem.at[0], adj_sem.at[1], lax.rem(me + k, n_sp)).start()
        return c

    lax.fori_loop(1, n_sp, tell, 0)
    pair_begin(packed, edge_sem)
    for c in range(chunks):
        lo = c * ROWS
        col_c[lo:lo + ROWS, :] = column(g_in[lo:lo + ROWS, 0:8, :].astype(F32), 0)
        col_d[lo:lo + ROWS, :] = column(g_in[lo:lo + ROWS, side - 8:side, :].astype(F32), 7)
    around = (
        flip(widen(g_in[0].astype(F32)).astype(BF16)).astype(BF16), flip(col_d[...].astype(BF16)).astype(BF16),
        widen(g_in[side - 1].astype(F32)).astype(BF16), col_c[...].astype(BF16))
    for k in range(7):
        turned[k] = around[(k + 3) % 4]
    for k in range(4):
        gends[me, k] = turned[turn + k]
    stretch_begin(turned, gends, 0, near_count, near_g_sem)

    lax.fori_loop(ahead, chunks, spread, 0)

    def grads(first, part):
        return gtaps[first:first + pairs, :, part * three:(part + 1) * three].reshape(pairs * wide, three)

    odd = jnp.dot(flat[...], grads(1, 1), preferred_element_type=F32)
    even = jnp.dot(flat[...], grads(1, 0), preferred_element_type=F32)
    below = jnp.dot(flat[0:chan], grads(0, 1), preferred_element_type=F32)
    above = jnp.dot(flat[chan:2 * chan], grads(2, 0), preferred_element_type=F32)
    for r, v in enumerate((odd[:chan] + above, odd[chan:] + even[:chan], even[chan:] + below)):
        for b in range(3):
            block = v[:, b * chan:(b + 1) * chan]
            if not corners:
                wgf[(3 * r + 2 - b) * chan:(3 * r + 3 - b) * chan, :] = block
            elif (r, b) == (1, 1):
                for k in range(n_sp):
                    wgf[k * size + chan:(k + 1) * size, :] = block[16 * k:16 * k + 16]
            else:
                kind = SIDES if (r + b) % 2 else CORNERS
                at = (kind.index((r, 2 - b)) + chips * ((r + b) % 2)) * size
                wgf[at:at + chan, :] = block
    used = 9 * chan
    if wgf.shape[0] > used:
        wgf[used:, :] = jnp.zeros((wgf.shape[0] - used, chan), F32)

    half = chips * size
    swap = remote(
        wgf.at[pl.ds(pl.multiple_of((1 - core) * half, 16), half)], half_in, swap_sem.at[0], swap_sem.at[1], partner)
    swap.start()
    take(adj_row, n_sp - 1, adj_sem.at[1])
    take(adj_row, n_sp - 1, adj_sem.at[0])
    spill = pltpu.make_async_copy(adj_row, adj_all, in_sem.at[5])
    spill.start()

    loads[3].wait()
    loads[4].wait()
    for r in range(3):
        for c in range(3):
            block = w_in[2 - r, (2 - c) * chan:(3 - c) * chan, :].astype(F32)
            wt[r, c * chan:(c + 1) * chan, :] = block.T.astype(BF16)
    for k in range(3):
        to = slice(k * chan, (k + 1) * chan)
        for e, (r, c) in enumerate(((2, 2 - k), (2 - k, 0), (0, k), (k, 2))):
            vt[e, to, :] = wt[r, c * chan:(c + 1) * chan, :]
    blank = jnp.zeros((three, chan), BF16)
    for buf, one in ((pair_w, w_in), (pair_t, wt)):
        for k in range(4):
            at = slice(k * three, (k + 1) * three)
            buf[at, 0:chan] = one[k] if k < 3 else blank
            buf[at, chan:] = one[k - 1] if k > 0 else blank
    def two_rows(buf, first, w):
        rows = jnp.concatenate([
            buf[pl.ds(first, PAIRS), :, three:].reshape(PAIRS * wide, three),
            buf[pl.ds(first + 1, PAIRS)].reshape(PAIRS * wide, 2 * three),
            buf[pl.ds(first + 2, PAIRS), :, 0:three].reshape(PAIRS * wide, three)], axis=1)
        return jnp.dot(rows, w[...], preferred_element_type=F32).reshape(PAIRS, wide, 2 * chan)

    def grad_chunk(c, carry):
        pad_grad[pl.ds(c * PAIRS, PAIRS)] = two_rows(gtaps, c * PAIRS, pair_t)
        return carry

    early = pairs // PAIRS // 2
    none = my_dp // n_dp
    lax.fori_loop(none, none + early // 2, grad_chunk, 0)
    swap.wait()

    def half_rows(h):
        at = pl.multiple_of(h * size, 16)
        return wgf[pl.ds(pl.multiple_of(core * half + h * size, 16), size), :] + half_in[pl.ds(at, size), :]

    def scatter(h):
        sent[h], sent_s[h] = encode(half_rows(h))
        remote(sent_s.at[h], parts_s.at[chip], scale_sem.at[0], scale_sem.at[1], 2 * h + core).start()

    each_chip(scatter)
    steps = 3 if size % 48 == 0 else 1
    step = size // steps
    for n in range(steps):
        rows = pl.ds(n * step, step)
        each_chip(lambda h, n=n, rows=rows: remote(
            sent.at[h, rows], parts.at[chip, rows], share_sem.at[0], share_sem.at[1 + n], 2 * h + core).start())

    pair_relay(packed, edge_sem)

    stretch_relay(gends, 0, near_count, near_g_sem)
    lax.fori_loop(none + early // 2, none + early, grad_chunk, 0)
    pair_finish(packed, edge_sem)

    def unpack(t, carry):
        for k in range(4):
            ends[t, k] = widen(packed[t, k * side:(k + 1) * side, :].astype(F32)).astype(BF16)
        return carry

    lax.fori_loop(0, n_sp, unpack, 0)
    spill.wait()

    def rim_cells(t, e):
        v = ends[adj_all[t, 0, 2 * e], adj_all[t, 0, 2 * e + 1]].astype(F32)
        k = ends[adj_all[t, 0, 8 + 2 * e], adj_all[t, 0, 9 + 2 * e]].astype(F32)[0:1]
        return jnp.where(r64 < side, v, jnp.where(r64 == side, k, 0.0)).astype(BF16)

    slot = core * chips + chip
    if corners:
        def tile_rows(t):
            return pl.ds(pl.multiple_of(t * wide, 16), wide)

        def turn_edges(t, carry):
            la[0, tile_rows(t), :] = rim_cells(t, chip)
            la[1, tile_rows(t), :] = rim_cells(t, lax.rem(chip + 3, 4))
            return carry

        def shift_edges(parity):
            def go(k, carry):
                t = 2 * k + parity
                g = gends[t, 1].astype(F32)
                lg[0, tile_rows(t), 0:chan] = pltpu.roll(g, 1, 0).astype(BF16)
                lg[0, tile_rows(t), chan:2 * chan] = gends[t, 1]
                lg[1, tile_rows(t), 0:chan] = pltpu.roll(gends[t, 0].astype(F32), wide - 1, 0).astype(BF16)
                return carry
            lax.fori_loop(0, chips, go, 0)

        lax.fori_loop(0, n_sp, turn_edges, 0)
        for k in range(2):
            lat[k] = la[k].T
        shift_edges(core)
        stretch_finish(gends, 0, near_count, near_g_sem)
        shift_edges(1 - core)
        here = jnp.dot(lat[0], lg[0, :, 0:2 * chan], preferred_element_type=F32)
        before = jnp.dot(lat[1], lg[1, :, 0:chan], preferred_element_type=F32)
        mine = half_rows(chip)
        rim = jnp.where(core == 0, here[:, 0:chan] + before, here[:, chan:])
        mine = jnp.concatenate([mine[0:chan] + rim, mine[chan:]], axis=0)
    else:
        stretch_finish(gends, 0, near_count, near_g_sem)
        group = la.shape[1] // wide
        corr[...] = jnp.zeros_like(corr)

        def rim_group(n, carry):
            def fill(j, c2):
                t = n * group + j
                at = pl.ds(pl.multiple_of(j * wide, 16), wide)
                for e in range(4):
                    la[e, at, :] = rim_cells(t, e)
                    lg[e, at, :] = shifts(gends[t, (e + 1) % 4].astype(F32))
                return c2

            lax.fori_loop(0, group, fill, 0)
            for e in range(4):
                res = jnp.dot(la[e].T, lg[e], preferred_element_type=F32)
                for k in range(3):
                    r, c = ((0, k), (k, 2), (2, 2 - k), (2 - k, 0))[e]
                    at = (3 * r + c) * chan
                    corr[at:at + chan, :] += res[:, k * chan:(k + 1) * chan]
            return carry

        lax.fori_loop(0, n_sp // group, rim_group, 0)
        mine = half_rows(chip) + corr[pl.ds(pl.multiple_of(slot * size, 16), size), :]

    def to_sample(n, j):
        one, scale = dps.at[my_dp, pl.ds(n * step, step)], dps_s.at[my_dp, n]
        remote(scale, scale, scale_sem.at[2], scale_sem.at[3 + n], me, other_dp(j)).start()
        remote(one, one, sample_sem.at[0], sample_sem.at[1 + n], me, other_dp(j)).start()

    take(parts_s, chips - 1, scale_sem.at[1])
    for n in range(steps):
        rows = pl.ds(n * step, step)
        take_rows(parts, chips - 1, n * step, step, share_sem.at[1 + n])

        def add_part(k, t, rows=rows):
            h = lax.rem(chip + k, chips)
            return t + decode(parts[h, rows], parts_s[h])

        some = lax.fori_loop(1, chips, add_part, mine[n * step:(n + 1) * step])
        dps[my_dp, rows], dps_s[my_dp, n] = encode(some)
        to_sample(n, 0)
    for n in range(steps):
        for j in range(1, n_dp - 1):
            to_sample(n, j)
    take(sent, chips - 1, share_sem.at[0])
    take(sent_s, chips - 1, scale_sem.at[0])
    if corners:
        stretch_begin(turned, gends, 2, 2, far_g_sem)

    def near(buf, e):
        return buf[adj[0, 0, e], adj[0, 1, e]]

    corner = [ends[adj[0, 0, 4 + k], adj[0, 1, 4 + k]].astype(F32)[0:1] for k in range(4)]

    def rim_row(v, behind, ahead):
        return jnp.where(r64 < side, v, jnp.where(r64 == side, behind, jnp.where(r64 == wide - 1, ahead, 0.0)))

    taps[0, :, three:] = shifts(rim_row(flip(near(ends, 0)), corner[1], corner[0]))
    taps[pairs + 1, :, 0:three] = shifts(rim_row(near(ends, 2).astype(F32), corner[2], corner[3]))
    col_a[...] = near(ends, 3).astype(F32)
    col_b[...] = flip(near(ends, 1))

    def spread_act(c, carry):
        for part in range(2):
            at = part * three
            for k in range(ROWS // 2):
                p = c * (ROWS // 2) + k + 1
                i = pl.ds(c * ROWS + 2 * k + part, 1)
                v = taps[p, :, at + chan:at + 2 * chan].astype(F32)
                taps[p, :, at:at + chan] = jnp.where(r64 == 0, col_a[i, :], pltpu.roll(v, 1, 0)).astype(BF16)
                taps[p, :, at + 2 * chan:at + three] = jnp.where(
                    r64 == side - 1, col_b[i, :], pltpu.roll(v, wide - 1, 0)).astype(BF16)
        return carry

    lax.fori_loop(0, chunks, spread_act, 0)
    lax.fori_loop(early, pairs // PAIRS, grad_chunk, 0)

    def conv_chunk(c, carry):
        conv = two_rows(taps, c * PAIRS, pair_w)
        for k in range(2 * PAIRS):
            i = 2 * PAIRS * c + k
            at = k % 2 * chan
            out[i] = (x_in[i].astype(F32) + conv[k // 2, 0:side, at:at + chan] + bias[...]).astype(BF16)
        return carry

    most = pairs // PAIRS - 1
    lax.fori_loop(0, most, conv_chunk, 0)

    for n in range(steps):
        take_rows(dps_s, n_dp - 1, n, 1, scale_sem.at[3 + n])
        take_rows(dps, n_dp - 1, n * step, step, sample_sem.at[1 + n])
        at = pl.ds(n * step, step)
        total = decode(dps[0, at], dps_s[0, n])
        for d in range(1, n_dp):
            total = total + decode(dps[d, at], dps_s[d, n])
        one = full.at[me, pl.ds(n * step, step)]
        one[...] = total.astype(BF16)

        last = n == steps - 1

        def share(h, one=one, n=n, last=last):
            remote(one, one, full_sem.at[0], near_sem.at[n], 2 * h + core).start()
            if last:
                remote(one, one, full_sem.at[0], near_sem.at[n], 2 * h + 1 - core).start()

        if chips == 4:
            for j in range(3):
                share(j + (j - chip + 4) // 4)
        else:
            each_chip(share)
        remote(one, one, full_sem.at[0], near_sem.at[n] if last else full_sem.at[1], partner).start()
    take(dps, n_dp - 1, sample_sem.at[0])
    take_rows(dps_s, n_dp - 1, 0, steps, scale_sem.at[2])
    if corners:
        stretch_relay(gends, 2, 2, far_g_sem)
    lax.fori_loop(most, pairs // PAIRS, conv_chunk, 0)

    if corners:
        stretch_finish(gends, 2, 2, far_g_sem)

    def rim_grad(e):
        at = adj[0, 1, e]
        g = gends[adj[0, 0, e], lax.rem(at + 5 - turn, 4)]
        v = jnp.dot(shifts(g.astype(F32)), vt[at], preferred_element_type=F32)
        return jnp.where(r64 < side, v, 0.0).astype(BF16)

    def rim_corner(k):
        at = adj[0, 1, 4 + k]
        v = jnp.dot(gends[adj[0, 0, 4 + k], lax.rem(at + 5 - turn, 4)], vt[at, 0:chan, :], preferred_element_type=F32)
        return v[side - 1:side].astype(BF16).astype(F32)

    add = [rim_corner(k) for k in range(4)]
    pad_grad[0, :, 0:chan] += rim_grad(0).astype(F32)
    pad_grad[pairs - 1, :, chan:] += flip(rim_grad(2))
    col_a[...] = flip(rim_grad(3)) + jnp.where(r64 == 0, add[0], jnp.where(r64 == side - 1, add[3], 0.0))
    col_b[...] = rim_grad(1).astype(F32) + jnp.where(r64 == 0, add[1], jnp.where(r64 == side - 1, add[2], 0.0))

    r56 = lax.broadcasted_iota(jnp.int32, (side, chan), 0)

    def finish_rows(c, carry):
        for k in range(ROWS):
            i = c * ROWS + k
            p = pad_grad[c * (ROWS // 2) + k // 2, 0:side, k % 2 * chan:(k % 2 + 1) * chan]
            p = p + jnp.where(r56 == 0, col_a[pl.ds(i, 1), :], jnp.where(r56 == side - 1, col_b[pl.ds(i, 1), :], 0.0))
            v = x_in[i].astype(F32)
            s = 0.5 + 0.5 * jnp.tanh(0.5 * v)
            gin_out[i] = (g_in[i].astype(F32) + p * s * (1.0 + v * (1.0 - s))).astype(BF16)
        return carry

    def share_relay(n):
        take_rows(full, chips - 1, n * step, step, near_sem.at[n])

        def go(h):
            one = full.at[2 * h + core, pl.ds(n * step, step)]
            remote(one, one, full_sem.at[0], full_sem.at[1], partner).start()

        each_chip(go)

    done = 0
    for n in range(steps - 1):
        share_relay(n)
        upto = chunks * (n + 1) // steps
        lax.fori_loop(done, upto, finish_rows, 0)
        done = upto
    lax.fori_loop(done, chunks, finish_rows, 0)
    take_rows(full, n_sp - 1, (steps - 1) * step, step, near_sem.at[steps - 1])
    if steps > 1:
        take_rows(full, chips, 0, (steps - 1) * step, full_sem.at[1])
    take(full, n_sp - 1, full_sem.at[0])

    if corners:
        for t in range(n_sp):
            v = full[t].astype(F32)
            r, c = (SIDES if t % 2 else CORNERS)[t // 2]
            wg_out[(3 * r + c) * chan:(3 * r + c + 1) * chan, :] = v[0:chan]
            at = 4 * chan + 16 * (t % 2 * chips + t // 2)
            wg_out[at:at + 16, :] = v[chan:]
    else:
        def open_rows(t, carry):
            at = (lax.rem(t, 2) * chips + t // 2) * size
            wg_out[pl.ds(pl.multiple_of(at, 16), size), :] = full[t].astype(F32)
            return carry

        lax.fori_loop(0, n_sp, open_rows, 0)


def hand_on(a, wg, c, a_out, wg_out, c_out, sems):
    def begin(src, dst, sem, parts=4):
        n = dst.shape[0] // parts
        for k in range(parts):
            rows = pl.ds(k * n, n)
            pltpu.make_async_copy(src.at[rows], dst.at[rows], sem).start()
        return pltpu.make_async_copy(dst, dst, sem)

    for one in [begin(a, a_out, sems.at[0]), begin(c, c_out, sems.at[1]), begin(wg, wg_out, sems.at[2])]:
        one.wait()


def per_device(n_sp, n_dp, block_in, weights, out_bias, adjacency, cotangent):
    side, chan = block_in.shape[2], block_in.shape[4]
    wide = wide_of(side)
    chips = n_sp // 2
    size = -(-9 * chan // (16 * n_sp)) * 16
    corners = chips == 4 and size == chan + 16
    group = n_sp if corners else 4
    edges = 2 if corners else 4
    vmem = pl.BlockSpec(memory_space=pltpu.VMEM)
    hbm = pl.BlockSpec(memory_space=pltpu.HBM)
    sem = pltpu.SemaphoreType.DMA
    tile = (side, side, chan)
    held = pl.pallas_call(
        functools.partial(block_kernel, n_sp, n_dp, side),
        out_shape=(pltpu.VMEM(tile, BF16), pltpu.VMEM((n_sp * size, chan), F32), pltpu.VMEM(tile, BF16)),
        in_specs=[hbm] * 5,
        out_specs=(vmem, vmem, vmem),
        scratch_shapes=[
            pltpu.VMEM(tile, BF16),
            pltpu.VMEM(tile, BF16),
            pltpu.VMEM((3, 3 * chan, chan), BF16),
            pltpu.VMEM((1, chan), F32),
            pltpu.SMEM((1, 2, 8), jnp.int32),
            pltpu.SMEM((n_sp, 1, chan), jnp.int32),
            pltpu.VMEM((n_sp, 1, chan), jnp.int32),
            pltpu.VMEM((side // 2 + 2, wide, 6 * chan), BF16),
            pltpu.VMEM((side // 2 + 2, wide, 6 * chan), BF16),
            pltpu.VMEM((2 * chan, side // 2 * wide), BF16),
            pltpu.VMEM((side // 2, wide, 2 * chan), F32),
            pltpu.VMEM((3, 3 * chan, chan), BF16),
            pltpu.VMEM((4, 3 * chan, chan), BF16),
            pltpu.VMEM((12 * chan, 2 * chan), BF16),
            pltpu.VMEM((12 * chan, 2 * chan), BF16),
            pltpu.VMEM((n_sp * size, chan), F32),
            pltpu.VMEM((n_sp * size, chan), F32),
            pltpu.VMEM((chips * size, chan), F32),
            pltpu.VMEM((wide, chan), F32),
            pltpu.VMEM((wide, chan), F32),
            pltpu.VMEM((wide, chan), F32),
            pltpu.VMEM((wide, chan), F32),
            pltpu.VMEM((n_sp, 4, wide, chan), BF16),
            pltpu.VMEM((n_sp, 4 * side, chan), BF16),
            pltpu.VMEM((7, wide, chan), BF16),
            pltpu.VMEM((n_sp, 4, wide, chan), BF16),
            pltpu.VMEM((edges, group * wide, chan), BF16),
            pltpu.VMEM((edges, chan, group * wide), BF16),
            pltpu.VMEM((edges, group * wide, 3 * chan), BF16),
            pltpu.VMEM((chips, size, chan), CODE),
            pltpu.VMEM((chips, 1, chan), F32),
            pltpu.VMEM((chips, size, chan), CODE),
            pltpu.VMEM((chips, 1, chan), F32),
            pltpu.VMEM((n_dp, size, chan), CODE),
            pltpu.VMEM((n_dp, 3, 1, chan), F32),
            pltpu.VMEM((n_sp, size, chan), BF16),
            sem((6,)), sem((3,)), sem((3,)), sem((3,)), sem((2,)), sem((2,)), sem((4,)), sem((4,)), sem((6,)), sem((2,)), sem((3,)),
        ],
        compiler_params=pltpu.CompilerParams(
            collective_id=0, has_side_effects=True, vmem_limit_bytes=58 * 2**20),
    )(
        adjacency.transpose(0, 2, 1), block_in[0, 0], weights.reshape(3, 3 * chan, chan), out_bias.reshape(1, chan),
        cotangent[0, 0],
    )
    result, wgrad, grad_in = pl.pallas_call(
        hand_on,
        out_shape=(
            jax.ShapeDtypeStruct(tile, BF16), jax.ShapeDtypeStruct((9 * chan, chan), F32), jax.ShapeDtypeStruct(tile, BF16)),
        in_specs=[vmem, vmem, vmem],
        out_specs=(hbm, hbm, hbm),
        scratch_shapes=[sem((3,))],
        compiler_params=pltpu.CompilerParams(vmem_limit_bytes=4 * 2**20),
    )(*held)
    return (result[None, None], wgrad.reshape(weights.shape), grad_in[None, None])


def solution(mesh):
    placed = (
        P("dp", "space", None, None, None),
        P(),
        P(),
        P("space", None, None),
        P("dp", "space", None, None, None),
    )
    return jax.shard_map(
        functools.partial(per_device, mesh.shape["space"], mesh.shape["dp"]),
        mesh=mesh,
        in_specs=placed,
        out_specs=(P("dp", "space", None, None, None), P(), P("dp", "space", None, None, None)),
        check_vma=False,
    )
```
